32 devices in a mesh: energy: 8 (over z, core), block: 4 (over y, x).
Axes of the slice: x: 2, y: 2, z: 4, core: 2. Of those that a mesh axis runs over, the one named last changes fastest.
Arguments:
- g_lesser: float32 [2, 8, 1024, 256], P(None, 'energy', 'block'), may hold values from -0.75 to 0.75
- g_greater: float32 [2, 8, 1024, 256], P(None, 'energy', 'block'), may hold values from -0.75 to 0.75
- onsite: float32 [2, 8, 1024, 256], P(None, 'energy', 'block'), may hold values from -1 to 7
- lower: float32 [2, 1024, 256], P(None, 'block'), may hold values from -0.5 to 2.7
- upper: float32 [2, 1024, 256], P(None, 'block'), may hold values from -0.5 to 2.7
- rhs: float32 [2, 8, 1024, 128], P(None, 'energy', 'block'), may hold values from -16 to 16
Outputs:
- solution: float32 [2, 8, 1024, 128], P(None, 'energy', 'block')
The draws below stay inside these ranges and needn't reach their ends.
All inputs are finite; a program needn't handle non-finite values.
Results may differ from the reference program's by a relative error of at most 0.0003.
Values sent between devices are 32-bit elements; how exact they have to be, the bound alone decides.
A program may use at most 64 MiB of HBM per device.

```python
import math
import jax
import jax.numpy as jnp
from jax import lax

BO = 256
NR = 128
NS_STEPS = 2
NE = 8
NB = 4
LEVELS = 2


def draw_onsite(key, part):
    first_key, second_key, third_key, fourth_key = jax.random.split(jax.random.fold_in(key, 11), 4)
    full_shape = (NE, NB * BO, BO)
    row_position = jnp.arange(NB * BO)[:, None] % BO
    column_position = jnp.arange(BO)[None, :]
    on_diagonal = (row_position == column_position).astype(jnp.float32)
    real_noise = jnp.clip(jax.random.normal(first_key, full_shape, jnp.float32), -4.0, 4.0)
    imag_noise = jnp.clip(jax.random.normal(second_key, full_shape, jnp.float32), -4.0, 4.0)
    real_diagonal = jax.random.uniform(third_key, full_shape, jnp.float32, 5.5, 6.5)
    imag_diagonal = jax.random.uniform(fourth_key, full_shape, jnp.float32, 0.2, 1.0)
    real_part = on_diagonal * real_diagonal + (1.0 - on_diagonal) * real_noise * (0.7 / math.sqrt(BO))
    imag_part = on_diagonal * imag_diagonal + (1.0 - on_diagonal) * imag_noise * (0.2 / math.sqrt(BO))
    return jnp.stack([real_part, imag_part])


def coupling_draw(key, draw_label):
    strength_key, real_key, imag_key = jax.random.split(jax.random.fold_in(key, draw_label), 3)
    full_shape = (NB * BO, BO)
    row_position = jnp.arange(NB * BO)[:, None] % BO
    column_position = jnp.arange(BO)[None, :]
    on_diagonal = (row_position == column_position).astype(jnp.float32)
    strength = jax.random.uniform(strength_key, full_shape, jnp.float32, 2.45, 2.7)
    real_noise = jnp.clip(jax.random.normal(real_key, full_shape, jnp.float32), -4.0, 4.0) * (0.7 / math.sqrt(BO))
    imag_noise = jnp.clip(jax.random.normal(imag_key, full_shape, jnp.float32), -4.0, 4.0) * (0.3 / math.sqrt(BO))
    real_part = on_diagonal * strength + (1.0 - on_diagonal) * real_noise
    return jnp.stack([real_part, imag_noise])


def draw_lower(key, part):
    return coupling_draw(key, 23)


def draw_upper(key, part):
    return coupling_draw(key, 37)


def block_scale(stream_key, dims, cuts, least, top_value):
    loudness, own = 1.0, jax.random.fold_in(stream_key, 6)
    for dim, shards_of in cuts:
        steps = jnp.exp(jax.random.uniform(jax.random.fold_in(own, dim), (shards_of,), jnp.float32, least / len(cuts), top_value / len(cuts)))
        loudness = loudness * jnp.repeat(steps, dims[dim] // shards_of).reshape([-1 if axis == dim else 1 for axis in range(len(dims))])
    return loudness


def bell_draw(rng, extent, deviation, reach, cuts=(), held_as=jnp.bfloat16):
    level = block_scale(rng, extent, cuts, -0.22, 0.18) if cuts else 1.0
    values = jax.random.normal(rng, extent, jnp.float32) * deviation * level
    return jnp.minimum(jnp.maximum(values, -reach), reach).astype(held_as)


def setup_inputs(seed: int = 0) -> dict:
    seeds = jax.random.split(jax.random.key(seed), 7)
    return {
        "g_lesser": bell_draw(seeds[0], (2, NE, NB * BO, BO), 0.12, 0.75, ((1, 8), (2, 4)), jnp.float32),
        "g_greater": bell_draw(seeds[1], (2, NE, NB * BO, BO), 0.12, 0.75, ((1, 8), (2, 4)), jnp.float32),
        "onsite": draw_onsite(jax.random.fold_in(seeds[6], 71), 0),
        "lower": draw_lower(jax.random.fold_in(seeds[6], 71), 0),
        "upper": draw_upper(jax.random.fold_in(seeds[6], 71), 0),
        "rhs": bell_draw(seeds[5], (2, NE, NB * BO, NR), 3.0, 16.0, ((1, 8), (2, 4)), jnp.float32),
    }


diagonal_guess = 5.0

def complex_product(left_factor, right_factor):
    exact_mode = lax.Precision.HIGHEST
    real_part = jnp.matmul(left_factor[0], right_factor[0], precision=exact_mode) - jnp.matmul(left_factor[1], right_factor[1], precision=exact_mode)
    imag_part = jnp.matmul(left_factor[0], right_factor[1], precision=exact_mode) + jnp.matmul(left_factor[1], right_factor[0], precision=exact_mode)
    return jnp.stack([real_part, imag_part])

def newton_inverse(matrix):
    block_order = matrix.shape[-1]
    identity = jnp.eye(block_order, dtype=jnp.float32)
    guess_real = jnp.broadcast_to(identity / diagonal_guess, matrix.shape[1:]).astype(jnp.float32)
    current = jnp.stack([guess_real, jnp.zeros_like(guess_real)])
    for sweep_index in range(NS_STEPS):
        product = complex_product(matrix, current)
        residue = jnp.stack([2.0 * identity - product[0], -product[1]])
        current = complex_product(current, residue)
    return current

def convolve(pair_arrays):
    lesser_part, greater_part = pair_arrays
    energies = lesser_part.shape[1]
    padded = jnp.concatenate([jnp.zeros_like(greater_part), greater_part], axis=1)

    def one_shift(offset):
        shifted = lax.dynamic_slice_in_dim(padded, (energies - offset).astype(jnp.int32), energies, 1)
        real_part = lax.optimization_barrier(jnp.sum(lesser_part[0] * shifted[0] - lesser_part[1] * shifted[1], axis=0))
        imag_part = lax.optimization_barrier(jnp.sum(lesser_part[0] * shifted[1] + lesser_part[1] * shifted[0], axis=0))
        return jnp.stack([real_part, imag_part])
    stacked = lax.map(one_shift, jnp.arange(energies, dtype=jnp.int32))
    return jnp.swapaxes(stacked, 0, 1) * (1.0 / math.sqrt(energies))

def from_before(values, stride):
    return jnp.concatenate([jnp.zeros_like(values[:, :, :stride]), values[:, :, :-stride]], axis=2)

def from_after(values, stride):
    return jnp.concatenate([values[:, :, stride:], jnp.zeros_like(values[:, :, :stride])], axis=2)

def reference(g_lesser, g_greater, onsite, lower, upper, rhs):
    lesser_blocks = g_lesser.reshape(2, NE, NB, BO, BO).transpose(2, 0, 1, 3, 4)
    greater_blocks = g_greater.reshape(2, NE, NB, BO, BO).transpose(2, 0, 1, 3, 4)
    polar = lax.map(convolve, (lesser_blocks, greater_blocks)).transpose(1, 2, 0, 3, 4)
    diag = onsite.reshape(2, NE, NB, BO, BO) - polar
    first_mask = (jnp.arange(NB) > 0).astype(jnp.float32)[None, :, None, None]
    last_mask = (jnp.arange(NB) < NB - 1).astype(jnp.float32)[None, :, None, None]
    lower_full = jnp.broadcast_to((lower.reshape(2, NB, BO, BO) * first_mask)[:, None], (2, NE, NB, BO, BO))
    upper_full = jnp.broadcast_to((upper.reshape(2, NB, BO, BO) * last_mask)[:, None], (2, NE, NB, BO, BO))
    source = rhs.reshape(2, NE, NB, BO, NR)
    for depth_index in range(LEVELS):
        stride = 1 << depth_index
        inverse = newton_inverse(diag)
        alpha = complex_product(inverse, lower_full)
        beta = complex_product(inverse, upper_full)
        rho = complex_product(inverse, source)
        alpha_left = from_before(alpha, stride)
        beta_left = from_before(beta, stride)
        rho_left = from_before(rho, stride)
        alpha_right = from_after(alpha, stride)
        beta_right = from_after(beta, stride)
        rho_right = from_after(rho, stride)
        diag = diag - complex_product(lower_full, beta_left) - complex_product(upper_full, alpha_right)
        source = source - complex_product(lower_full, rho_left) - complex_product(upper_full, rho_right)
        new_lower = -complex_product(lower_full, alpha_left)
        new_upper = -complex_product(upper_full, beta_right)
        lower_full = new_lower
        upper_full = new_upper
    solution = complex_product(newton_inverse(diag), source)
    return solution.reshape(2, NE, NB * BO, NR)
```

```python
import math

import jax
import jax.numpy as jnp
from jax import lax
from jax.experimental import pallas as pl
from jax.experimental.pallas import tpu as pltpu
from jax.sharding import PartitionSpec as P

diagonal_guess = 5.0
MODE = lax.Precision.HIGH
MESH = pl.DeviceIdType.MESH


def real_product(a, b):
    return jnp.matmul(a, b, precision=MODE)


def product(a, b):
    ar, ai = a
    br, bi = b
    return (
        real_product(ar, br) - real_product(ai, bi),
        real_product(ar, bi) + real_product(ai, br),
    )


def parts(a):
    return a[0], a[1]


def plus(a, b):
    return a[0] + b[0], a[1] + b[1]


def minus(a, b):
    return a[0] - b[0], a[1] - b[1]


def wide(*pieces):
    return tuple(jnp.concatenate([p[k] for p in pieces], axis=-1) for k in (0, 1))


def cut(a, start, stop):
    return a[0][:, start:stop], a[1][:, start:stop]


def remainder(matrix):
    eye = jnp.eye(matrix[0].shape[-1], dtype=jnp.float32)
    return eye - matrix[0] * (1.0 / diagonal_guess), -matrix[1] * (1.0 / diagonal_guess)


def inverse(matrix):
    eye = jnp.eye(matrix[0].shape[-1], dtype=jnp.float32)
    b = remainder(matrix)
    square = product(b, b)
    cube = product(b, square)
    scale = 1.0 / diagonal_guess
    return (eye + b[0] + square[0] + cube[0]) * scale, (b[1] + square[1] + cube[1]) * scale


def solve(matrix, source):
    b = remainder(matrix)
    value = source
    for _ in range(3):
        value = plus(source, product(b, value))
    scale = 1.0 / diagonal_guess
    return value[0] * scale, value[1] * scale


def front_kernel(
    gl, gg, onsite, lower, upper, rhs, diag, near_lu, near_s,
    lu, gl_all, gg_all, res, pol,
    in_send, in_recv, out_send, out_recv, lu_send, lu_recv, hop_send, hop_recv,
    mate_send, mate_recv, local, rows_out=None, partner=None,
):
    e, i = lax.axis_index("energy"), lax.axis_index("block")
    energies, count = lax.axis_size("energy"), lax.axis_size("block")
    share = gl.shape[2] // energies
    c, p = lax.rem(e, 2), lax.rem(i, 2)
    mate, side = e + 1 - 2 * c, 1 - p
    pair, onward, behind = i + 1 - 2 * p, i + 2 - 4 * p, i - 2 + 4 * p
    has_onward = jnp.logical_and(onward >= 0, onward < count)
    has_behind = jnp.logical_and(behind >= 0, behind < count)

    fill = [pltpu.make_async_copy((lower, upper)[k], lu.at[k], local.at[k]) for k in (0, 1)]
    for copy in fill:
        copy.start()
    barrier = pltpu.get_barrier_semaphore()
    for k in range(1, energies):
        pl.semaphore_signal(barrier, inc=1, device_id={"energy": lax.rem(e + k, energies)}, device_id_type=MESH)
    pl.semaphore_signal(barrier, inc=1, device_id={"block": pair}, device_id_type=MESH)

    @pl.when(has_onward)
    def _():
        pl.semaphore_signal(barrier, inc=1, device_id={"block": onward}, device_id_type=MESH)

    @pl.when(has_behind)
    def _():
        pl.semaphore_signal(barrier, inc=1, device_id={"block": behind}, device_id_type=MESH)

    peers = energies
    if partner is not None:
        peers = energies + 1
        pl.semaphore_signal(barrier, inc=1, device_id={"block": partner}, device_id_type=MESH)
    pl.semaphore_wait(barrier, peers + has_onward.astype(jnp.int32) + has_behind.astype(jnp.int32))

    def remote(src, dst, send, recv, **where):
        return pltpu.make_async_remote_copy(
            src_ref=src, dst_ref=dst, send_sem=send, recv_sem=recv, device_id=where, device_id_type=MESH
        )

    part = share // 2

    def in_copy(h, k, q, source):
        src, dst = ((gl, gl_all), (gg, gg_all))[k]
        rows = src.at[:, 0, pl.ds(q * share + h * part, part), :]
        there = dst.at[source, :, pl.ds(h * part, part), :]
        return remote(rows, there, in_send.at[h, k, q], in_recv.at[h, k, source], energy=q)

    def out_copy(h, w, source):
        rows = pl.ds(h * part, part)
        return remote(
            res.at[w, :, rows, :], pol.at[source, :, rows, :], out_send.at[h, w], out_recv.at[h, source], energy=w
        )

    for copy in fill:
        copy.wait()
    for h in (0, 1):
        for k in (0, 1):
            for q in range(energies):

                @pl.when(q != e)
                def _():
                    in_copy(h, k, q, e).start()

    own = []
    for k, (src, dst) in enumerate(((gl, gl_all), (gg, gg_all))):
        rows = src.at[:, 0, pl.ds(pl.multiple_of(e * share, 8), share), :]
        own.append(pltpu.make_async_copy(rows, dst.at[e], local.at[k]))
        own[-1].start()

    mine = (lu.at[c, 0], lu.at[c, 1], rhs.at[:, 0])

    def slot(s, k):
        return near_s.at[s] if k == 2 else near_lu.at[s, c, k]

    direct = [remote(mine[k], slot(p, k), lu_send.at[k], lu_recv.at[k], block=pair) for k in range(3)]
    hops = [remote(slot(side, k), slot(p, k), hop_send.at[k], hop_recv.at[k], block=onward) for k in range(3)]
    for copy in direct:
        copy.start()
    shared = [
        remote(slot(s, k), slot(s, k), mate_send.at[j, k], mate_recv.at[j, k], energy=mate)
        for j, s in enumerate((side, p))
        for k in (0, 1)
    ]
    for k in range(3):
        direct[k].wait_recv()

        @pl.when(has_onward)
        def _():
            hops[k].start()

        if k < 2:
            shared[k].start()

    for copy in own:
        copy.wait()
    scale = 1.0 / math.sqrt(energies)
    for h in (0, 1):
        for k in (0, 1):
            for q in range(energies):

                @pl.when(q != e)
                def _():
                    in_copy(h, k, q, q).wait_recv()

        for w in range(energies):

            def step(row, carry, w=w, h=h):
                rows = pl.ds(pl.multiple_of(h * part + row * 8, 8), 8)
                real = imag = None
                for k in range(w, energies):
                    a, b = gl_all[k, 0, rows], gl_all[k, 1, rows]
                    x, y = gg_all[k - w, 0, rows], gg_all[k - w, 1, rows]
                    s, t = a * x - b * y, a * y + b * x
                    real, imag = (s, t) if real is None else (real + s, imag + t)
                res[w, 0, rows] = real * scale
                res[w, 1, rows] = imag * scale
                return carry

            lax.fori_loop(0, part // 8, step, 0)

            @pl.when(w != e)
            def _():
                out_copy(h, w, e).start()

    keep = pltpu.make_async_copy(res.at[e], pol.at[e], local.at[0])
    keep.start()

    @pl.when(has_behind)
    def _():
        for k in range(3):
            hops[k].wait_recv()
            if k < 2:
                shared[2 + k].start()

    def hand_on(q):
        rows_out[0][q].wait_recv()

        @pl.when(has_onward)
        def _():
            rows_out[1][q].start()

    keep.wait()
    for q in range(energies):

        @pl.when(q != e)
        def _():
            out_copy(0, q, q).wait_recv()
            out_copy(1, q, q).wait_recv()

        rows = pl.ds(q * share, share)
        for k in (0, 1):
            diag[k, rows] = onsite[k, 0, rows] - pol[q, k]
        if rows_out is not None:
            rows_out[0][q].start()
            if q > 0:
                hand_on(q - 1)
    if rows_out is not None:
        hand_on(energies - 1)

    for k in range(2):
        shared[k].wait_recv()

    @pl.when(has_behind)
    def _():
        for k in range(2):
            shared[2 + k].wait()

    for k in range(2):
        shared[k].wait_send()
    for k in range(3):
        direct[k].wait_send()

        @pl.when(has_onward)
        def _():
            hops[k].wait_send()

    for q in range(energies):

        @pl.when(q != e)
        def _():
            for h in (0, 1):
                in_copy(h, 0, q, e).wait_send()
                in_copy(h, 1, q, e).wait_send()
                out_copy(h, q, e).wait_send()


def front(g_lesser, g_greater, onsite, lower, upper, rhs):
    energies = lax.axis_size("energy")
    n, columns = onsite.shape[2], rhs.shape[-1]
    share = n // energies
    vmem = pl.BlockSpec(memory_space=pltpu.VMEM)
    f32 = jnp.float32
    dma = pltpu.SemaphoreType.DMA
    pieces = pltpu.VMEM((energies, 2, share, n), f32)
    return pl.pallas_call(
        front_kernel,
        name="front",
        out_shape=(
            jax.ShapeDtypeStruct((2, n, n), f32),
            jax.ShapeDtypeStruct((2, 2, 2, n, n), f32),
            jax.ShapeDtypeStruct((2, 2, n, columns), f32),
        ),
        in_specs=[vmem] * 6,
        out_specs=(vmem,) * 3,
        scratch_shapes=[
            pltpu.VMEM((2, 2, n, n), f32),
            pieces, pieces, pieces, pieces,
            dma((2, 2, energies)), dma((2, 2, energies)), dma((2, energies)), dma((2, energies)),
            dma((3,)), dma((3,)), dma((3,)), dma((3,)),
            dma((2, 2)), dma((2, 2)), dma((2,)),
        ],
        compiler_params=pltpu.CompilerParams(collective_id=0, has_side_effects=True),
    )(g_lesser, g_greater, onsite, lower, upper, rhs)


def halves(x):
    high = x.astype(jnp.bfloat16)
    return high, (x - high.astype(jnp.float32)).astype(jnp.bfloat16)


def factor(a):
    return halves(a[0]), halves(a[1]), halves(a[0] + a[1])


def three_pass(a, b):
    dot = lambda u, v: jnp.dot(u, v, preferred_element_type=jnp.float32)
    return dot(a[0], b[0]) + (dot(a[0], b[1]) + dot(a[1], b[0]))


def times(a, b):
    first, second, third = (three_pass(a[k], b[k]) for k in range(3))
    return first - second, third - first - second


def inverse_of(matrix):
    eye_rows = lax.broadcasted_iota(jnp.int32, matrix[0].shape, 0)
    eye_columns = lax.broadcasted_iota(jnp.int32, matrix[0].shape, 1)
    eye = jnp.where(eye_rows == eye_columns, 1.0, 0.0)
    scale = 1.0 / diagonal_guess
    b = eye - matrix[0] * scale, -matrix[1] * scale
    fb = factor(b)
    square = times(fb, fb)
    cube = times(fb, factor(square))
    return (eye + b[0] + square[0] + cube[0]) * scale, (b[1] + square[1] + cube[1]) * scale


def line_kernel(
    gl, gg, onsite, lower, upper, rhs, out,
    gl2, gg2, on2, zin, res, pin, dpair, diag, src, lu, dp, fp, sp, value,
    z_send, z_recv, p_send, p_recv, pair_send, pair_recv, pair_local,
    d_send, d_recv, d_local, dm_send, dm_recv,
    s_send, s_recv, s_local, sm_send, sm_recv,
    l_send, l_recv, l_local, lm_send, lm_recv, out_sem,
):
    e, i = lax.axis_index("energy"), lax.axis_index("block")
    energies, count = lax.axis_size("energy"), lax.axis_size("block")
    n = diag.shape[-1]
    chunks, r = zin.shape[0], zin.shape[3]
    half = n // 2
    mid = energies // 2
    z, h = e // 2, lax.rem(e, 2)
    y, x = i // 2, lax.rem(i, 2)
    sib, xn, yn = e + 1 - 2 * h, i + 1 - 2 * x, i + 2 - 4 * y
    dn = yn + 1 - 2 * x
    outer, inner, center, far = z == 0, z == 1, z == 2, z == 3
    mine = pl.ds(pl.multiple_of(h * half, half), half)
    other = pl.ds(pl.multiple_of((1 - h) * half, half), half)
    scale = 1.0 / math.sqrt(energies)

    def remote(a, b, send, recv, energy=e, block=i):
        return pltpu.make_async_remote_copy(
            src_ref=a, dst_ref=b, send_sem=send, recv_sem=recv,
            device_id={"energy": energy, "block": block}, device_id_type=MESH,
        )

    barrier = pltpu.get_barrier_semaphore()
    for k in range(1, energies):
        pl.semaphore_signal(barrier, inc=1, device_id={"energy": lax.rem(e + k, energies)}, device_id_type=MESH)
    for block in (xn, yn):
        for c in (0, 1):
            pl.semaphore_signal(
                barrier, inc=1, device_id={"energy": 2 * z + c, "block": block}, device_id_type=MESH
            )
    pair_own = []
    for k, (a, b) in enumerate(((gg, gg2), (gl, gl2), (onsite, on2))):
        pair_own.append(pltpu.make_async_copy(a.at[:, 0, mine], b.at[h], pair_local.at[k]))
        pair_own[-1].start()
    pl.semaphore_wait(barrier, energies + 3)

    def piece(a, g, k):
        return a.at[:, 0, pl.ds(pl.multiple_of(g * half + k * r, 8), r)]

    def z_copies(k, which):
        def to(a, slot, g, base, sem):
            return remote(piece(a, g, k), zin.at[k, slot], z_send.at[sem], z_recv.at[k], energy=base + g)

        for g in (0, 1):
            if which == 0:
                to(gg, e, g, mid, 0).start()
                to(gg, e, g, mid - 2, 1).start()
            elif which == 1:
                to(gg, e, g, mid, 0).start()
            else:
                to(gl, e - mid + 2, g, mid, 1).start()
                to(gg, e - mid + 4, g, mid, 0).start()

    for which, role in ((0, outer), (1, inner), (3, far)):

        @pl.when(role)
        def _(which=which):
            def body(k, carry):
                z_copies(k, which)
                return carry

            lax.fori_loop(0, chunks, body, 0)

    pairs = []
    for k, (a, b) in enumerate(((gg, gg2), (gl, gl2), (onsite, on2))):
        pairs.append(remote(a.at[:, 0, other], b.at[h], pair_send.at[k], pair_recv.at[k], energy=sib))
        pairs[-1].start()

    def valid(j, w):
        return j > 0 if w == 0 else j < count - 1

    coupling = (lower, upper)
    for w in (0, 1):

        @pl.when(valid(i, w))
        def _(w=w):
            remote(coupling[w].at[:, mine], lu.at[i, w, :, mine], l_send.at[0, w], l_recv.at[0, w], block=xn).start()
            remote(coupling[w].at[:, mine], lu.at[i, w, :, mine], l_send.at[1, w], l_recv.at[1, w], block=yn).start()
            pltpu.make_async_copy(coupling[w], lu.at[i, w], l_local.at[w]).start()

    def rows_of(g):
        return pl.ds(g * half, half)

    @pl.when(y == h)
    def _():
        pltpu.make_async_copy(rhs.at[:, 0], src.at[i], s_local).start()
        remote(rhs.at[:, 0], src.at[i], sm_send.at[0], sm_recv.at[0], energy=sib).start()
        for g in (0, 1):
            remote(
                rhs.at[:, 0, rows_of(g)], src.at[i, :, rows_of(g)], s_send.at[0], s_recv.at[0],
                energy=2 * z + g, block=xn,
            ).start()

    @pl.when(y != h)
    def _():
        for g in (0, 1):
            remote(
                rhs.at[:, 0, rows_of(g)], src.at[i, :, rows_of(g)], s_send.at[0], s_recv.at[1],
                energy=2 * z + g, block=yn,
            ).start()

    def arrived(ref, sem):
        remote(ref, ref, sem, sem).wait_recv()

    def sent(ref, sem):
        remote(ref, ref, sem, sem).wait_send()

    def lu_direct_x(w):
        @pl.when(valid(xn, w))
        def _():
            part = lu.at[xn, w, :, mine]
            arrived(part, l_recv.at[0, w])
            remote(part, part, l_send.at[2, w], l_recv.at[2, w], block=yn).start()
            remote(part, part, lm_send.at[0, w], lm_recv.at[0, w], energy=sib).start()

    def lu_direct_y(w):
        @pl.when(valid(yn, w))
        def _():
            part = lu.at[yn, w, :, mine]
            arrived(part, l_recv.at[1, w])
            remote(part, part, lm_send.at[1, w], lm_recv.at[1, w], energy=sib).start()

    def lu_passed(w):
        @pl.when(valid(dn, w))
        def _():
            part = lu.at[dn, w, :, mine]
            arrived(part, l_recv.at[2, w])
            remote(part, part, lm_send.at[2, w], lm_recv.at[2, w], energy=sib).start()

    def src_direct():
        part = src.at[yn, :, mine]
        arrived(part, s_recv.at[1])
        remote(part, part, s_send.at[1], s_recv.at[2], block=xn).start()
        remote(part, part, sm_send.at[2], sm_recv.at[2], energy=sib).start()
        part = src.at[xn, :, mine]
        arrived(part, s_recv.at[0])
        remote(part, part, sm_send.at[1], sm_recv.at[1], energy=sib).start()

    def src_passed():
        part = src.at[dn, :, mine]
        arrived(part, s_recv.at[2])
        remote(part, part, sm_send.at[3], sm_recv.at[3], energy=sib).start()

    for copy in pair_own:
        copy.wait()
    for copy in pairs:
        copy.wait_recv()

    def tiles(k):
        for q in range(r // 8):
            for lane in range(n // 128):
                cols = slice(lane * 128, lane * 128 + 128)
                yield slice(q * 8, q * 8 + 8), pl.ds(pl.multiple_of(k * r + q * 8, 8), 8), cols

    def correlate(left, right, w):
        real = imag = None
        for k in left:
            if k - w in right:
                (a, b), (u, v) = left[k], right[k - w]
                s, t = a * u - b * v, a * v + b * u
                real, imag = (s, t) if real is None else (real + s, imag + t)
        return real, imag

    def p_copies(k):
        ahead = res.at[k, pl.ds(0, 2)]
        return (
            remote(ahead, pin.at[k, pl.ds(0, 2)], p_send.at[0], p_recv.at[k], energy=h),
            remote(res.at[k, pl.ds(2, 2)], pin.at[k, pl.ds(0, 2)], p_send.at[1], p_recv.at[k], energy=2 + h),
            remote(res.at[k, pl.ds(4, 2)], pin.at[k, pl.ds(0, 2)], p_send.at[2], p_recv.at[k], energy=mid + 2 + h),
            remote(ahead, pin.at[k, pl.ds(2, 2)], p_send.at[0], p_recv.at[k], energy=h),
        )

    def polarize(k):
        @pl.when(center)
        def _():
            arrived(zin.at[k], z_recv.at[k])
            for here, rows, cols in tiles(k):
                both = lambda ref, *at: (ref[(*at, 0, here, cols)], ref[(*at, 1, here, cols)])
                pair = lambda ref, c: (ref[c, 0, rows, cols], ref[c, 1, rows, cols])
                left = {mid: pair(gl2, 0), mid + 1: pair(gl2, 1), mid + 2: both(zin, k, 4), mid + 3: both(zin, k, 5)}
                right = {c: both(zin, k, c) for c in range(4)}
                right.update({mid: pair(gg2, 0), mid + 1: pair(gg2, 1)})
                right.update({mid + 2: both(zin, k, 6), mid + 3: both(zin, k, 7)})
                for w in range(energies):
                    value = correlate(left, right, w)
                    for m in (0, 1):
                        if w in (mid, mid + 1):
                            dpair[w - mid, m, rows, cols] = on2[w - mid, m, rows, cols] - value[m] * scale
                        else:
                            res[k, w if w < mid else w - 2, m, here, cols] = value[m]
            for copy in p_copies(k)[:3]:
                copy.start()

        @pl.when(inner)
        def _():
            arrived(zin.at[k, pl.ds(0, 2)], z_recv.at[k])
            for here, rows, cols in tiles(k):
                both = lambda ref, *at: (ref[(*at, 0, here, cols)], ref[(*at, 1, here, cols)])
                pair = lambda ref, c: (ref[c, 0, rows, cols], ref[c, 1, rows, cols])
                left = {2: pair(gl2, 0), 3: pair(gl2, 1)}
                right = {0: both(zin, k, 0), 1: both(zin, k, 1), 2: pair(gg2, 0), 3: pair(gg2, 1)}
                for w in range(mid):
                    value = correlate(left, right, w)
                    for m in (0, 1):
                        res[k, w, m, here, cols] = value[m]
            p_copies(k)[3].start()
            arrived(pin.at[k, pl.ds(0, 2)], p_recv.at[k])
            for here, rows, cols in tiles(k):
                for c in (0, 1):
                    for m in (0, 1):
                        total = res[k, 2 + c, m, here, cols] + pin[k, c, m, here, cols]
                        dpair[c, m, rows, cols] = on2[c, m, rows, cols] - total * scale

        @pl.when(outer)
        def _():
            arrived(pin.at[k], p_recv.at[k])
            for here, rows, cols in tiles(k):
                pair = lambda ref, c: (ref[c, 0, rows, cols], ref[c, 1, rows, cols])
                left = {0: pair(gl2, 0), 1: pair(gl2, 1)}
                right = {0: pair(gg2, 0), 1: pair(gg2, 1)}
                for c in (0, 1):
                    value = correlate(left, right, c)
                    for m in (0, 1):
                        total = value[m] + (pin[k, c, m, here, cols] + pin[k, 2 + c, m, here, cols])
                        dpair[c, m, rows, cols] = on2[c, m, rows, cols] - total * scale

        @pl.when(far)
        def _():
            arrived(pin.at[k, pl.ds(0, 2)], p_recv.at[k])
            for here, rows, cols in tiles(k):
                for c in (0, 1):
                    for m in (0, 1):
                        dpair[c, m, rows, cols] = on2[c, m, rows, cols] - pin[k, c, m, here, cols] * scale

    def strip(k):
        return pl.ds(pl.multiple_of(h * half + k * r, 8), r)

    def spread(k):
        sub = pl.ds(pl.multiple_of(k * r, 8), r)
        there = diag.at[i, :, strip(k)]
        remote(dpair.at[1 - y, :, sub], there, d_send.at[1], d_recv.at[1, k], block=yn).start()
        remote(dpair.at[y, :, sub], there, d_send.at[0], d_recv.at[0, k], block=xn).start()
        remote(dpair.at[y, :, sub], there, dm_send.at[0], dm_recv.at[0], energy=sib).start()
        pltpu.make_async_copy(dpair.at[y, :, sub], there, d_local).start()

    def gather(k):
        part = diag.at[yn, :, strip(k)]
        arrived(part, d_recv.at[1, k])
        remote(part, part, d_send.at[2], d_recv.at[2, k], block=xn).start()
        remote(part, part, dm_send.at[2], dm_recv.at[2], energy=sib).start()
        part = diag.at[xn, :, strip(k)]
        arrived(part, d_recv.at[0, k])
        remote(part, part, dm_send.at[1], dm_recv.at[1], energy=sib).start()

    def gather_passed(k):
        part = diag.at[dn, :, strip(k)]
        arrived(part, d_recv.at[2, k])
        remote(part, part, dm_send.at[3], dm_recv.at[3], energy=sib).start()

    extra = {
        0: [lambda: lu_direct_x(0)],
        1: [lambda: lu_direct_y(0)],
        2: [lambda: lu_direct_x(1)],
        3: [lambda: lu_direct_y(1)],
        4: [src_direct],
        5: [src_passed],
        6: [lambda: lu_passed(0)],
        7: [lambda: lu_passed(1)],
    }

    def turn(k, carry):
        polarize(k)
        spread(k)

        @pl.when(k >= 1)
        def _():
            gather(k - 1)

        @pl.when(k >= 2)
        def _():
            gather_passed(k - 2)

        for at, work in extra.items():

            @pl.when(k == at * chunks // 8)
            def _(work=work):
                for step in work:
                    step()

        return carry

    lax.fori_loop(0, chunks, turn, 0)
    gather(chunks - 1)
    gather_passed(chunks - 2)
    gather_passed(chunks - 1)

    pltpu.make_async_copy(dpair.at[y], diag.at[i, :, mine], d_local).wait()
    for k, j in enumerate((i, xn, yn, dn)):
        arrived(diag.at[j, :, other], dm_recv.at[k])

    for w in (0, 1):

        @pl.when(valid(i, w))
        def _(w=w):
            pltpu.make_async_copy(coupling[w], lu.at[i, w], l_local.at[w]).wait()

        for k, j in enumerate((xn, yn, dn)):

            @pl.when(valid(j, w))
            def _(k=k, j=j, w=w):
                arrived(lu.at[j, w, :, other], lm_recv.at[k, w])

    @pl.when(y == h)
    def _():
        pltpu.make_async_copy(rhs.at[:, 0], src.at[i], s_local).wait()

    @pl.when(y != h)
    def _():
        arrived(src.at[i], sm_recv.at[0])

    for k, j in enumerate((xn, yn, dn)):
        arrived(src.at[j, :, other], sm_recv.at[k + 1])

    a, b, m, q = 3 * x, 2 - x, 1 + x, 3 - 3 * x
    couple = lambda j, w: factor((lu[j, w, 0], lu[j, w, 1]))
    diagonal = lambda j: (diag[j, 0], diag[j, 1])
    source = lambda j: (src[j, 0], src[j, 1])

    def put(ref, at, v):
        ref[at, 0], ref[at, 1] = v

    inv = factor(inverse_of(diagonal(m)))
    sm = factor(source(m))
    to_a, to_b = couple(m, x), couple(m, 1 - x)
    t = factor(times(couple(a, 1 - x), inv))
    put(dp, 0, minus(diagonal(a), times(t, to_a)))
    put(fp, 0, times(t, to_b))
    put(sp, 0, minus(source(a), times(t, sm)))
    t = factor(times(couple(b, x), inv))
    put(dp, 1, minus(diagonal(b), times(t, to_b)))
    put(fp, 1, times(t, to_a))
    put(sp, 1, minus(source(b), times(t, sm)))
    t = factor(times(couple(b, 1 - x), factor(inverse_of(diagonal(q)))))
    put(dp, 1, minus((dp[1, 0], dp[1, 1]), times(t, couple(q, x))))
    put(sp, 1, minus((sp[1, 0], sp[1, 1]), times(t, factor(source(q)))))

    this = jnp.where(h == x, 0, 1)
    that = 1 - this
    at = lambda ref, k: (ref[k, 0], ref[k, 1])
    t = factor(times(factor(at(fp, this)), factor(inverse_of(at(dp, that)))))
    last = minus(at(dp, this), times(t, factor(at(fp, that))))
    right = plus(at(sp, this), times(t, factor(at(sp, that))))
    eye = jnp.where(
        lax.broadcasted_iota(jnp.int32, (n, n), 0) == lax.broadcasted_iota(jnp.int32, (n, n), 1), 1.0, 0.0
    )
    inverse_guess = 1.0 / diagonal_guess
    rest = factor((eye - last[0] * inverse_guess, -last[1] * inverse_guess))
    found = right
    for _ in range(2):
        found = plus(right, times(rest, factor(found)))
    found = plus(right, times(rest, factor(found)))
    value[0], value[1] = found[0] * inverse_guess, found[1] * inverse_guess

    home = remote(value, out.at[:, 0], out_sem.at[0], out_sem.at[1], energy=2 * z + y, block=2 * h + x)
    keep = pltpu.make_async_copy(value, out.at[:, 0], out_sem.at[0])

    @pl.when(h != y)
    def _():
        home.start()

    @pl.when(h == y)
    def _():
        keep.start()
        keep.wait()

    whole_array = gg.at[:, 0]

    @pl.when(outer)
    def _():
        sent(whole_array, z_send.at[0])
        sent(whole_array, z_send.at[1])

    @pl.when(inner)
    def _():
        sent(whole_array, z_send.at[0])
        sent(res.at[:, pl.ds(0, 2)], p_send.at[0])

    @pl.when(far)
    def _():
        sent(whole_array, z_send.at[0])
        sent(whole_array, z_send.at[1])

    @pl.when(center)
    def _():
        for k in range(3):
            sent(res.at[:, pl.ds(2 * k, 2)], p_send.at[k])

    for copy in pairs:
        copy.wait_send()
    for k in range(3):
        sent(dpair.at[0], d_send.at[k])
    for k in range(4):
        sent(dpair.at[0], dm_send.at[k])
    part = src.at[0, :, mine]

    @pl.when(y == h)
    def _():
        sent(rhs.at[:, 0], sm_send.at[0])

    sent(rhs.at[:, 0], s_send.at[0])
    sent(part, s_send.at[1])
    for k in range(3):
        sent(part, sm_send.at[k + 1])
    for w in (0, 1):
        part = lu.at[0, w, :, mine]

        @pl.when(valid(i, w))
        def _(w=w, part=part):
            sent(part, l_send.at[0, w])
            sent(part, l_send.at[1, w])

        for k, j in enumerate((xn, yn, dn)):

            @pl.when(valid(j, w))
            def _(k=k, w=w, part=part):
                if k == 0:
                    sent(part, l_send.at[2, w])
                sent(part, lm_send.at[k, w])

    @pl.when(h != y)
    def _():
        home.wait()


def line(g_lesser, g_greater, onsite, lower, upper, rhs):
    count = lax.axis_size("block")
    n, columns = onsite.shape[2], rhs.shape[-1]
    chunks = 8
    half = n // 2
    r = half // chunks
    f32 = jnp.float32
    dma = pltpu.SemaphoreType.DMA
    anywhere = pl.BlockSpec(memory_space=pl.ANY)
    pair = pltpu.VMEM((2, 2, half, n), f32)
    return pl.pallas_call(
        line_kernel,
        name="line",
        out_shape=jax.ShapeDtypeStruct((2, 1, n, columns), f32),
        in_specs=[anywhere] * 6,
        out_specs=anywhere,
        scratch_shapes=[
            pair, pair, pair,
            pltpu.VMEM((chunks, 8, 2, r, n), f32),
            pltpu.VMEM((chunks, 6, 2, r, n), f32),
            pltpu.VMEM((chunks, 4, 2, r, n), f32),
            pair,
            pltpu.VMEM((count, 2, n, n), f32),
            pltpu.VMEM((count, 2, n, columns), f32),
            pltpu.VMEM((count, 2, 2, n, n), f32),
            pltpu.VMEM((2, 2, n, n), f32),
            pltpu.VMEM((2, 2, n, n), f32),
            pltpu.VMEM((2, 2, n, columns), f32),
            pltpu.VMEM((2, n, columns), f32),
            dma((2,)), dma((chunks,)), dma((3,)), dma((chunks,)), dma((3,)), dma((3,)), dma((3,)),
            dma((3,)), dma((3, chunks)), dma, dma((4,)), dma((4,)),
            dma((2,)), dma((3,)), dma, dma((4,)), dma((4,)),
            dma((3, 2)), dma((3, 2)), dma((2,)), dma((3, 2)), dma((3, 2)), dma((2,)),
        ],
        compiler_params=pltpu.CompilerParams(
            collective_id=1, has_side_effects=True, vmem_limit_bytes=48 * 1024 * 1024
        ),
    )(g_lesser, g_greater, onsite, lower, upper, rhs)


def shifted(value, steps):
    count = lax.axis_size("block")
    leading, last = max(0, -steps), min(count, count - steps)
    pairs = [(k, k + steps) for k in range(leading, last)]
    return lax.ppermute(value, "block", pairs)


def shards(g_lesser, g_greater, onsite, lower, upper, rhs):
    index = lax.axis_index("block")
    count = lax.axis_size("block")
    levels = count.bit_length() - 1
    n = onsite.shape[-1]
    both = jnp.concatenate(
        [jnp.where(index > 0, lower, 0.0), jnp.where(index < count - 1, upper, 0.0)], axis=-1
    )
    if levels == 2 and lax.axis_size("energy") == 8:
        return line(g_lesser, g_greater, onsite, lower, upper, rhs)
    diag, near_lu, near_s = front(g_lesser, g_greater, onsite, lower, upper, rhs)
    diag = parts(diag)
    first, final = index < 2, index >= count - 2
    low, up = cut(parts(both), 0, n), cut(parts(both), n, 2 * n)
    source = parts(rhs[:, 0])
    for depth in range(levels):
        stride = 1 << depth
        inv = inverse(diag)
        if depth == levels - 1:
            coupling = tuple(jnp.where(index < stride, up[k], low[k]) for k in (0, 1))
            sent = product(inv, wide(coupling, source))
            swap = [(k, k ^ stride) for k in range(count)]
            got = parts(lax.ppermute(jnp.stack(sent), "block", swap))
            change = product(coupling, got)
            diag = minus(diag, cut(change, 0, n))
            source = minus(source, cut(change, n, None))
        elif depth == 0:
            packed = jnp.stack(inv)
            inv_left, inv_right = parts(shifted(packed, 1)), parts(shifted(packed, -1))
            t, w = product(low, inv_left), product(up, inv_right)
            lu_l, lu_r = near_lu[0], near_lu[1]
            change = product(t, wide(parts(lu_l[0]), parts(lu_l[1]), parts(near_s[0])))
            other = product(w, wide(parts(lu_r[0]), parts(lu_r[1]), parts(near_s[1])))
            change = tuple(jnp.where(index > 0, v, 0.0) for v in change)
            other = tuple(jnp.where(index < count - 1, v, 0.0) for v in other)
            diag = minus(minus(diag, cut(change, n, 2 * n)), cut(other, 0, n))
            source = minus(minus(source, cut(change, 2 * n, None)), cut(other, 2 * n, None))
            low = tuple(jnp.where(first, 0.0, -v) for v in cut(change, 0, n))
            up = tuple(jnp.where(final, 0.0, -v) for v in cut(other, n, 2 * n))
        else:
            sent = jnp.stack(product(inv, wide(low, up, source)))
            left, right = parts(shifted(sent, stride)), parts(shifted(sent, -stride))
            change, other = product(low, left), product(up, right)
            diag = minus(minus(diag, cut(change, n, 2 * n)), cut(other, 0, n))
            source = minus(minus(source, cut(change, 2 * n, None)), cut(other, 2 * n, None))
            low = tuple(-v for v in cut(change, 0, n))
            up = tuple(-v for v in cut(other, n, 2 * n))
    return jnp.stack(solve(diag, source))[:, None]


def solution(mesh):
    placed = (
        P(None, "energy", "block", None),
        P(None, "energy", "block", None),
        P(None, "energy", "block", None),
        P(None, "block", None),
        P(None, "block", None),
        P(None, "energy", "block", None),
    )
    return jax.shard_map(
        shards,
        mesh=mesh,
        in_specs=placed,
        out_specs=P(None, "energy", "block", None),
        check_vma=False,
    )
```

```python
import math

import jax
import jax.numpy as jnp
from jax import lax
from jax.experimental import pallas as pl
from jax.experimental.pallas import tpu as pltpu
from jax.sharding import PartitionSpec as P

diagonal_guess = 5.0
MODE = lax.Precision.HIGH
MESH = pl.DeviceIdType.MESH


def real_product(a, b):
    return jnp.matmul(a, b, precision=MODE)


def product(a, b):
    ar, ai = a
    br, bi = b
    return (
        real_product(ar, br) - real_product(ai, bi),
        real_product(ar, bi) + real_product(ai, br),
    )


def parts(a):
    return a[0], a[1]


def plus(a, b):
    return a[0] + b[0], a[1] + b[1]


def minus(a, b):
    return a[0] - b[0], a[1] - b[1]


def wide(*pieces):
    return tuple(jnp.concatenate([p[k] for p in pieces], axis=-1) for k in (0, 1))


def cut(a, start, stop):
    return a[0][:, start:stop], a[1][:, start:stop]


def remainder(matrix):
    eye = jnp.eye(matrix[0].shape[-1], dtype=jnp.float32)
    return eye - matrix[0] * (1.0 / diagonal_guess), -matrix[1] * (1.0 / diagonal_guess)


def inverse(matrix):
    eye = jnp.eye(matrix[0].shape[-1], dtype=jnp.float32)
    b = remainder(matrix)
    square = product(b, b)
    cube = product(b, square)
    scale = 1.0 / diagonal_guess
    return (eye + b[0] + square[0] + cube[0]) * scale, (b[1] + square[1] + cube[1]) * scale


def solve(matrix, source):
    b = remainder(matrix)
    value = source
    for _ in range(3):
        value = plus(source, product(b, value))
    scale = 1.0 / diagonal_guess
    return value[0] * scale, value[1] * scale


def front_kernel(
    gl, gg, onsite, lower, upper, rhs, diag, near_lu, near_s,
    lu, gl_all, gg_all, res, pol,
    in_send, in_recv, out_send, out_recv, lu_send, lu_recv, hop_send, hop_recv,
    mate_send, mate_recv, local, rows_out=None, partner=None,
):
    e, i = lax.axis_index("energy"), lax.axis_index("block")
    energies, count = lax.axis_size("energy"), lax.axis_size("block")
    share = gl.shape[2] // energies
    c, p = lax.rem(e, 2), lax.rem(i, 2)
    mate, side = e + 1 - 2 * c, 1 - p
    pair, onward, behind = i + 1 - 2 * p, i + 2 - 4 * p, i - 2 + 4 * p
    has_onward = jnp.logical_and(onward >= 0, onward < count)
    has_behind = jnp.logical_and(behind >= 0, behind < count)

    fill = [pltpu.make_async_copy((lower, upper)[k], lu.at[k], local.at[k]) for k in (0, 1)]
    for copy in fill:
        copy.start()
    barrier = pltpu.get_barrier_semaphore()
    for k in range(1, energies):
        pl.semaphore_signal(barrier, inc=1, device_id={"energy": lax.rem(e + k, energies)}, device_id_type=MESH)
    pl.semaphore_signal(barrier, inc=1, device_id={"block": pair}, device_id_type=MESH)

    @pl.when(has_onward)
    def _():
        pl.semaphore_signal(barrier, inc=1, device_id={"block": onward}, device_id_type=MESH)

    @pl.when(has_behind)
    def _():
        pl.semaphore_signal(barrier, inc=1, device_id={"block": behind}, device_id_type=MESH)

    peers = energies
    if partner is not None:
        peers = energies + 1
        pl.semaphore_signal(barrier, inc=1, device_id={"block": partner}, device_id_type=MESH)
    pl.semaphore_wait(barrier, peers + has_onward.astype(jnp.int32) + has_behind.astype(jnp.int32))

    def remote(src, dst, send, recv, **where):
        return pltpu.make_async_remote_copy(
            src_ref=src, dst_ref=dst, send_sem=send, recv_sem=recv, device_id=where, device_id_type=MESH
        )

    part = share // 2

    def in_copy(h, k, q, source):
        src, dst = ((gl, gl_all), (gg, gg_all))[k]
        rows = src.at[:, 0, pl.ds(q * share + h * part, part), :]
        there = dst.at[source, :, pl.ds(h * part, part), :]
        return remote(rows, there, in_send.at[h, k, q], in_recv.at[h, k, source], energy=q)

    def out_copy(h, w, source):
        rows = pl.ds(h * part, part)
        return remote(
            res.at[w, :, rows, :], pol.at[source, :, rows, :], out_send.at[h, w], out_recv.at[h, source], energy=w
        )

    for copy in fill:
        copy.wait()
    for h in (0, 1):
        for k in (0, 1):
            for q in range(energies):

                @pl.when(q != e)
                def _():
                    in_copy(h, k, q, e).start()

    own = []
    for k, (src, dst) in enumerate(((gl, gl_all), (gg, gg_all))):
        rows = src.at[:, 0, pl.ds(pl.multiple_of(e * share, 8), share), :]
        own.append(pltpu.make_async_copy(rows, dst.at[e], local.at[k]))
        own[-1].start()

    mine = (lu.at[c, 0], lu.at[c, 1], rhs.at[:, 0])

    def slot(s, k):
        return near_s.at[s] if k == 2 else near_lu.at[s, c, k]

    direct = [remote(mine[k], slot(p, k), lu_send.at[k], lu_recv.at[k], block=pair) for k in range(3)]
    hops = [remote(slot(side, k), slot(p, k), hop_send.at[k], hop_recv.at[k], block=onward) for k in range(3)]
    for copy in direct:
        copy.start()
    shared = [
        remote(slot(s, k), slot(s, k), mate_send.at[j, k], mate_recv.at[j, k], energy=mate)
        for j, s in enumerate((side, p))
        for k in (0, 1)
    ]
    for k in range(3):
        direct[k].wait_recv()

        @pl.when(has_onward)
        def _():
            hops[k].start()

        if k < 2:
            shared[k].start()

    for copy in own:
        copy.wait()
    scale = 1.0 / math.sqrt(energies)
    for h in (0, 1):
        for k in (0, 1):
            for q in range(energies):

                @pl.when(q != e)
                def _():
                    in_copy(h, k, q, q).wait_recv()

        for w in range(energies):

            def step(row, carry, w=w, h=h):
                rows = pl.ds(pl.multiple_of(h * part + row * 8, 8), 8)
                real = imag = None
                for k in range(w, energies):
                    a, b = gl_all[k, 0, rows], gl_all[k, 1, rows]
                    x, y = gg_all[k - w, 0, rows], gg_all[k - w, 1, rows]
                    s, t = a * x - b * y, a * y + b * x
                    real, imag = (s, t) if real is None else (real + s, imag + t)
                res[w, 0, rows] = real * scale
                res[w, 1, rows] = imag * scale
                return carry

            lax.fori_loop(0, part // 8, step, 0)

            @pl.when(w != e)
            def _():
                out_copy(h, w, e).start()

    keep = pltpu.make_async_copy(res.at[e], pol.at[e], local.at[0])
    keep.start()

    @pl.when(has_behind)
    def _():
        for k in range(3):
            hops[k].wait_recv()
            if k < 2:
                shared[2 + k].start()

    def hand_on(q):
        rows_out[0][q].wait_recv()

        @pl.when(has_onward)
        def _():
            rows_out[1][q].start()

    keep.wait()
    for q in range(energies):

        @pl.when(q != e)
        def _():
            out_copy(0, q, q).wait_recv()
            out_copy(1, q, q).wait_recv()

        rows = pl.ds(q * share, share)
        for k in (0, 1):
            diag[k, rows] = onsite[k, 0, rows] - pol[q, k]
        if rows_out is not None:
            rows_out[0][q].start()
            if q > 0:
                hand_on(q - 1)
    if rows_out is not None:
        hand_on(energies - 1)

    for k in range(2):
        shared[k].wait_recv()

    @pl.when(has_behind)
    def _():
        for k in range(2):
            shared[2 + k].wait()

    for k in range(2):
        shared[k].wait_send()
    for k in range(3):
        direct[k].wait_send()

        @pl.when(has_onward)
        def _():
            hops[k].wait_send()

    for q in range(energies):

        @pl.when(q != e)
        def _():
            for h in (0, 1):
                in_copy(h, 0, q, e).wait_send()
                in_copy(h, 1, q, e).wait_send()
                out_copy(h, q, e).wait_send()


def front(g_lesser, g_greater, onsite, lower, upper, rhs):
    energies = lax.axis_size("energy")
    n, columns = onsite.shape[2], rhs.shape[-1]
    share = n // energies
    vmem = pl.BlockSpec(memory_space=pltpu.VMEM)
    f32 = jnp.float32
    dma = pltpu.SemaphoreType.DMA
    pieces = pltpu.VMEM((energies, 2, share, n), f32)
    return pl.pallas_call(
        front_kernel,
        name="front",
        out_shape=(
            jax.ShapeDtypeStruct((2, n, n), f32),
            jax.ShapeDtypeStruct((2, 2, 2, n, n), f32),
            jax.ShapeDtypeStruct((2, 2, n, columns), f32),
        ),
        in_specs=[vmem] * 6,
        out_specs=(vmem,) * 3,
        scratch_shapes=[
            pltpu.VMEM((2, 2, n, n), f32),
            pieces, pieces, pieces, pieces,
            dma((2, 2, energies)), dma((2, 2, energies)), dma((2, energies)), dma((2, energies)),
            dma((3,)), dma((3,)), dma((3,)), dma((3,)),
            dma((2, 2)), dma((2, 2)), dma((2,)),
        ],
        compiler_params=pltpu.CompilerParams(collective_id=0, has_side_effects=True),
    )(g_lesser, g_greater, onsite, lower, upper, rhs)


def halves(x):
    high = x.astype(jnp.bfloat16)
    return high, (x - high.astype(jnp.float32)).astype(jnp.bfloat16)


def factor(a):
    return halves(a[0]), halves(a[1]), halves(a[0] + a[1])


def three_pass(a, b):
    dot = lambda u, v: jnp.dot(u, v, preferred_element_type=jnp.float32)
    return dot(a[0], b[0]) + (dot(a[0], b[1]) + dot(a[1], b[0]))


def times(a, b):
    first, second, third = (three_pass(a[k], b[k]) for k in range(3))
    return first - second, third - first - second


def inverse_of(matrix):
    eye_rows = lax.broadcasted_iota(jnp.int32, matrix[0].shape, 0)
    eye_columns = lax.broadcasted_iota(jnp.int32, matrix[0].shape, 1)
    eye = jnp.where(eye_rows == eye_columns, 1.0, 0.0)
    scale = 1.0 / diagonal_guess
    b = eye - matrix[0] * scale, -matrix[1] * scale
    fb = factor(b)
    square = times(fb, fb)
    cube = times(fb, factor(square))
    return (eye + b[0] + square[0] + cube[0]) * scale, (b[1] + square[1] + cube[1]) * scale


def line_kernel(
    gl, gg, onsite, lower, upper, rhs, out,
    gl2, gg2, on2, zin, res, pin, dpair, diag, src, lu, dp, fp, sp, value,
    z_send, z_recv, p_send, p_recv, pair_send, pair_recv, pair_local,
    d_send, d_recv, d_local, dm_send, dm_recv,
    s_send, s_recv, s_local, sm_send, sm_recv,
    l_send, l_recv, l_local, lm_send, lm_recv, out_sem,
):
    e, i = lax.axis_index("energy"), lax.axis_index("block")
    energies, count = lax.axis_size("energy"), lax.axis_size("block")
    n = diag.shape[-1]
    chunks, r = zin.shape[0], zin.shape[3]
    half = n // 2
    mid = energies // 2
    z, h = e // 2, lax.rem(e, 2)
    y, x = i // 2, lax.rem(i, 2)
    sib, xn, yn = e + 1 - 2 * h, i + 1 - 2 * x, i + 2 - 4 * y
    dn = yn + 1 - 2 * x
    outer, inner, center, far = z == 0, z == 1, z == 2, z == 3
    mine = pl.ds(pl.multiple_of(h * half, half), half)
    other = pl.ds(pl.multiple_of((1 - h) * half, half), half)
    scale = 1.0 / math.sqrt(energies)

    def remote(a, b, send, recv, energy=e, block=i):
        return pltpu.make_async_remote_copy(
            src_ref=a, dst_ref=b, send_sem=send, recv_sem=recv,
            device_id={"energy": energy, "block": block}, device_id_type=MESH,
        )

    barrier = pltpu.get_barrier_semaphore()
    for k in range(1, energies):
        pl.semaphore_signal(barrier, inc=1, device_id={"energy": lax.rem(e + k, energies)}, device_id_type=MESH)
    for block in (xn, yn):
        for c in (0, 1):
            pl.semaphore_signal(
                barrier, inc=1, device_id={"energy": 2 * z + c, "block": block}, device_id_type=MESH
            )
    pair_own = []
    for k, (a, b) in enumerate(((gg, gg2), (gl, gl2), (onsite, on2))):
        pair_own.append(pltpu.make_async_copy(a.at[:, 0, mine], b.at[h], pair_local.at[k]))
        pair_own[-1].start()
    pl.semaphore_wait(barrier, energies + 3)

    def piece(a, g, k):
        return a.at[:, 0, pl.ds(pl.multiple_of(g * half + k * r, 8), r)]

    def z_copies(k, which):
        def to(a, slot, g, base, sem):
            return remote(piece(a, g, k), zin.at[k, slot], z_send.at[sem], z_recv.at[k], energy=base + g)

        for g in (0, 1):
            if which == 0:
                to(gg, e, g, mid, 0).start()
                to(gg, e, g, mid - 2, 1).start()
            elif which == 1:
                to(gg, e, g, mid, 0).start()
            else:
                to(gl, e - mid + 2, g, mid, 1).start()
                to(gg, e - mid + 4, g, mid, 0).start()

    for which, role in ((0, outer), (1, inner), (3, far)):

        @pl.when(role)
        def _(which=which):
            def body(k, carry):
                z_copies(k, which)
                return carry

            lax.fori_loop(0, chunks, body, 0)

    pairs = []
    for k, (a, b) in enumerate(((gg, gg2), (gl, gl2), (onsite, on2))):
        pairs.append(remote(a.at[:, 0, other], b.at[h], pair_send.at[k], pair_recv.at[k], energy=sib))
        pairs[-1].start()

    def valid(j, w):
        return j > 0 if w == 0 else j < count - 1

    coupling = (lower, upper)
    for w in (0, 1):

        @pl.when(valid(i, w))
        def _(w=w):
            remote(coupling[w].at[:, mine], lu.at[i, w, :, mine], l_send.at[0, w], l_recv.at[0, w], block=xn).start()
            remote(coupling[w].at[:, mine], lu.at[i, w, :, mine], l_send.at[1, w], l_recv.at[1, w], block=yn).start()
            pltpu.make_async_copy(coupling[w], lu.at[i, w], l_local.at[w]).start()

    def rows_of(g):
        return pl.ds(g * half, half)

    @pl.when(y == h)
    def _():
        pltpu.make_async_copy(rhs.at[:, 0], src.at[i], s_local).start()
        remote(rhs.at[:, 0], src.at[i], sm_send.at[0], sm_recv.at[0], energy=sib).start()
        for g in (0, 1):
            remote(
                rhs.at[:, 0, rows_of(g)], src.at[i, :, rows_of(g)], s_send.at[0], s_recv.at[0],
                energy=2 * z + g, block=xn,
            ).start()

    @pl.when(y != h)
    def _():
        for g in (0, 1):
            remote(
                rhs.at[:, 0, rows_of(g)], src.at[i, :, rows_of(g)], s_send.at[0], s_recv.at[1],
                energy=2 * z + g, block=yn,
            ).start()

    def arrived(ref, sem):
        remote(ref, ref, sem, sem).wait_recv()

    def sent(ref, sem):
        remote(ref, ref, sem, sem).wait_send()

    def lu_direct_x(w):
        @pl.when(valid(xn, w))
        def _():
            part = lu.at[xn, w, :, mine]
            arrived(part, l_recv.at[0, w])
            remote(part, part, l_send.at[2, w], l_recv.at[2, w], block=yn).start()
            remote(part, part, lm_send.at[0, w], lm_recv.at[0, w], energy=sib).start()

    def lu_direct_y(w):
        @pl.when(valid(yn, w))
        def _():
            part = lu.at[yn, w, :, mine]
            arrived(part, l_recv.at[1, w])
            remote(part, part, lm_send.at[1, w], lm_recv.at[1, w], energy=sib).start()

    def lu_passed(w):
        @pl.when(valid(dn, w))
        def _():
            part = lu.at[dn, w, :, mine]
            arrived(part, l_recv.at[2, w])
            remote(part, part, lm_send.at[2, w], lm_recv.at[2, w], energy=sib).start()

    def src_direct():
        part = src.at[yn, :, mine]
        arrived(part, s_recv.at[1])
        remote(part, part, s_send.at[1], s_recv.at[2], block=xn).start()
        remote(part, part, sm_send.at[2], sm_recv.at[2], energy=sib).start()
        part = src.at[xn, :, mine]
        arrived(part, s_recv.at[0])
        remote(part, part, sm_send.at[1], sm_recv.at[1], energy=sib).start()

    def src_passed():
        part = src.at[dn, :, mine]
        arrived(part, s_recv.at[2])
        remote(part, part, sm_send.at[3], sm_recv.at[3], energy=sib).start()

    for copy in pair_own:
        copy.wait()
    for copy in pairs:
        copy.wait_recv()

    def tiles(k):
        for q in range(r // 8):
            for lane in range(n // 128):
                cols = slice(lane * 128, lane * 128 + 128)
                yield slice(q * 8, q * 8 + 8), pl.ds(pl.multiple_of(k * r + q * 8, 8), 8), cols

    def correlate(left, right, w):
        real = imag = None
        for k in left:
            if k - w in right:
                (a, b), (u, v) = left[k], right[k - w]
                s, t = a * u - b * v, a * v + b * u
                real, imag = (s, t) if real is None else (real + s, imag + t)
        return real, imag

    def p_copies(k):
        ahead = res.at[k, pl.ds(0, 2)]
        return (
            remote(ahead, pin.at[k, pl.ds(0, 2)], p_send.at[0], p_recv.at[k], energy=h),
            remote(res.at[k, pl.ds(2, 2)], pin.at[k, pl.ds(0, 2)], p_send.at[1], p_recv.at[k], energy=2 + h),
            remote(res.at[k, pl.ds(4, 2)], pin.at[k, pl.ds(0, 2)], p_send.at[2], p_recv.at[k], energy=mid + 2 + h),
            remote(ahead, pin.at[k, pl.ds(2, 2)], p_send.at[0], p_recv.at[k], energy=h),
        )

    def polarize(k):
        @pl.when(center)
        def _():
            arrived(zin.at[k], z_recv.at[k])
            for here, rows, cols in tiles(k):
                both = lambda ref, *at: (ref[(*at, 0, here, cols)], ref[(*at, 1, here, cols)])
                pair = lambda ref, c: (ref[c, 0, rows, cols], ref[c, 1, rows, cols])
                left = {mid: pair(gl2, 0), mid + 1: pair(gl2, 1), mid + 2: both(zin, k, 4), mid + 3: both(zin, k, 5)}
                right = {c: both(zin, k, c) for c in range(4)}
                right.update({mid: pair(gg2, 0), mid + 1: pair(gg2, 1)})
                right.update({mid + 2: both(zin, k, 6), mid + 3: both(zin, k, 7)})
                for w in range(energies):
                    value = correlate(left, right, w)
                    for m in (0, 1):
                        if w in (mid, mid + 1):
                            dpair[w - mid, m, rows, cols] = on2[w - mid, m, rows, cols] - value[m] * scale
                        else:
                            res[k, w if w < mid else w - 2, m, here, cols] = value[m]
            for copy in p_copies(k)[:3]:
                copy.start()

        @pl.when(inner)
        def _():
            arrived(zin.at[k, pl.ds(0, 2)], z_recv.at[k])
            for here, rows, cols in tiles(k):
                both = lambda ref, *at: (ref[(*at, 0, here, cols)], ref[(*at, 1, here, cols)])
                pair = lambda ref, c: (ref[c, 0, rows, cols], ref[c, 1, rows, cols])
                left = {2: pair(gl2, 0), 3: pair(gl2, 1)}
                right = {0: both(zin, k, 0), 1: both(zin, k, 1), 2: pair(gg2, 0), 3: pair(gg2, 1)}
                for w in range(mid):
                    value = correlate(left, right, w)
                    for m in (0, 1):
                        res[k, w, m, here, cols] = value[m]
            p_copies(k)[3].start()
            arrived(pin.at[k, pl.ds(0, 2)], p_recv.at[k])
            for here, rows, cols in tiles(k):
                for c in (0, 1):
                    for m in (0, 1):
                        total = res[k, 2 + c, m, here, cols] + pin[k, c, m, here, cols]
                        dpair[c, m, rows, cols] = on2[c, m, rows, cols] - total * scale

        @pl.when(outer)
        def _():
            arrived(pin.at[k], p_recv.at[k])
            for here, rows, cols in tiles(k):
                pair = lambda ref, c: (ref[c, 0, rows, cols], ref[c, 1, rows, cols])
                left = {0: pair(gl2, 0), 1: pair(gl2, 1)}
                right = {0: pair(gg2, 0), 1: pair(gg2, 1)}
                for c in (0, 1):
                    value = correlate(left, right, c)
                    for m in (0, 1):
                        total = value[m] + (pin[k, c, m, here, cols] + pin[k, 2 + c, m, here, cols])
                        dpair[c, m, rows, cols] = on2[c, m, rows, cols] - total * scale

        @pl.when(far)
        def _():
            arrived(pin.at[k, pl.ds(0, 2)], p_recv.at[k])
            for here, rows, cols in tiles(k):
                for c in (0, 1):
                    for m in (0, 1):
                        dpair[c, m, rows, cols] = on2[c, m, rows, cols] - pin[k, c, m, here, cols] * scale

    def strip(k, span=1):
        return pl.ds(pl.multiple_of(h * half + k * r, 8), span * r)

    def spread(k):
        sub = pl.ds(pl.multiple_of(k * r, 8), r)
        there = diag.at[i, :, strip(k)]
        remote(dpair.at[1 - y, :, sub], there, d_send.at[1], d_recv.at[1, k], block=yn).start()
        remote(dpair.at[y, :, sub], there, d_send.at[0], d_recv.at[0, k], block=xn).start()
        remote(dpair.at[y, :, sub], there, dm_send.at[0], dm_recv.at[0], energy=sib).start()
        pltpu.make_async_copy(dpair.at[y, :, sub], there, d_local).start()

    def gather(first, last):
        for k in range(first, last):
            arrived(diag.at[yn, :, strip(k)], d_recv.at[1, k])
        part = diag.at[yn, :, strip(first, last - first)]
        remote(part, part, d_send.at[2], d_recv.at[2, first], block=xn).start()
        remote(part, part, dm_send.at[2], dm_recv.at[2], energy=sib).start()
        for k in range(first, last):
            arrived(diag.at[xn, :, strip(k)], d_recv.at[0, k])
        part = diag.at[xn, :, strip(first, last - first)]
        remote(part, part, dm_send.at[1], dm_recv.at[1], energy=sib).start()

    def gather_passed(first, last):
        part = diag.at[dn, :, strip(first, last - first)]
        arrived(part, d_recv.at[2, first])
        remote(part, part, dm_send.at[3], dm_recv.at[3], energy=sib).start()

    plan = {
        0: [lambda: lu_direct_x(0)],
        2: [lambda: lu_direct_x(1), lambda: lu_direct_y(0)],
        3: [lambda: lu_direct_y(1), src_direct],
        4: [lambda: gather(0, 2)],
        5: [lambda: gather(2, 4), lambda: lu_passed(0), src_passed],
        6: [lambda: gather(4, 5), lambda: gather_passed(0, 2), lambda: lu_passed(1)],
        7: [lambda: gather(5, 7), lambda: gather_passed(2, 4)],
    }

    def turn(k, carry):
        polarize(k)
        spread(k)
        for at, work in plan.items():

            @pl.when(k == at)
            def _(work=work):
                for step in work:
                    step()

        return carry

    lax.fori_loop(0, chunks, turn, 0)
    gather_passed(4, 5)
    gather(7, 8)
    gather_passed(5, 7)
    gather_passed(7, 8)

    pltpu.make_async_copy(dpair.at[y], diag.at[i, :, mine], d_local).wait()
    for k, j in enumerate((i, xn, yn, dn)):
        arrived(diag.at[j, :, other], dm_recv.at[k])

    for w in (0, 1):

        @pl.when(valid(i, w))
        def _(w=w):
            pltpu.make_async_copy(coupling[w], lu.at[i, w], l_local.at[w]).wait()

        for k, j in enumerate((xn, yn, dn)):

            @pl.when(valid(j, w))
            def _(k=k, j=j, w=w):
                arrived(lu.at[j, w, :, other], lm_recv.at[k, w])

    @pl.when(y == h)
    def _():
        pltpu.make_async_copy(rhs.at[:, 0], src.at[i], s_local).wait()

    @pl.when(y != h)
    def _():
        arrived(src.at[i], sm_recv.at[0])

    for k, j in enumerate((xn, yn, dn)):
        arrived(src.at[j, :, other], sm_recv.at[k + 1])

    a, b, m, q = 3 * x, 2 - x, 1 + x, 3 - 3 * x
    couple = lambda j, w: factor((lu[j, w, 0], lu[j, w, 1]))
    diagonal = lambda j: (diag[j, 0], diag[j, 1])
    source = lambda j: (src[j, 0], src[j, 1])

    def put(ref, at, v):
        ref[at, 0], ref[at, 1] = v

    inv = factor(inverse_of(diagonal(m)))
    sm = factor(source(m))
    to_a, to_b = couple(m, x), couple(m, 1 - x)
    t = factor(times(couple(a, 1 - x), inv))
    put(dp, 0, minus(diagonal(a), times(t, to_a)))
    put(fp, 0, times(t, to_b))
    put(sp, 0, minus(source(a), times(t, sm)))
    t = factor(times(couple(b, x), inv))
    put(dp, 1, minus(diagonal(b), times(t, to_b)))
    put(fp, 1, times(t, to_a))
    put(sp, 1, minus(source(b), times(t, sm)))
    t = factor(times(couple(b, 1 - x), factor(inverse_of(diagonal(q)))))
    put(dp, 1, minus((dp[1, 0], dp[1, 1]), times(t, couple(q, x))))
    put(sp, 1, minus((sp[1, 0], sp[1, 1]), times(t, factor(source(q)))))

    this = jnp.where(h == x, 0, 1)
    that = 1 - this
    at = lambda ref, k: (ref[k, 0], ref[k, 1])
    t = factor(times(factor(at(fp, this)), factor(inverse_of(at(dp, that)))))
    last = minus(at(dp, this), times(t, factor(at(fp, that))))
    right = plus(at(sp, this), times(t, factor(at(sp, that))))
    eye = jnp.where(
        lax.broadcasted_iota(jnp.int32, (n, n), 0) == lax.broadcasted_iota(jnp.int32, (n, n), 1), 1.0, 0.0
    )
    inverse_guess = 1.0 / diagonal_guess
    rest = factor((eye - last[0] * inverse_guess, -last[1] * inverse_guess))
    found = right
    for _ in range(2):
        found = plus(right, times(rest, factor(found)))
    found = plus(right, times(rest, factor(found)))
    value[0], value[1] = found[0] * inverse_guess, found[1] * inverse_guess

    home = remote(value, out.at[:, 0], out_sem.at[0], out_sem.at[1], energy=2 * z + y, block=2 * h + x)
    keep = pltpu.make_async_copy(value, out.at[:, 0], out_sem.at[0])

    @pl.when(h != y)
    def _():
        home.start()

    @pl.when(h == y)
    def _():
        keep.start()
        keep.wait()

    whole_array = gg.at[:, 0]

    @pl.when(outer)
    def _():
        sent(whole_array, z_send.at[0])
        sent(whole_array, z_send.at[1])

    @pl.when(inner)
    def _():
        sent(whole_array, z_send.at[0])
        sent(res.at[:, pl.ds(0, 2)], p_send.at[0])

    @pl.when(far)
    def _():
        sent(whole_array, z_send.at[0])
        sent(whole_array, z_send.at[1])

    @pl.when(center)
    def _():
        for k in range(3):
            sent(res.at[:, pl.ds(2 * k, 2)], p_send.at[k])

    for copy in pairs:
        copy.wait_send()
    for k in range(3):
        sent(dpair.at[0], d_send.at[k])
    for k in range(4):
        sent(dpair.at[0], dm_send.at[k])
    part = src.at[0, :, mine]

    @pl.when(y == h)
    def _():
        sent(rhs.at[:, 0], sm_send.at[0])

    sent(rhs.at[:, 0], s_send.at[0])
    sent(part, s_send.at[1])
    for k in range(3):
        sent(part, sm_send.at[k + 1])
    for w in (0, 1):
        part = lu.at[0, w, :, mine]

        @pl.when(valid(i, w))
        def _(w=w, part=part):
            sent(part, l_send.at[0, w])
            sent(part, l_send.at[1, w])

        for k, j in enumerate((xn, yn, dn)):

            @pl.when(valid(j, w))
            def _(k=k, w=w, part=part):
                if k == 0:
                    sent(part, l_send.at[2, w])
                sent(part, lm_send.at[k, w])

    @pl.when(h != y)
    def _():
        home.wait()


def line(g_lesser, g_greater, onsite, lower, upper, rhs):
    count = lax.axis_size("block")
    n, columns = onsite.shape[2], rhs.shape[-1]
    chunks = 8
    half = n // 2
    r = half // chunks
    f32 = jnp.float32
    dma = pltpu.SemaphoreType.DMA
    anywhere = pl.BlockSpec(memory_space=pl.ANY)
    pair = pltpu.VMEM((2, 2, half, n), f32)
    return pl.pallas_call(
        line_kernel,
        name="line",
        out_shape=pltpu.VMEM((2, 1, n, columns), f32),
        in_specs=[anywhere] * 6,
        out_specs=anywhere,
        scratch_shapes=[
            pair, pair, pair,
            pltpu.VMEM((chunks, 8, 2, r, n), f32),
            pltpu.VMEM((chunks, 6, 2, r, n), f32),
            pltpu.VMEM((chunks, 4, 2, r, n), f32),
            pair,
            pltpu.VMEM((count, 2, n, n), f32),
            pltpu.VMEM((count, 2, n, columns), f32),
            pltpu.VMEM((count, 2, 2, n, n), f32),
            pltpu.VMEM((2, 2, n, n), f32),
            pltpu.VMEM((2, 2, n, n), f32),
            pltpu.VMEM((2, 2, n, columns), f32),
            pltpu.VMEM((2, n, columns), f32),
            dma((2,)), dma((chunks,)), dma((3,)), dma((chunks,)), dma((3,)), dma((3,)), dma((3,)),
            dma((3,)), dma((3, chunks)), dma, dma((4,)), dma((4,)),
            dma((2,)), dma((3,)), dma, dma((4,)), dma((4,)),
            dma((3, 2)), dma((3, 2)), dma((2,)), dma((3, 2)), dma((3, 2)), dma((2,)),
        ],
        compiler_params=pltpu.CompilerParams(
            collective_id=1, has_side_effects=True, vmem_limit_bytes=60 * 1024 * 1024
        ),
    )(g_lesser, g_greater, onsite, lower, upper, rhs)


def shifted(value, steps):
    count = lax.axis_size("block")
    leading, last = max(0, -steps), min(count, count - steps)
    pairs = [(k, k + steps) for k in range(leading, last)]
    return lax.ppermute(value, "block", pairs)


def shards(g_lesser, g_greater, onsite, lower, upper, rhs):
    index = lax.axis_index("block")
    count = lax.axis_size("block")
    levels = count.bit_length() - 1
    n = onsite.shape[-1]
    both = jnp.concatenate(
        [jnp.where(index > 0, lower, 0.0), jnp.where(index < count - 1, upper, 0.0)], axis=-1
    )
    if levels == 2 and lax.axis_size("energy") == 8:
        return line(g_lesser, g_greater, onsite, lower, upper, rhs)
    diag, near_lu, near_s = front(g_lesser, g_greater, onsite, lower, upper, rhs)
    diag = parts(diag)
    first, final = index < 2, index >= count - 2
    low, up = cut(parts(both), 0, n), cut(parts(both), n, 2 * n)
    source = parts(rhs[:, 0])
    for depth in range(levels):
        stride = 1 << depth
        inv = inverse(diag)
        if depth == levels - 1:
            coupling = tuple(jnp.where(index < stride, up[k], low[k]) for k in (0, 1))
            sent = product(inv, wide(coupling, source))
            swap = [(k, k ^ stride) for k in range(count)]
            got = parts(lax.ppermute(jnp.stack(sent), "block", swap))
            change = product(coupling, got)
            diag = minus(diag, cut(change, 0, n))
            source = minus(source, cut(change, n, None))
        elif depth == 0:
            packed = jnp.stack(inv)
            inv_left, inv_right = parts(shifted(packed, 1)), parts(shifted(packed, -1))
            t, w = product(low, inv_left), product(up, inv_right)
            lu_l, lu_r = near_lu[0], near_lu[1]
            change = product(t, wide(parts(lu_l[0]), parts(lu_l[1]), parts(near_s[0])))
            other = product(w, wide(parts(lu_r[0]), parts(lu_r[1]), parts(near_s[1])))
            change = tuple(jnp.where(index > 0, v, 0.0) for v in change)
            other = tuple(jnp.where(index < count - 1, v, 0.0) for v in other)
            diag = minus(minus(diag, cut(change, n, 2 * n)), cut(other, 0, n))
            source = minus(minus(source, cut(change, 2 * n, None)), cut(other, 2 * n, None))
            low = tuple(jnp.where(first, 0.0, -v) for v in cut(change, 0, n))
            up = tuple(jnp.where(final, 0.0, -v) for v in cut(other, n, 2 * n))
        else:
            sent = jnp.stack(product(inv, wide(low, up, source)))
            left, right = parts(shifted(sent, stride)), parts(shifted(sent, -stride))
            change, other = product(low, left), product(up, right)
            diag = minus(minus(diag, cut(change, n, 2 * n)), cut(other, 0, n))
            source = minus(minus(source, cut(change, 2 * n, None)), cut(other, 2 * n, None))
            low = tuple(-v for v in cut(change, 0, n))
            up = tuple(-v for v in cut(other, n, 2 * n))
    return jnp.stack(solve(diag, source))[:, None]


def solution(mesh):
    placed = (
        P(None, "energy", "block", None),
        P(None, "energy", "block", None),
        P(None, "energy", "block", None),
        P(None, "block", None),
        P(None, "block", None),
        P(None, "energy", "block", None),
    )
    return jax.shard_map(
        shards,
        mesh=mesh,
        in_specs=placed,
        out_specs=P(None, "energy", "block", None),
        check_vma=False,
    )
```

```python
import math

import jax
import jax.numpy as jnp
from jax import lax
from jax.experimental import pallas as pl
from jax.experimental.pallas import tpu as pltpu
from jax.sharding import PartitionSpec as P

diagonal_guess = 5.0
MODE = lax.Precision.HIGH
MESH = pl.DeviceIdType.MESH


def real_product(a, b):
    return jnp.matmul(a, b, precision=MODE)


def product(a, b):
    ar, ai = a
    br, bi = b
    return (
        real_product(ar, br) - real_product(ai, bi),
        real_product(ar, bi) + real_product(ai, br),
    )


def parts(a):
    return a[0], a[1]


def plus(a, b):
    return a[0] + b[0], a[1] + b[1]


def minus(a, b):
    return a[0] - b[0], a[1] - b[1]


def wide(*pieces):
    return tuple(jnp.concatenate([p[k] for p in pieces], axis=-1) for k in (0, 1))


def cut(a, start, stop):
    return a[0][:, start:stop], a[1][:, start:stop]


def remainder(matrix):
    eye = jnp.eye(matrix[0].shape[-1], dtype=jnp.float32)
    return eye - matrix[0] * (1.0 / diagonal_guess), -matrix[1] * (1.0 / diagonal_guess)


def inverse(matrix):
    eye = jnp.eye(matrix[0].shape[-1], dtype=jnp.float32)
    b = remainder(matrix)
    square = product(b, b)
    cube = product(b, square)
    scale = 1.0 / diagonal_guess
    return (eye + b[0] + square[0] + cube[0]) * scale, (b[1] + square[1] + cube[1]) * scale


def solve(matrix, source):
    b = remainder(matrix)
    value = source
    for _ in range(3):
        value = plus(source, product(b, value))
    scale = 1.0 / diagonal_guess
    return value[0] * scale, value[1] * scale


def front_kernel(
    gl, gg, onsite, lower, upper, rhs, diag, near_lu, near_s,
    lu, gl_all, gg_all, res, pol,
    in_send, in_recv, out_send, out_recv, lu_send, lu_recv, hop_send, hop_recv,
    mate_send, mate_recv, local, rows_out=None, partner=None,
):
    e, i = lax.axis_index("energy"), lax.axis_index("block")
    energies, count = lax.axis_size("energy"), lax.axis_size("block")
    share = gl.shape[2] // energies
    c, p = lax.rem(e, 2), lax.rem(i, 2)
    mate, side = e + 1 - 2 * c, 1 - p
    pair, onward, behind = i + 1 - 2 * p, i + 2 - 4 * p, i - 2 + 4 * p
    has_onward = jnp.logical_and(onward >= 0, onward < count)
    has_behind = jnp.logical_and(behind >= 0, behind < count)

    fill = [pltpu.make_async_copy((lower, upper)[k], lu.at[k], local.at[k]) for k in (0, 1)]
    for copy in fill:
        copy.start()
    barrier = pltpu.get_barrier_semaphore()
    for k in range(1, energies):
        pl.semaphore_signal(barrier, inc=1, device_id={"energy": lax.rem(e + k, energies)}, device_id_type=MESH)
    pl.semaphore_signal(barrier, inc=1, device_id={"block": pair}, device_id_type=MESH)

    @pl.when(has_onward)
    def _():
        pl.semaphore_signal(barrier, inc=1, device_id={"block": onward}, device_id_type=MESH)

    @pl.when(has_behind)
    def _():
        pl.semaphore_signal(barrier, inc=1, device_id={"block": behind}, device_id_type=MESH)

    peers = energies
    if partner is not None:
        peers = energies + 1
        pl.semaphore_signal(barrier, inc=1, device_id={"block": partner}, device_id_type=MESH)
    pl.semaphore_wait(barrier, peers + has_onward.astype(jnp.int32) + has_behind.astype(jnp.int32))

    def remote(src, dst, send, recv, **where):
        return pltpu.make_async_remote_copy(
            src_ref=src, dst_ref=dst, send_sem=send, recv_sem=recv, device_id=where, device_id_type=MESH
        )

    part = share // 2

    def in_copy(h, k, q, source):
        src, dst = ((gl, gl_all), (gg, gg_all))[k]
        rows = src.at[:, 0, pl.ds(q * share + h * part, part), :]
        there = dst.at[source, :, pl.ds(h * part, part), :]
        return remote(rows, there, in_send.at[h, k, q], in_recv.at[h, k, source], energy=q)

    def out_copy(h, w, source):
        rows = pl.ds(h * part, part)
        return remote(
            res.at[w, :, rows, :], pol.at[source, :, rows, :], out_send.at[h, w], out_recv.at[h, source], energy=w
        )

    for copy in fill:
        copy.wait()
    for h in (0, 1):
        for k in (0, 1):
            for q in range(energies):

                @pl.when(q != e)
                def _():
                    in_copy(h, k, q, e).start()

    own = []
    for k, (src, dst) in enumerate(((gl, gl_all), (gg, gg_all))):
        rows = src.at[:, 0, pl.ds(pl.multiple_of(e * share, 8), share), :]
        own.append(pltpu.make_async_copy(rows, dst.at[e], local.at[k]))
        own[-1].start()

    mine = (lu.at[c, 0], lu.at[c, 1], rhs.at[:, 0])

    def slot(s, k):
        return near_s.at[s] if k == 2 else near_lu.at[s, c, k]

    direct = [remote(mine[k], slot(p, k), lu_send.at[k], lu_recv.at[k], block=pair) for k in range(3)]
    hops = [remote(slot(side, k), slot(p, k), hop_send.at[k], hop_recv.at[k], block=onward) for k in range(3)]
    for copy in direct:
        copy.start()
    shared = [
        remote(slot(s, k), slot(s, k), mate_send.at[j, k], mate_recv.at[j, k], energy=mate)
        for j, s in enumerate((side, p))
        for k in (0, 1)
    ]
    for k in range(3):
        direct[k].wait_recv()

        @pl.when(has_onward)
        def _():
            hops[k].start()

        if k < 2:
            shared[k].start()

    for copy in own:
        copy.wait()
    scale = 1.0 / math.sqrt(energies)
    for h in (0, 1):
        for k in (0, 1):
            for q in range(energies):

                @pl.when(q != e)
                def _():
                    in_copy(h, k, q, q).wait_recv()

        for w in range(energies):

            def step(row, carry, w=w, h=h):
                rows = pl.ds(pl.multiple_of(h * part + row * 8, 8), 8)
                real = imag = None
                for k in range(w, energies):
                    a, b = gl_all[k, 0, rows], gl_all[k, 1, rows]
                    x, y = gg_all[k - w, 0, rows], gg_all[k - w, 1, rows]
                    s, t = a * x - b * y, a * y + b * x
                    real, imag = (s, t) if real is None else (real + s, imag + t)
                res[w, 0, rows] = real * scale
                res[w, 1, rows] = imag * scale
                return carry

            lax.fori_loop(0, part // 8, step, 0)

            @pl.when(w != e)
            def _():
                out_copy(h, w, e).start()

    keep = pltpu.make_async_copy(res.at[e], pol.at[e], local.at[0])
    keep.start()

    @pl.when(has_behind)
    def _():
        for k in range(3):
            hops[k].wait_recv()
            if k < 2:
                shared[2 + k].start()

    def hand_on(q):
        rows_out[0][q].wait_recv()

        @pl.when(has_onward)
        def _():
            rows_out[1][q].start()

    keep.wait()
    for q in range(energies):

        @pl.when(q != e)
        def _():
            out_copy(0, q, q).wait_recv()
            out_copy(1, q, q).wait_recv()

        rows = pl.ds(q * share, share)
        for k in (0, 1):
            diag[k, rows] = onsite[k, 0, rows] - pol[q, k]
        if rows_out is not None:
            rows_out[0][q].start()
            if q > 0:
                hand_on(q - 1)
    if rows_out is not None:
        hand_on(energies - 1)

    for k in range(2):
        shared[k].wait_recv()

    @pl.when(has_behind)
    def _():
        for k in range(2):
            shared[2 + k].wait()

    for k in range(2):
        shared[k].wait_send()
    for k in range(3):
        direct[k].wait_send()

        @pl.when(has_onward)
        def _():
            hops[k].wait_send()

    for q in range(energies):

        @pl.when(q != e)
        def _():
            for h in (0, 1):
                in_copy(h, 0, q, e).wait_send()
                in_copy(h, 1, q, e).wait_send()
                out_copy(h, q, e).wait_send()


def front(g_lesser, g_greater, onsite, lower, upper, rhs):
    energies = lax.axis_size("energy")
    n, columns = onsite.shape[2], rhs.shape[-1]
    share = n // energies
    vmem = pl.BlockSpec(memory_space=pltpu.VMEM)
    f32 = jnp.float32
    dma = pltpu.SemaphoreType.DMA
    pieces = pltpu.VMEM((energies, 2, share, n), f32)
    return pl.pallas_call(
        front_kernel,
        name="front",
        out_shape=(
            jax.ShapeDtypeStruct((2, n, n), f32),
            jax.ShapeDtypeStruct((2, 2, 2, n, n), f32),
            jax.ShapeDtypeStruct((2, 2, n, columns), f32),
        ),
        in_specs=[vmem] * 6,
        out_specs=(vmem,) * 3,
        scratch_shapes=[
            pltpu.VMEM((2, 2, n, n), f32),
            pieces, pieces, pieces, pieces,
            dma((2, 2, energies)), dma((2, 2, energies)), dma((2, energies)), dma((2, energies)),
            dma((3,)), dma((3,)), dma((3,)), dma((3,)),
            dma((2, 2)), dma((2, 2)), dma((2,)),
        ],
        compiler_params=pltpu.CompilerParams(collective_id=0, has_side_effects=True),
    )(g_lesser, g_greater, onsite, lower, upper, rhs)


def halves(x):
    high = x.astype(jnp.bfloat16)
    return high, (x - high.astype(jnp.float32)).astype(jnp.bfloat16)


def factor(a):
    return halves(a[0]), halves(a[1]), halves(a[0] + a[1])


def three_pass(a, b):
    dot = lambda u, v: jnp.dot(u, v, preferred_element_type=jnp.float32)
    return dot(a[0], b[0]) + (dot(a[0], b[1]) + dot(a[1], b[0]))


def times(a, b):
    first, second, third = (three_pass(a[k], b[k]) for k in range(3))
    return first - second, third - first - second


def inverse_of(matrix):
    eye_rows = lax.broadcasted_iota(jnp.int32, matrix[0].shape, 0)
    eye_columns = lax.broadcasted_iota(jnp.int32, matrix[0].shape, 1)
    eye = jnp.where(eye_rows == eye_columns, 1.0, 0.0)
    scale = 1.0 / diagonal_guess
    b = eye - matrix[0] * scale, -matrix[1] * scale
    fb = factor(b)
    square = times(fb, fb)
    cube = times(fb, factor(square))
    return (eye + b[0] + square[0] + cube[0]) * scale, (b[1] + square[1] + cube[1]) * scale


def rounded_product(a, b):
    dot = lambda u, v: jnp.dot(u, v, preferred_element_type=jnp.float32)
    first, second, third = (dot(a[k], b[k]) for k in range(3))
    return first - second, third - first - second


def rounded(a):
    return tuple(v.astype(jnp.bfloat16) for v in (a[0], a[1], a[0] + a[1]))


def unit_of(matrix):
    rows = lax.broadcasted_iota(jnp.int32, matrix[0].shape, 0)
    columns = lax.broadcasted_iota(jnp.int32, matrix[0].shape, 1)
    return jnp.where(rows == columns, 1.0, 0.0)


def remainder_of(matrix):
    return unit_of(matrix) - matrix[0] * (1.0 / diagonal_guess), -matrix[1] * (1.0 / diagonal_guess)


def lean_inverse(matrix):
    eye, b = unit_of(matrix), remainder_of(matrix)
    scale = 1.0 / diagonal_guess
    split = factor(b)
    square = times(split, split)
    cube = rounded_product(rounded(b), rounded(square))
    return (eye + b[0] + square[0] + cube[0]) * scale, (b[1] + square[1] + cube[1]) * scale


def stacked(a, b):
    return tuple(tuple(jnp.concatenate([a[k][j], b[k][j]], axis=0) for j in (0, 1)) for k in range(3))


def apply(a, b):
    columns = b[0].shape[1]
    w = halves(jnp.concatenate([b[0], b[1]], axis=1))
    p, q = three_pass(a[0], w), three_pass(a[1], w)
    return p[:, :columns] - q[:, columns:], p[:, columns:] + q[:, :columns]


def line_kernel(
    gl, gg, onsite, lower, upper, rhs, out,
    gl2, gg2, on2, zin_a, res_a, pin_a, zin_b, res_b, pin_b, dpair, diag, src, lu, dp, fp, sp, value,
    z_send, z_recv_a, p_send, p_recv_a, z_recv_b, p_recv_b, pair_send, pair_recv, pair_local,
    d_send, d_recv, d_local, dm_send, dm_recv, t_send, t_recv,
    s_send, s_recv, s_local, sm_send, sm_recv,
    l_send, l_recv, l_local, lm_send, lm_recv, out_sem, edge_diag, edge_src, e_sem,
):
    e, i = lax.axis_index("energy"), lax.axis_index("block")
    energies, count = lax.axis_size("energy"), lax.axis_size("block")
    n = diag.shape[-1]
    half = n // 2
    many, r = zin_a.shape[0], zin_a.shape[3]
    few, fine = zin_b.shape[0], zin_b.shape[3]
    starts = [k * r for k in range(many)] + [many * r + k * fine for k in range(few + 1)]
    segments = ((0, r, 0, zin_a, res_a, pin_a, z_recv_a, p_recv_a), (1, fine, many * r, zin_b, res_b, pin_b, z_recv_b, p_recv_b))
    mid = energies // 2
    z, h = e // 2, lax.rem(e, 2)
    y, x = i // 2, lax.rem(i, 2)
    sib, xn, yn = e + 1 - 2 * h, i + 1 - 2 * x, i + 2 - 4 * y
    dn = yn + 1 - 2 * x
    outer, inner, center, far = z == 0, z == 1, z == 2, z == 3
    mine = pl.ds(pl.multiple_of(h * half, half), half)
    other = pl.ds(pl.multiple_of((1 - h) * half, half), half)
    scale = 1.0 / math.sqrt(energies)

    def remote(a, b, send, recv, energy=e, block=i):
        return pltpu.make_async_remote_copy(
            src_ref=a, dst_ref=b, send_sem=send, recv_sem=recv,
            device_id={"energy": energy, "block": block}, device_id_type=MESH,
        )

    barrier = pltpu.get_barrier_semaphore()
    for k in range(1, energies):
        pl.semaphore_signal(barrier, inc=1, device_id={"energy": lax.rem(e + k, energies)}, device_id_type=MESH)
    for block in (xn, yn):
        for c in (0, 1):
            pl.semaphore_signal(
                barrier, inc=1, device_id={"energy": 2 * z + c, "block": block}, device_id_type=MESH
            )
    pair_own = []
    for k, (a, b) in enumerate(((gg, gg2), (gl, gl2), (onsite, on2))):
        pair_own.append(pltpu.make_async_copy(a.at[:, 0, mine], b.at[h], pair_local.at[k]))
        pair_own[-1].start()
    pl.semaphore_wait(barrier, energies + 3)

    def valid(j, w):
        return j > 0 if w == 0 else j < count - 1

    coupling = (lower, upper)
    for w in (0, 1):

        @pl.when(valid(i, w))
        def _(w=w):
            remote(coupling[w].at[:, mine], lu.at[i, w, :, mine], l_send.at[0, w], l_recv.at[0, w], block=xn).start()
            remote(coupling[w].at[:, mine], lu.at[i, w, :, mine], l_send.at[1, w], l_recv.at[1, w], block=yn).start()
            pltpu.make_async_copy(coupling[w], lu.at[i, w], l_local.at[w]).start()

    def rows_of(g):
        return pl.ds(g * half, half)

    @pl.when(y == h)
    def _():
        pltpu.make_async_copy(rhs.at[:, 0], src.at[i], s_local).start()
        remote(rhs.at[:, 0], src.at[i], sm_send.at[0], sm_recv.at[0], energy=sib).start()
        for g in (0, 1):
            remote(
                rhs.at[:, 0, rows_of(g)], src.at[i, :, rows_of(g)], s_send.at[0], s_recv.at[0],
                energy=2 * z + g, block=xn,
            ).start()

    @pl.when(y != h)
    def _():
        for g in (0, 1):
            remote(
                rhs.at[:, 0, rows_of(g)], src.at[i, :, rows_of(g)], s_send.at[0], s_recv.at[1],
                energy=2 * z + g, block=yn,
            ).start()

    def z_copies(seg, k, which):
        _, size, base, zin, _, _, z_recv, _ = seg

        def to(a, slot, g, target, sem):
            piece = a.at[:, 0, pl.ds(pl.multiple_of(g * half + base + k * size, 8), size)]
            return remote(piece, zin.at[k, slot], z_send.at[sem], z_recv.at[k], energy=target + g)

        for g in (0, 1):
            if which == 0:
                to(gg, e, g, mid, 0).start()
                to(gg, e, g, mid - 2, 1).start()
            elif which == 1:
                to(gg, e, g, mid, 0).start()
            else:
                to(gl, e - mid + 2, g, mid, 1).start()
                to(gg, e - mid + 4, g, mid, 0).start()

    for which, role in ((0, outer), (1, inner), (3, far)):

        @pl.when(role)
        def _(which=which):
            for seg, steps in zip(segments, (many, few)):

                def body(k, carry, seg=seg):
                    z_copies(seg, k, which)
                    return carry

                lax.fori_loop(0, steps, body, 0)

    pairs = []
    for k, (a, b) in enumerate(((gg, gg2), (gl, gl2), (onsite, on2))):
        pairs.append(remote(a.at[:, 0, other], b.at[h], pair_send.at[k], pair_recv.at[k], energy=sib))
        pairs[-1].start()

    def arrived(ref, sem):
        remote(ref, ref, sem, sem).wait_recv()

    def sent(ref, sem):
        remote(ref, ref, sem, sem).wait_send()

    def lu_direct_x(w):
        @pl.when(valid(xn, w))
        def _():
            part = lu.at[xn, w, :, mine]
            arrived(part, l_recv.at[0, w])
            remote(part, part, l_send.at[2, w], l_recv.at[2, w], block=yn).start()
            remote(part, part, lm_send.at[0, w], lm_recv.at[0, w], energy=sib).start()

    def lu_direct_y(w):
        @pl.when(valid(yn, w))
        def _():
            part = lu.at[yn, w, :, mine]
            arrived(part, l_recv.at[1, w])
            remote(part, part, lm_send.at[1, w], lm_recv.at[1, w], energy=sib).start()

    def lu_passed(w):
        @pl.when(valid(dn, w))
        def _():
            part = lu.at[dn, w, :, mine]
            arrived(part, l_recv.at[2, w])
            remote(part, part, lm_send.at[2, w], lm_recv.at[2, w], energy=sib).start()

    def src_direct():
        part = src.at[yn, :, mine]
        arrived(part, s_recv.at[1])
        remote(part, part, s_send.at[1], s_recv.at[2], block=xn).start()
        remote(part, part, sm_send.at[2], sm_recv.at[2], energy=sib).start()
        part = src.at[xn, :, mine]
        arrived(part, s_recv.at[0])
        remote(part, part, sm_send.at[1], sm_recv.at[1], energy=sib).start()

    def src_passed():
        part = src.at[dn, :, mine]
        arrived(part, s_recv.at[2])
        remote(part, part, sm_send.at[3], sm_recv.at[3], energy=sib).start()

    for copy in pair_own:
        copy.wait()
    for copy in pairs:
        copy.wait_recv()

    def tiles(seg, k):
        size, base = seg[1], seg[2]
        for q in range(size // 8):
            for lane in range(n // 128):
                cols = slice(lane * 128, lane * 128 + 128)
                yield slice(q * 8, q * 8 + 8), pl.ds(pl.multiple_of(base + k * size + q * 8, 8), 8), cols

    def correlate(left, right, w):
        real = imag = None
        for k in left:
            if k - w in right:
                (a, b), (u, v) = left[k], right[k - w]
                s, t = a * u - b * v, a * v + b * u
                real, imag = (s, t) if real is None else (real + s, imag + t)
        return real, imag

    def p_copy(seg, k, part, slot, target, sem=None):
        where, _, _, _, res, pin, _, p_recv = seg
        sem = part if sem is None else sem
        return remote(
            res.at[k, pl.ds(2 * part, 2)], pin.at[k, pl.ds(slot, 2)], p_send.at[where, sem], p_recv.at[k],
            energy=target + h,
        )

    def polarize(seg, k):
        _, _, _, zin, res, pin, z_recv, p_recv = seg

        @pl.when(center)
        def _():
            arrived(zin.at[k], z_recv.at[k])
            for here, rows, cols in tiles(seg, k):
                both = lambda ref, *at: (ref[(*at, 0, here, cols)], ref[(*at, 1, here, cols)])
                pair = lambda ref, c: (ref[c, 0, rows, cols], ref[c, 1, rows, cols])
                left = {mid: pair(gl2, 0), mid + 1: pair(gl2, 1), mid + 2: both(zin, k, 4), mid + 3: both(zin, k, 5)}
                right = {c: both(zin, k, c) for c in range(4)}
                right.update({mid: pair(gg2, 0), mid + 1: pair(gg2, 1)})
                right.update({mid + 2: both(zin, k, 6), mid + 3: both(zin, k, 7)})
                for w in range(energies):
                    value = correlate(left, right, w)
                    for m in (0, 1):
                        if w in (mid, mid + 1):
                            dpair[w - mid, m, rows, cols] = on2[w - mid, m, rows, cols] - value[m] * scale
                        else:
                            res[k, w if w < mid else w - 2, m, here, cols] = value[m]
            for part, target in enumerate((0, 2, mid + 2)):
                p_copy(seg, k, part, 0, target).start()

        @pl.when(inner)
        def _():
            arrived(zin.at[k, pl.ds(0, 2)], z_recv.at[k])
            for here, rows, cols in tiles(seg, k):
                both = lambda ref, *at: (ref[(*at, 0, here, cols)], ref[(*at, 1, here, cols)])
                pair = lambda ref, c: (ref[c, 0, rows, cols], ref[c, 1, rows, cols])
                left = {2: pair(gl2, 0), 3: pair(gl2, 1)}
                right = {0: both(zin, k, 0), 1: both(zin, k, 1), 2: pair(gg2, 0), 3: pair(gg2, 1)}
                for w in range(mid):
                    value = correlate(left, right, w)
                    for m in (0, 1):
                        res[k, w, m, here, cols] = value[m]
            p_copy(seg, k, 0, 2, 0).start()
            arrived(pin.at[k, pl.ds(0, 2)], p_recv.at[k])
            for here, rows, cols in tiles(seg, k):
                for c in (0, 1):
                    for m in (0, 1):
                        total = res[k, 2 + c, m, here, cols] + pin[k, c, m, here, cols]
                        dpair[c, m, rows, cols] = on2[c, m, rows, cols] - total * scale

        @pl.when(outer)
        def _():
            arrived(pin.at[k], p_recv.at[k])
            for here, rows, cols in tiles(seg, k):
                pair = lambda ref, c: (ref[c, 0, rows, cols], ref[c, 1, rows, cols])
                left = {0: pair(gl2, 0), 1: pair(gl2, 1)}
                right = {0: pair(gg2, 0), 1: pair(gg2, 1)}
                for c in (0, 1):
                    value = correlate(left, right, c)
                    for m in (0, 1):
                        total = value[m] + (pin[k, c, m, here, cols] + pin[k, 2 + c, m, here, cols])
                        dpair[c, m, rows, cols] = on2[c, m, rows, cols] - total * scale

        @pl.when(far)
        def _():
            arrived(pin.at[k, pl.ds(0, 2)], p_recv.at[k])
            for here, rows, cols in tiles(seg, k):
                for c in (0, 1):
                    for m in (0, 1):
                        dpair[c, m, rows, cols] = on2[c, m, rows, cols] - pin[k, c, m, here, cols] * scale

    def strip(first, last):
        return pl.ds(pl.multiple_of(h * half + starts[first], 8), starts[last] - starts[first])

    def spread(seg, k, at, passed=True):
        size, base = seg[1], seg[2]
        sub = pl.ds(pl.multiple_of(base + k * size, 8), size)
        there = diag.at[i, :, pl.ds(pl.multiple_of(h * half + base + k * size, 8), size)]
        if not passed:
            remote(dpair.at[1 - y, :, sub], there, t_send.at[0], d_recv.at[2, at], block=dn).start()
        remote(dpair.at[1 - y, :, sub], there, d_send.at[1], d_recv.at[1, at], block=yn).start()
        remote(dpair.at[y, :, sub], there, d_send.at[0], d_recv.at[0, at], block=xn).start()
        remote(dpair.at[y, :, sub], there, dm_send.at[0], dm_recv.at[0], energy=sib).start()
        pltpu.make_async_copy(dpair.at[y, :, sub], there, d_local).start()

    def gather_y(first, last):
        for k in range(first, last):
            arrived(diag.at[yn, :, strip(k, k + 1)], d_recv.at[1, k])
        part = diag.at[yn, :, strip(first, last)]
        if first < many:
            remote(part, part, d_send.at[2], d_recv.at[2, first], block=xn).start()
        remote(part, part, dm_send.at[2], dm_recv.at[2], energy=sib).start()

    def gather_x(first, last):
        for k in range(first, last):
            arrived(diag.at[xn, :, strip(k, k + 1)], d_recv.at[0, k])
        part = diag.at[xn, :, strip(first, last)]
        remote(part, part, dm_send.at[1], dm_recv.at[1], energy=sib).start()

    def gather(first, last):
        gather_y(first, last)
        gather_x(first, last)

    def gather_passed(first, last):
        part = diag.at[dn, :, strip(first, last)]
        arrived(part, d_recv.at[2, first])
        remote(part, part, dm_send.at[3], dm_recv.at[3], energy=sib).start()

    plan = {
        0: [lambda: lu_direct_x(0)],
        2: [lambda: lu_direct_x(1)],
        3: [src_direct],
        5: [lambda: gather_y(0, 2)],
        6: [lambda: gather_y(2, 4)],
    }

    def turn(k, carry):
        polarize(segments[0], k)
        spread(segments[0], k, k)
        for at, work in plan.items():

            @pl.when(k == at)
            def _(work=work):
                for step in work:
                    step()

        return carry

    lax.fori_loop(0, many, turn, 0)
    polarize(segments[1], 0)
    spread(segments[1], 0, many, passed=False)
    gather_y(4, 5)
    polarize(segments[1], 1)
    spread(segments[1], 1, many + 1, passed=False)
    gather_y(5, 7)
    gather_x(0, 7)
    src_passed()
    lu_direct_y(0)
    lu_direct_y(1)
    lu_passed(0)
    lu_passed(1)
    gather_passed(0, 2)
    gather_passed(2, 4)
    gather_passed(4, 5)
    for k in (many, many + 1):
        gather(k, k + 1)
        gather_passed(k, k + 1)
    gather_passed(5, 7)

    pltpu.make_async_copy(dpair.at[y], diag.at[i, :, mine], d_local).wait()
    for k, j in enumerate((i, xn, yn, dn)):
        arrived(diag.at[j, :, other], dm_recv.at[k])

    for w in (0, 1):

        @pl.when(valid(i, w))
        def _(w=w):
            pltpu.make_async_copy(coupling[w], lu.at[i, w], l_local.at[w]).wait()

        for k, j in enumerate((xn, yn, dn)):

            @pl.when(valid(j, w))
            def _(k=k, j=j, w=w):
                arrived(lu.at[j, w, :, other], lm_recv.at[k, w])

    @pl.when(y == h)
    def _():
        pltpu.make_async_copy(rhs.at[:, 0], src.at[i], s_local).wait()

    @pl.when(y != h)
    def _():
        arrived(src.at[i], sm_recv.at[0])

    for k, j in enumerate((xn, yn, dn)):
        arrived(src.at[j, :, other], sm_recv.at[k + 1])

    a, b, m, q = 3 * x, 2 - x, 1 + x, 3 - 3 * x
    couple = lambda j, w: factor((lu[j, w, 0], lu[j, w, 1]))
    diagonal = lambda j: (diag[j, 0], diag[j, 1])
    source = lambda j: (src[j, 0], src[j, 1])

    def put(ref, at, v):
        ref[at, 0], ref[at, 1] = v

    edge_d = remote(edge_diag, edge_diag, e_sem.at[0], e_sem.at[1], energy=sib)
    edge_s = remote(edge_src, edge_src, e_sem.at[2], e_sem.at[3], energy=sib)

    @pl.when(h == y)
    def _():
        t = factor(times(couple(b, 1 - x), factor(inverse_of(diagonal(q)))))
        edge_diag[0], edge_diag[1] = times(t, couple(q, x))
        edge_d.start()
        edge_src[0], edge_src[1] = apply(t, source(q))
        edge_s.start()

    inv = factor(inverse_of(diagonal(m)))
    t = factor(times(stacked(couple(a, 1 - x), couple(b, x)), inv))
    top, low = (lambda v: (v[0][:n], v[1][:n])), (lambda v: (v[0][n:], v[1][n:]))
    v = times(t, couple(m, x))
    put(dp, 0, minus(diagonal(a), top(v)))
    put(fp, 1, low(v))
    v = times(t, couple(m, 1 - x))
    put(dp, 1, minus(diagonal(b), low(v)))
    put(fp, 0, top(v))
    v = apply(t, source(m))
    put(sp, 0, minus(source(a), top(v)))
    put(sp, 1, minus(source(b), low(v)))

    @pl.when(h != y)
    def _():
        edge_d.wait_recv()
        edge_s.wait_recv()

    for k in (0, 1):
        dp[1, k] = dp[1, k] - edge_diag[k]
        sp[1, k] = sp[1, k] - edge_src[k]

    this = jnp.where(h == x, 0, 1)
    that = 1 - this
    at = lambda ref, k: (ref[k, 0], ref[k, 1])
    t = factor(times(factor(at(fp, this)), factor(lean_inverse(at(dp, that)))))
    last = minus(at(dp, this), times(t, factor(at(fp, that))))
    right = plus(at(sp, this), apply(t, at(sp, that)))
    rest = factor(remainder_of(last))
    inverse_guess = 1.0 / diagonal_guess
    found = right
    for _ in range(3):
        found = plus(right, apply(rest, found))
    value[0], value[1] = found[0] * inverse_guess, found[1] * inverse_guess

    home = remote(value, out.at[:, 0], out_sem.at[0], out_sem.at[1], energy=2 * z + y, block=2 * h + x)
    keep = pltpu.make_async_copy(value, out.at[:, 0], out_sem.at[0])

    @pl.when(h != y)
    def _():
        home.start()

    @pl.when(h == y)
    def _():
        keep.start()
        keep.wait()

    whole_array = gg.at[:, 0]

    @pl.when(outer)
    def _():
        sent(whole_array, z_send.at[0])
        sent(whole_array, z_send.at[1])

    @pl.when(inner)
    def _():
        sent(whole_array, z_send.at[0])
        for seg in segments:
            sent(seg[4].at[:, pl.ds(0, 2)], p_send.at[seg[0], 0])

    @pl.when(far)
    def _():
        sent(whole_array, z_send.at[0])
        sent(whole_array, z_send.at[1])

    @pl.when(center)
    def _():
        for seg in segments:
            for k in range(3):
                sent(seg[4].at[:, pl.ds(2 * k, 2)], p_send.at[seg[0], k])

    for copy in pairs:
        copy.wait_send()
    for k in range(2):
        sent(dpair.at[0], d_send.at[k])
    sent(dpair.at[0, :, pl.ds(0, many * r)], d_send.at[2])
    sent(dpair.at[0, :, pl.ds(0, few * fine)], t_send.at[0])
    for k in range(4):
        sent(dpair.at[0], dm_send.at[k])
    part = src.at[0, :, mine]

    @pl.when(y == h)
    def _():
        sent(rhs.at[:, 0], sm_send.at[0])

    sent(rhs.at[:, 0], s_send.at[0])
    sent(part, s_send.at[1])
    for k in range(3):
        sent(part, sm_send.at[k + 1])
    for w in (0, 1):
        part = lu.at[0, w, :, mine]

        @pl.when(valid(i, w))
        def _(w=w, part=part):
            sent(part, l_send.at[0, w])
            sent(part, l_send.at[1, w])

        for k, j in enumerate((xn, yn, dn)):

            @pl.when(valid(j, w))
            def _(k=k, w=w, part=part):
                if k == 0:
                    sent(part, l_send.at[2, w])
                sent(part, lm_send.at[k, w])

    @pl.when(h == y)
    def _():
        edge_d.wait_send()
        edge_s.wait_send()

    @pl.when(h != y)
    def _():
        home.wait()


def line(g_lesser, g_greater, onsite, lower, upper, rhs):
    count = lax.axis_size("block")
    n, columns = onsite.shape[2], rhs.shape[-1]
    half = n // 2
    r = half // 8
    many, few, fine = 7, 2, r // 2
    f32 = jnp.float32
    dma = pltpu.SemaphoreType.DMA
    anywhere = pl.BlockSpec(memory_space=pl.ANY)
    pair = pltpu.VMEM((2, 2, half, n), f32)
    return pl.pallas_call(
        line_kernel,
        name="line",
        out_shape=pltpu.VMEM((2, 1, n, columns), f32),
        in_specs=[anywhere] * 6,
        out_specs=anywhere,
        scratch_shapes=[
            pair, pair, pair,
            pltpu.VMEM((many, 8, 2, r, n), f32),
            pltpu.VMEM((many, 6, 2, r, n), f32),
            pltpu.VMEM((many, 4, 2, r, n), f32),
            pltpu.VMEM((few, 8, 2, fine, n), f32),
            pltpu.VMEM((few, 6, 2, fine, n), f32),
            pltpu.VMEM((few, 4, 2, fine, n), f32),
            pair,
            pltpu.VMEM((count, 2, n, n), f32),
            pltpu.VMEM((count, 2, n, columns), f32),
            pltpu.VMEM((count, 2, 2, n, n), f32),
            pltpu.VMEM((2, 2, n, n), f32),
            pltpu.VMEM((2, 2, n, n), f32),
            pltpu.VMEM((2, 2, n, columns), f32),
            pltpu.VMEM((2, n, columns), f32),
            dma((2,)), dma((many,)), dma((2, 3)), dma((many,)), dma((few,)), dma((few,)), dma((3,)), dma((3,)), dma((3,)),
            dma((3,)), dma((3, many + few)), dma, dma((4,)), dma((4,)), dma((1,)), dma((1,)),
            dma((2,)), dma((3,)), dma, dma((4,)), dma((4,)),
            dma((3, 2)), dma((3, 2)), dma((2,)), dma((3, 2)), dma((3, 2)), dma((2,)),
            pltpu.VMEM((2, n, n), f32), pltpu.VMEM((2, n, columns), f32), dma((4,)),
        ],
        compiler_params=pltpu.CompilerParams(
            collective_id=1, has_side_effects=True, vmem_limit_bytes=60 * 1024 * 1024
        ),
    )(g_lesser, g_greater, onsite, lower, upper, rhs)


def shifted(value, steps):
    count = lax.axis_size("block")
    leading, last = max(0, -steps), min(count, count - steps)
    pairs = [(k, k + steps) for k in range(leading, last)]
    return lax.ppermute(value, "block", pairs)


def shards(g_lesser, g_greater, onsite, lower, upper, rhs):
    index = lax.axis_index("block")
    count = lax.axis_size("block")
    levels = count.bit_length() - 1
    n = onsite.shape[-1]
    both = jnp.concatenate(
        [jnp.where(index > 0, lower, 0.0), jnp.where(index < count - 1, upper, 0.0)], axis=-1
    )
    if levels == 2 and lax.axis_size("energy") == 8:
        return line(g_lesser, g_greater, onsite, lower, upper, rhs)
    diag, near_lu, near_s = front(g_lesser, g_greater, onsite, lower, upper, rhs)
    diag = parts(diag)
    first, final = index < 2, index >= count - 2
    low, up = cut(parts(both), 0, n), cut(parts(both), n, 2 * n)
    source = parts(rhs[:, 0])
    for depth in range(levels):
        stride = 1 << depth
        inv = inverse(diag)
        if depth == levels - 1:
            coupling = tuple(jnp.where(index < stride, up[k], low[k]) for k in (0, 1))
            sent = product(inv, wide(coupling, source))
            swap = [(k, k ^ stride) for k in range(count)]
            got = parts(lax.ppermute(jnp.stack(sent), "block", swap))
            change = product(coupling, got)
            diag = minus(diag, cut(change, 0, n))
            source = minus(source, cut(change, n, None))
        elif depth == 0:
            packed = jnp.stack(inv)
            inv_left, inv_right = parts(shifted(packed, 1)), parts(shifted(packed, -1))
            t, w = product(low, inv_left), product(up, inv_right)
            lu_l, lu_r = near_lu[0], near_lu[1]
            change = product(t, wide(parts(lu_l[0]), parts(lu_l[1]), parts(near_s[0])))
            other = product(w, wide(parts(lu_r[0]), parts(lu_r[1]), parts(near_s[1])))
            change = tuple(jnp.where(index > 0, v, 0.0) for v in change)
            other = tuple(jnp.where(index < count - 1, v, 0.0) for v in other)
            diag = minus(minus(diag, cut(change, n, 2 * n)), cut(other, 0, n))
            source = minus(minus(source, cut(change, 2 * n, None)), cut(other, 2 * n, None))
            low = tuple(jnp.where(first, 0.0, -v) for v in cut(change, 0, n))
            up = tuple(jnp.where(final, 0.0, -v) for v in cut(other, n, 2 * n))
        else:
            sent = jnp.stack(product(inv, wide(low, up, source)))
            left, right = parts(shifted(sent, stride)), parts(shifted(sent, -stride))
            change, other = product(low, left), product(up, right)
            diag = minus(minus(diag, cut(change, n, 2 * n)), cut(other, 0, n))
            source = minus(minus(source, cut(change, 2 * n, None)), cut(other, 2 * n, None))
            low = tuple(-v for v in cut(change, 0, n))
            up = tuple(-v for v in cut(other, n, 2 * n))
    return jnp.stack(solve(diag, source))[:, None]


def solution(mesh):
    placed = (
        P(None, "energy", "block", None),
        P(None, "energy", "block", None),
        P(None, "energy", "block", None),
        P(None, "block", None),
        P(None, "block", None),
        P(None, "energy", "block", None),
    )
    return jax.shard_map(
        shards,
        mesh=mesh,
        in_specs=placed,
        out_specs=P(None, "energy", "block", None),
        check_vma=False,
    )
```

```python
import math

import jax
import jax.numpy as jnp
from jax import lax
from jax.experimental import pallas as pl
from jax.experimental.pallas import tpu as pltpu
from jax.sharding import PartitionSpec as P

diagonal_guess = 5.0
MODE = lax.Precision.HIGH
MESH = pl.DeviceIdType.MESH


def real_product(a, b):
    return jnp.matmul(a, b, precision=MODE)


def product(a, b):
    ar, ai = a
    br, bi = b
    return (
        real_product(ar, br) - real_product(ai, bi),
        real_product(ar, bi) + real_product(ai, br),
    )


def parts(a):
    return a[0], a[1]


def plus(a, b):
    return a[0] + b[0], a[1] + b[1]


def minus(a, b):
    return a[0] - b[0], a[1] - b[1]


def wide(*pieces):
    return tuple(jnp.concatenate([p[k] for p in pieces], axis=-1) for k in (0, 1))


def cut(a, start, stop):
    return a[0][:, start:stop], a[1][:, start:stop]


def remainder(matrix):
    eye = jnp.eye(matrix[0].shape[-1], dtype=jnp.float32)
    return eye - matrix[0] * (1.0 / diagonal_guess), -matrix[1] * (1.0 / diagonal_guess)


def inverse(matrix):
    eye = jnp.eye(matrix[0].shape[-1], dtype=jnp.float32)
    b = remainder(matrix)
    square = product(b, b)
    cube = product(b, square)
    scale = 1.0 / diagonal_guess
    return (eye + b[0] + square[0] + cube[0]) * scale, (b[1] + square[1] + cube[1]) * scale


def solve(matrix, source):
    b = remainder(matrix)
    value = source
    for _ in range(3):
        value = plus(source, product(b, value))
    scale = 1.0 / diagonal_guess
    return value[0] * scale, value[1] * scale


def front_kernel(
    gl, gg, onsite, lower, upper, rhs, diag, near_lu, near_s,
    lu, gl_all, gg_all, res, pol,
    in_send, in_recv, out_send, out_recv, lu_send, lu_recv, hop_send, hop_recv,
    mate_send, mate_recv, local, rows_out=None, partner=None,
):
    e, i = lax.axis_index("energy"), lax.axis_index("block")
    energies, count = lax.axis_size("energy"), lax.axis_size("block")
    share = gl.shape[2] // energies
    c, p = lax.rem(e, 2), lax.rem(i, 2)
    mate, side = e + 1 - 2 * c, 1 - p
    pair, onward, behind = i + 1 - 2 * p, i + 2 - 4 * p, i - 2 + 4 * p
    has_onward = jnp.logical_and(onward >= 0, onward < count)
    has_behind = jnp.logical_and(behind >= 0, behind < count)

    fill = [pltpu.make_async_copy((lower, upper)[k], lu.at[k], local.at[k]) for k in (0, 1)]
    for copy in fill:
        copy.start()
    barrier = pltpu.get_barrier_semaphore()
    for k in range(1, energies):
        pl.semaphore_signal(barrier, inc=1, device_id={"energy": lax.rem(e + k, energies)}, device_id_type=MESH)
    pl.semaphore_signal(barrier, inc=1, device_id={"block": pair}, device_id_type=MESH)

    @pl.when(has_onward)
    def _():
        pl.semaphore_signal(barrier, inc=1, device_id={"block": onward}, device_id_type=MESH)

    @pl.when(has_behind)
    def _():
        pl.semaphore_signal(barrier, inc=1, device_id={"block": behind}, device_id_type=MESH)

    peers = energies
    if partner is not None:
        peers = energies + 1
        pl.semaphore_signal(barrier, inc=1, device_id={"block": partner}, device_id_type=MESH)
    pl.semaphore_wait(barrier, peers + has_onward.astype(jnp.int32) + has_behind.astype(jnp.int32))

    def remote(src, dst, send, recv, **where):
        return pltpu.make_async_remote_copy(
            src_ref=src, dst_ref=dst, send_sem=send, recv_sem=recv, device_id=where, device_id_type=MESH
        )

    part = share // 2

    def in_copy(h, k, q, source):
        src, dst = ((gl, gl_all), (gg, gg_all))[k]
        rows = src.at[:, 0, pl.ds(q * share + h * part, part), :]
        there = dst.at[source, :, pl.ds(h * part, part), :]
        return remote(rows, there, in_send.at[h, k, q], in_recv.at[h, k, source], energy=q)

    def out_copy(h, w, source):
        rows = pl.ds(h * part, part)
        return remote(
            res.at[w, :, rows, :], pol.at[source, :, rows, :], out_send.at[h, w], out_recv.at[h, source], energy=w
        )

    for copy in fill:
        copy.wait()
    for h in (0, 1):
        for k in (0, 1):
            for q in range(energies):

                @pl.when(q != e)
                def _():
                    in_copy(h, k, q, e).start()

    own = []
    for k, (src, dst) in enumerate(((gl, gl_all), (gg, gg_all))):
        rows = src.at[:, 0, pl.ds(pl.multiple_of(e * share, 8), share), :]
        own.append(pltpu.make_async_copy(rows, dst.at[e], local.at[k]))
        own[-1].start()

    mine = (lu.at[c, 0], lu.at[c, 1], rhs.at[:, 0])

    def slot(s, k):
        return near_s.at[s] if k == 2 else near_lu.at[s, c, k]

    direct = [remote(mine[k], slot(p, k), lu_send.at[k], lu_recv.at[k], block=pair) for k in range(3)]
    hops = [remote(slot(side, k), slot(p, k), hop_send.at[k], hop_recv.at[k], block=onward) for k in range(3)]
    for copy in direct:
        copy.start()
    shared = [
        remote(slot(s, k), slot(s, k), mate_send.at[j, k], mate_recv.at[j, k], energy=mate)
        for j, s in enumerate((side, p))
        for k in (0, 1)
    ]
    for k in range(3):
        direct[k].wait_recv()

        @pl.when(has_onward)
        def _():
            hops[k].start()

        if k < 2:
            shared[k].start()

    for copy in own:
        copy.wait()
    scale = 1.0 / math.sqrt(energies)
    for h in (0, 1):
        for k in (0, 1):
            for q in range(energies):

                @pl.when(q != e)
                def _():
                    in_copy(h, k, q, q).wait_recv()

        for w in range(energies):

            def step(row, carry, w=w, h=h):
                rows = pl.ds(pl.multiple_of(h * part + row * 8, 8), 8)
                real = imag = None
                for k in range(w, energies):
                    a, b = gl_all[k, 0, rows], gl_all[k, 1, rows]
                    x, y = gg_all[k - w, 0, rows], gg_all[k - w, 1, rows]
                    s, t = a * x - b * y, a * y + b * x
                    real, imag = (s, t) if real is None else (real + s, imag + t)
                res[w, 0, rows] = real * scale
                res[w, 1, rows] = imag * scale
                return carry

            lax.fori_loop(0, part // 8, step, 0)

            @pl.when(w != e)
            def _():
                out_copy(h, w, e).start()

    keep = pltpu.make_async_copy(res.at[e], pol.at[e], local.at[0])
    keep.start()

    @pl.when(has_behind)
    def _():
        for k in range(3):
            hops[k].wait_recv()
            if k < 2:
                shared[2 + k].start()

    def hand_on(q):
        rows_out[0][q].wait_recv()

        @pl.when(has_onward)
        def _():
            rows_out[1][q].start()

    keep.wait()
    for q in range(energies):

        @pl.when(q != e)
        def _():
            out_copy(0, q, q).wait_recv()
            out_copy(1, q, q).wait_recv()

        rows = pl.ds(q * share, share)
        for k in (0, 1):
            diag[k, rows] = onsite[k, 0, rows] - pol[q, k]
        if rows_out is not None:
            rows_out[0][q].start()
            if q > 0:
                hand_on(q - 1)
    if rows_out is not None:
        hand_on(energies - 1)

    for k in range(2):
        shared[k].wait_recv()

    @pl.when(has_behind)
    def _():
        for k in range(2):
            shared[2 + k].wait()

    for k in range(2):
        shared[k].wait_send()
    for k in range(3):
        direct[k].wait_send()

        @pl.when(has_onward)
        def _():
            hops[k].wait_send()

    for q in range(energies):

        @pl.when(q != e)
        def _():
            for h in (0, 1):
                in_copy(h, 0, q, e).wait_send()
                in_copy(h, 1, q, e).wait_send()
                out_copy(h, q, e).wait_send()


def front(g_lesser, g_greater, onsite, lower, upper, rhs):
    energies = lax.axis_size("energy")
    n, columns = onsite.shape[2], rhs.shape[-1]
    share = n // energies
    vmem = pl.BlockSpec(memory_space=pltpu.VMEM)
    f32 = jnp.float32
    dma = pltpu.SemaphoreType.DMA
    pieces = pltpu.VMEM((energies, 2, share, n), f32)
    return pl.pallas_call(
        front_kernel,
        name="front",
        out_shape=(
            jax.ShapeDtypeStruct((2, n, n), f32),
            jax.ShapeDtypeStruct((2, 2, 2, n, n), f32),
            jax.ShapeDtypeStruct((2, 2, n, columns), f32),
        ),
        in_specs=[vmem] * 6,
        out_specs=(vmem,) * 3,
        scratch_shapes=[
            pltpu.VMEM((2, 2, n, n), f32),
            pieces, pieces, pieces, pieces,
            dma((2, 2, energies)), dma((2, 2, energies)), dma((2, energies)), dma((2, energies)),
            dma((3,)), dma((3,)), dma((3,)), dma((3,)),
            dma((2, 2)), dma((2, 2)), dma((2,)),
        ],
        compiler_params=pltpu.CompilerParams(collective_id=0, has_side_effects=True),
    )(g_lesser, g_greater, onsite, lower, upper, rhs)


def halves(x):
    high = x.astype(jnp.bfloat16)
    return high, (x - high.astype(jnp.float32)).astype(jnp.bfloat16)


def factor(a):
    return halves(a[0]), halves(a[1]), halves(a[0] + a[1])


def three_pass(a, b):
    dot = lambda u, v: jnp.dot(u, v, preferred_element_type=jnp.float32)
    return dot(a[0], b[0]) + (dot(a[0], b[1]) + dot(a[1], b[0]))


def times(a, b):
    first, second, third = (three_pass(a[k], b[k]) for k in range(3))
    return first - second, third - first - second


def inverse_of(matrix):
    eye_rows = lax.broadcasted_iota(jnp.int32, matrix[0].shape, 0)
    eye_columns = lax.broadcasted_iota(jnp.int32, matrix[0].shape, 1)
    eye = jnp.where(eye_rows == eye_columns, 1.0, 0.0)
    scale = 1.0 / diagonal_guess
    b = eye - matrix[0] * scale, -matrix[1] * scale
    fb = factor(b)
    square = times(fb, fb)
    cube = times(fb, factor(square))
    return (eye + b[0] + square[0] + cube[0]) * scale, (b[1] + square[1] + cube[1]) * scale


def rounded_product(a, b):
    dot = lambda u, v: jnp.dot(u, v, preferred_element_type=jnp.float32)
    first, second, third = (dot(a[k], b[k]) for k in range(3))
    return first - second, third - first - second


def rounded(a):
    return tuple(v.astype(jnp.bfloat16) for v in (a[0], a[1], a[0] + a[1]))


def unit_of(matrix):
    rows = lax.broadcasted_iota(jnp.int32, matrix[0].shape, 0)
    columns = lax.broadcasted_iota(jnp.int32, matrix[0].shape, 1)
    return jnp.where(rows == columns, 1.0, 0.0)


def remainder_of(matrix):
    return unit_of(matrix) - matrix[0] * (1.0 / diagonal_guess), -matrix[1] * (1.0 / diagonal_guess)


def lean_inverse(matrix):
    eye, b = unit_of(matrix), remainder_of(matrix)
    scale = 1.0 / diagonal_guess
    split = factor(b)
    square = times(split, split)
    cube = rounded_product(rounded(b), rounded(square))
    return (eye + b[0] + square[0] + cube[0]) * scale, (b[1] + square[1] + cube[1]) * scale


def stacked(a, b):
    return tuple(tuple(jnp.concatenate([a[k][j], b[k][j]], axis=0) for j in (0, 1)) for k in range(3))


def apply(a, b):
    columns = b[0].shape[1]
    w = halves(jnp.concatenate([b[0], b[1]], axis=1))
    p, q = three_pass(a[0], w), three_pass(a[1], w)
    return p[:, :columns] - q[:, columns:], p[:, columns:] + q[:, :columns]


def line_kernel(
    gl, gg, onsite, lower, upper, rhs, out,
    gl2, gg2, on2, zin_h, res_h, pin_h, zin_a, res_a, pin_a, zin_b, res_b, pin_b, dpair, diag, src, lu, dp, fp, sp, value,
    z_send, z_recv_h, p_send, p_recv_h, z_recv_a, p_recv_a, z_recv_b, p_recv_b, pair_send, pair_recv, pair_local,
    d_send, d_recv, d_local, dm_send, dm_recv, t_send, t_recv,
    s_send, s_recv, s_local, sm_send, sm_recv,
    l_send, l_recv, l_local, lm_send, lm_recv, out_sem, edge_diag, edge_src, e_sem, flu,
):
    e, i = lax.axis_index("energy"), lax.axis_index("block")
    energies, count = lax.axis_size("energy"), lax.axis_size("block")
    n = diag.shape[-1]
    half = n // 2
    many, r = zin_a.shape[0], zin_a.shape[3]
    few, fine = zin_b.shape[0], zin_b.shape[3]
    edge, end = few * fine, few + many
    starts = [k * fine for k in range(few)] + [edge + k * r for k in range(many)]
    starts += [half - edge + k * fine for k in range(few + 1)]
    segments = (
        (0, fine, 0, zin_h, res_h, pin_h, z_recv_h, p_recv_h),
        (1, r, edge, zin_a, res_a, pin_a, z_recv_a, p_recv_a),
        (2, fine, half - edge, zin_b, res_b, pin_b, z_recv_b, p_recv_b),
    )
    mid = energies // 2
    z, h = e // 2, lax.rem(e, 2)
    y, x = i // 2, lax.rem(i, 2)
    sib, xn, yn = e + 1 - 2 * h, i + 1 - 2 * x, i + 2 - 4 * y
    dn = yn + 1 - 2 * x
    outer, inner, center, far = z == 0, z == 1, z == 2, z == 3
    mine = pl.ds(pl.multiple_of(h * half, half), half)
    other = pl.ds(pl.multiple_of((1 - h) * half, half), half)
    scale = 1.0 / math.sqrt(energies)

    def remote(a, b, send, recv, energy=e, block=i):
        return pltpu.make_async_remote_copy(
            src_ref=a, dst_ref=b, send_sem=send, recv_sem=recv,
            device_id={"energy": energy, "block": block}, device_id_type=MESH,
        )

    barrier = pltpu.get_barrier_semaphore()
    for k in range(1, energies):
        pl.semaphore_signal(barrier, inc=1, device_id={"energy": lax.rem(e + k, energies)}, device_id_type=MESH)
    for block in (xn, yn):
        for c in (0, 1):
            pl.semaphore_signal(
                barrier, inc=1, device_id={"energy": 2 * z + c, "block": block}, device_id_type=MESH
            )
    pair_own = []
    for k, (a, b) in enumerate(((gg, gg2), (gl, gl2), (onsite, on2))):
        pair_own.append(pltpu.make_async_copy(a.at[:, 0, mine], b.at[h], pair_local.at[k]))
        pair_own[-1].start()
    pl.semaphore_wait(barrier, energies + 3)

    def valid(j, w):
        return j > 0 if w == 0 else j < count - 1

    coupling = (lower, upper)
    for w in (0, 1):

        @pl.when(valid(i, w))
        def _(w=w):
            remote(coupling[w].at[:, mine], lu.at[i, w, :, mine], l_send.at[0, w], l_recv.at[0, w], block=xn).start()
            remote(coupling[w].at[:, mine], lu.at[i, w, :, mine], l_send.at[1, w], l_recv.at[1, w], block=yn).start()
            pltpu.make_async_copy(coupling[w], lu.at[i, w], l_local.at[w]).start()

    def rows_of(g):
        return pl.ds(g * half, half)

    @pl.when(y == h)
    def _():
        pltpu.make_async_copy(rhs.at[:, 0], src.at[i], s_local).start()
        remote(rhs.at[:, 0], src.at[i], sm_send.at[0], sm_recv.at[0], energy=sib).start()
        for g in (0, 1):
            remote(
                rhs.at[:, 0, rows_of(g)], src.at[i, :, rows_of(g)], s_send.at[0], s_recv.at[0],
                energy=2 * z + g, block=xn,
            ).start()

    @pl.when(y != h)
    def _():
        for g in (0, 1):
            remote(
                rhs.at[:, 0, rows_of(g)], src.at[i, :, rows_of(g)], s_send.at[0], s_recv.at[1],
                energy=2 * z + g, block=yn,
            ).start()

    def z_copies(seg, k, which):
        _, size, base, zin, _, _, z_recv, _ = seg

        def to(a, slot, g, target, sem):
            piece = a.at[:, 0, pl.ds(pl.multiple_of(g * half + base + k * size, 8), size)]
            return remote(piece, zin.at[k, slot], z_send.at[sem], z_recv.at[k], energy=target + g)

        for g in (0, 1):
            if which == 0:
                to(gg, e, g, mid, 0).start()
                to(gg, e, g, mid - 2, 1).start()
            elif which == 1:
                to(gg, e, g, mid, 0).start()
            else:
                to(gl, e - mid + 2, g, mid, 1).start()
                to(gg, e - mid + 4, g, mid, 0).start()

    for which, role in ((0, outer), (1, inner), (3, far)):

        @pl.when(role)
        def _(which=which):
            for seg, steps in zip(segments, (few, many, few)):

                def body(k, carry, seg=seg):
                    z_copies(seg, k, which)
                    return carry

                lax.fori_loop(0, steps, body, 0)

    pairs = []
    for k, (a, b) in enumerate(((gg, gg2), (gl, gl2), (onsite, on2))):
        pairs.append(remote(a.at[:, 0, other], b.at[h], pair_send.at[k], pair_recv.at[k], energy=sib))
        pairs[-1].start()

    def arrived(ref, sem):
        remote(ref, ref, sem, sem).wait_recv()

    def sent(ref, sem):
        remote(ref, ref, sem, sem).wait_send()

    def lu_direct_x(w):
        @pl.when(valid(xn, w))
        def _():
            part = lu.at[xn, w, :, mine]
            arrived(part, l_recv.at[0, w])
            remote(part, part, l_send.at[2, w], l_recv.at[2, w], block=yn).start()
            remote(part, part, lm_send.at[0, w], lm_recv.at[0, w], energy=sib).start()

    def lu_direct_y(w):
        @pl.when(valid(yn, w))
        def _():
            part = lu.at[yn, w, :, mine]
            arrived(part, l_recv.at[1, w])
            remote(part, part, lm_send.at[1, w], lm_recv.at[1, w], energy=sib).start()

    def lu_passed(w):
        @pl.when(valid(dn, w))
        def _():
            part = lu.at[dn, w, :, mine]
            arrived(part, l_recv.at[2, w])
            remote(part, part, lm_send.at[2, w], lm_recv.at[2, w], energy=sib).start()

    def src_direct():
        part = src.at[yn, :, mine]
        arrived(part, s_recv.at[1])
        remote(part, part, s_send.at[1], s_recv.at[2], block=xn).start()
        remote(part, part, sm_send.at[2], sm_recv.at[2], energy=sib).start()
        part = src.at[xn, :, mine]
        arrived(part, s_recv.at[0])
        remote(part, part, sm_send.at[1], sm_recv.at[1], energy=sib).start()

    def src_passed():
        part = src.at[dn, :, mine]
        arrived(part, s_recv.at[2])
        remote(part, part, sm_send.at[3], sm_recv.at[3], energy=sib).start()

    for copy in pair_own:
        copy.wait()
    for copy in pairs:
        copy.wait_recv()

    def tiles(seg, k):
        size, base = seg[1], seg[2]
        for q in range(size // 8):
            for lane in range(n // 128):
                cols = slice(lane * 128, lane * 128 + 128)
                yield slice(q * 8, q * 8 + 8), pl.ds(pl.multiple_of(base + k * size + q * 8, 8), 8), cols

    def correlate(left, right, w):
        real = imag = None
        for k in left:
            if k - w in right:
                (a, b), (u, v) = left[k], right[k - w]
                s, t = a * u - b * v, a * v + b * u
                real, imag = (s, t) if real is None else (real + s, imag + t)
        return real, imag

    def p_copy(seg, k, part, slot, target, sem=None):
        where, _, _, _, res, pin, _, p_recv = seg
        sem = part if sem is None else sem
        return remote(
            res.at[k, pl.ds(2 * part, 2)], pin.at[k, pl.ds(slot, 2)], p_send.at[where, sem], p_recv.at[k],
            energy=target + h,
        )

    def ahead(seg, k):
        _, _, _, zin, res, _, z_recv, _ = seg

        @pl.when(inner)
        def _():
            arrived(zin.at[k, pl.ds(0, 2)], z_recv.at[k])
            for here, rows, cols in tiles(seg, k):
                both = lambda ref, *at: (ref[(*at, 0, here, cols)], ref[(*at, 1, here, cols)])
                pair = lambda ref, c: (ref[c, 0, rows, cols], ref[c, 1, rows, cols])
                left = {2: pair(gl2, 0), 3: pair(gl2, 1)}
                right = {0: both(zin, k, 0), 1: both(zin, k, 1), 2: pair(gg2, 0), 3: pair(gg2, 1)}
                for w in range(mid):
                    value = correlate(left, right, w)
                    for m in (0, 1):
                        res[k, w, m, here, cols] = value[m]
            p_copy(seg, k, 0, 2, 0).start()

    def polarize(seg, k):
        _, _, _, zin, res, pin, z_recv, p_recv = seg

        @pl.when(center)
        def _():
            arrived(zin.at[k], z_recv.at[k])
            for here, rows, cols in tiles(seg, k):
                both = lambda ref, *at: (ref[(*at, 0, here, cols)], ref[(*at, 1, here, cols)])
                pair = lambda ref, c: (ref[c, 0, rows, cols], ref[c, 1, rows, cols])
                left = {mid: pair(gl2, 0), mid + 1: pair(gl2, 1), mid + 2: both(zin, k, 4), mid + 3: both(zin, k, 5)}
                right = {c: both(zin, k, c) for c in range(4)}
                right.update({mid: pair(gg2, 0), mid + 1: pair(gg2, 1)})
                right.update({mid + 2: both(zin, k, 6), mid + 3: both(zin, k, 7)})
                for w in range(energies):
                    value = correlate(left, right, w)
                    for m in (0, 1):
                        if w in (mid, mid + 1):
                            dpair[w - mid, m, rows, cols] = on2[w - mid, m, rows, cols] - value[m] * scale
                        else:
                            res[k, w if w < mid else w - 2, m, here, cols] = value[m]
            for part, target in enumerate((0, 2, mid + 2)):
                p_copy(seg, k, part, 0, target).start()

        @pl.when(inner)
        def _():
            arrived(pin.at[k, pl.ds(0, 2)], p_recv.at[k])
            for here, rows, cols in tiles(seg, k):
                for c in (0, 1):
                    for m in (0, 1):
                        total = res[k, 2 + c, m, here, cols] + pin[k, c, m, here, cols]
                        dpair[c, m, rows, cols] = on2[c, m, rows, cols] - total * scale

        @pl.when(outer)
        def _():
            arrived(pin.at[k], p_recv.at[k])
            for here, rows, cols in tiles(seg, k):
                pair = lambda ref, c: (ref[c, 0, rows, cols], ref[c, 1, rows, cols])
                left = {0: pair(gl2, 0), 1: pair(gl2, 1)}
                right = {0: pair(gg2, 0), 1: pair(gg2, 1)}
                for c in (0, 1):
                    value = correlate(left, right, c)
                    for m in (0, 1):
                        total = value[m] + (pin[k, c, m, here, cols] + pin[k, 2 + c, m, here, cols])
                        dpair[c, m, rows, cols] = on2[c, m, rows, cols] - total * scale

        @pl.when(far)
        def _():
            arrived(pin.at[k, pl.ds(0, 2)], p_recv.at[k])
            for here, rows, cols in tiles(seg, k):
                for c in (0, 1):
                    for m in (0, 1):
                        dpair[c, m, rows, cols] = on2[c, m, rows, cols] - pin[k, c, m, here, cols] * scale

    def strip(first, last):
        return pl.ds(pl.multiple_of(h * half + starts[first], 8), starts[last] - starts[first])

    def spread(seg, k, at, passed=True):
        size, base = seg[1], seg[2]
        sub = pl.ds(pl.multiple_of(base + k * size, 8), size)
        there = diag.at[i, :, pl.ds(pl.multiple_of(h * half + base + k * size, 8), size)]
        if not passed:
            remote(dpair.at[1 - y, :, sub], there, t_send.at[0], d_recv.at[2, at], block=dn).start()
        remote(dpair.at[1 - y, :, sub], there, d_send.at[1], d_recv.at[1, at], block=yn).start()
        remote(dpair.at[y, :, sub], there, d_send.at[0], d_recv.at[0, at], block=xn).start()
        remote(dpair.at[y, :, sub], there, dm_send.at[0], dm_recv.at[0], energy=sib).start()
        pltpu.make_async_copy(dpair.at[y, :, sub], there, d_local).start()

    def gather_y(first, last):
        for k in range(first, last):
            arrived(diag.at[yn, :, strip(k, k + 1)], d_recv.at[1, k])
        part = diag.at[yn, :, strip(first, last)]
        if first < end:
            remote(part, part, d_send.at[2], d_recv.at[2, first], block=xn).start()
        remote(part, part, dm_send.at[2], dm_recv.at[2], energy=sib).start()

    def gather_x(first, last):
        for k in range(first, last):
            arrived(diag.at[xn, :, strip(k, k + 1)], d_recv.at[0, k])
        part = diag.at[xn, :, strip(first, last)]
        remote(part, part, dm_send.at[1], dm_recv.at[1], energy=sib).start()

    def gather(first, last):
        gather_y(first, last)
        gather_x(first, last)

    def gather_passed(first, last):
        part = diag.at[dn, :, strip(first, last)]
        arrived(part, d_recv.at[2, first])
        remote(part, part, dm_send.at[3], dm_recv.at[3], energy=sib).start()

    def prefactor(k, j, w):
        @pl.when(valid(j, w))
        def _():
            if k is None:
                pltpu.make_async_copy(coupling[w], lu.at[i, w], l_local.at[w]).wait()
            else:
                arrived(lu.at[j, w, :, other], lm_recv.at[k, w])

            def step(block, carry):
                rows = pl.ds(pl.multiple_of(block * 16, 16), 16)
                split = factor((lu[j, w, 0, rows], lu[j, w, 1, rows]))
                for at in range(3):
                    for part in (0, 1):
                        flu[j, w, 2 * at + part, rows] = split[at][part]
                return carry

            lax.fori_loop(0, n // 16, step, 0)

    plan = {
        0: [lambda: prefactor(None, i, 0)],
        1: [lambda: lu_direct_x(1), lambda: prefactor(None, i, 1)],
        2: [src_direct, lambda: prefactor(0, xn, 0)],
        3: [lambda: lu_direct_y(0), lambda: lu_direct_y(1), lambda: prefactor(0, xn, 1)],
        4: [lambda: gather_y(0, 3), lambda: prefactor(1, yn, 0)],
        5: [lambda: gather_y(3, 5), lambda: prefactor(1, yn, 1)],
    }

    def turn(k, carry):
        @pl.when(k < many - 1)
        def _():
            ahead(segments[1], k + 1)

        @pl.when(k == many - 1)
        def _():
            ahead(segments[2], 0)

        polarize(segments[1], k)
        spread(segments[1], k, few + k)
        for at, work in plan.items():

            @pl.when(k == at)
            def _(work=work):
                for step in work:
                    step()

        return carry

    ahead(segments[0], 0)
    ahead(segments[0], 1)
    polarize(segments[0], 0)
    spread(segments[0], 0, 0)
    ahead(segments[1], 0)
    polarize(segments[0], 1)
    spread(segments[0], 1, 1)
    lu_direct_x(0)
    lax.fori_loop(0, many, turn, 0)
    ahead(segments[2], 1)
    polarize(segments[2], 0)
    spread(segments[2], 0, end, passed=False)
    gather_y(5, 6)
    polarize(segments[2], 1)
    spread(segments[2], 1, end + 1, passed=False)
    gather_y(6, 8)
    gather_x(0, 8)
    src_passed()
    lu_passed(0)
    lu_passed(1)
    gather_passed(0, 3)
    gather_passed(3, 5)
    gather_passed(5, 6)
    prefactor(2, dn, 0)
    prefactor(2, dn, 1)
    for k in (end, end + 1):
        gather(k, k + 1)
        gather_passed(k, k + 1)
    gather_passed(6, 8)

    pltpu.make_async_copy(dpair.at[y], diag.at[i, :, mine], d_local).wait()
    for k, j in enumerate((i, xn, yn, dn)):
        arrived(diag.at[j, :, other], dm_recv.at[k])

    @pl.when(y == h)
    def _():
        pltpu.make_async_copy(rhs.at[:, 0], src.at[i], s_local).wait()

    @pl.when(y != h)
    def _():
        arrived(src.at[i], sm_recv.at[0])

    for k, j in enumerate((xn, yn, dn)):
        arrived(src.at[j, :, other], sm_recv.at[k + 1])

    a, b, m, q = 3 * x, 2 - x, 1 + x, 3 - 3 * x
    couple = lambda j, w: tuple((flu[j, w, 2 * k], flu[j, w, 2 * k + 1]) for k in range(3))
    diagonal = lambda j: (diag[j, 0], diag[j, 1])
    source = lambda j: (src[j, 0], src[j, 1])

    def put(ref, at, v):
        ref[at, 0], ref[at, 1] = v

    edge_d = remote(edge_diag, edge_diag, e_sem.at[0], e_sem.at[1], energy=sib)
    edge_s = remote(edge_src, edge_src, e_sem.at[2], e_sem.at[3], energy=sib)

    @pl.when(h == y)
    def _():
        t = factor(times(couple(b, 1 - x), factor(inverse_of(diagonal(q)))))
        edge_diag[0], edge_diag[1] = times(t, couple(q, x))
        edge_d.start()
        edge_src[0], edge_src[1] = apply(t, source(q))
        edge_s.start()

    inv = factor(inverse_of(diagonal(m)))
    t = factor(times(stacked(couple(a, 1 - x), couple(b, x)), inv))
    top, low = (lambda v: (v[0][:n], v[1][:n])), (lambda v: (v[0][n:], v[1][n:]))
    v = times(t, couple(m, x))
    put(dp, 0, minus(diagonal(a), top(v)))
    put(fp, 1, low(v))
    v = times(t, couple(m, 1 - x))
    put(dp, 1, minus(diagonal(b), low(v)))
    put(fp, 0, top(v))
    v = apply(t, source(m))
    put(sp, 0, minus(source(a), top(v)))
    put(sp, 1, minus(source(b), low(v)))

    @pl.when(h != y)
    def _():
        edge_d.wait_recv()
        edge_s.wait_recv()

    for k in (0, 1):
        dp[1, k] = dp[1, k] - edge_diag[k]
        sp[1, k] = sp[1, k] - edge_src[k]

    this = jnp.where(h == x, 0, 1)
    that = 1 - this
    at = lambda ref, k: (ref[k, 0], ref[k, 1])
    t = factor(times(factor(at(fp, this)), factor(lean_inverse(at(dp, that)))))
    last = minus(at(dp, this), times(t, factor(at(fp, that))))
    right = plus(at(sp, this), apply(t, at(sp, that)))
    rest = factor(remainder_of(last))
    inverse_guess = 1.0 / diagonal_guess
    found = right
    for _ in range(3):
        found = plus(right, apply(rest, found))
    value[0], value[1] = found[0] * inverse_guess, found[1] * inverse_guess

    home = remote(value, out.at[:, 0], out_sem.at[0], out_sem.at[1], energy=2 * z + y, block=2 * h + x)
    keep = pltpu.make_async_copy(value, out.at[:, 0], out_sem.at[0])

    @pl.when(h != y)
    def _():
        home.start()

    @pl.when(h == y)
    def _():
        keep.start()
        keep.wait()

    whole_array = gg.at[:, 0]

    @pl.when(outer)
    def _():
        sent(whole_array, z_send.at[0])
        sent(whole_array, z_send.at[1])

    @pl.when(inner)
    def _():
        sent(whole_array, z_send.at[0])
        for seg in segments:
            sent(seg[4].at[:, pl.ds(0, 2)], p_send.at[seg[0], 0])

    @pl.when(far)
    def _():
        sent(whole_array, z_send.at[0])
        sent(whole_array, z_send.at[1])

    @pl.when(center)
    def _():
        for seg in segments:
            for k in range(3):
                sent(seg[4].at[:, pl.ds(2 * k, 2)], p_send.at[seg[0], k])

    for copy in pairs:
        copy.wait_send()
    for k in range(2):
        sent(dpair.at[0], d_send.at[k])
    sent(dpair.at[0, :, pl.ds(0, half - edge)], d_send.at[2])
    sent(dpair.at[0, :, pl.ds(0, edge)], t_send.at[0])
    for k in range(4):
        sent(dpair.at[0], dm_send.at[k])
    part = src.at[0, :, mine]

    @pl.when(y == h)
    def _():
        sent(rhs.at[:, 0], sm_send.at[0])

    sent(rhs.at[:, 0], s_send.at[0])
    sent(part, s_send.at[1])
    for k in range(3):
        sent(part, sm_send.at[k + 1])
    for w in (0, 1):
        part = lu.at[0, w, :, mine]

        @pl.when(valid(i, w))
        def _(w=w, part=part):
            sent(part, l_send.at[0, w])
            sent(part, l_send.at[1, w])

        for k, j in enumerate((xn, yn, dn)):

            @pl.when(valid(j, w))
            def _(k=k, w=w, part=part):
                if k == 0:
                    sent(part, l_send.at[2, w])
                sent(part, lm_send.at[k, w])

    @pl.when(h == y)
    def _():
        edge_d.wait_send()
        edge_s.wait_send()

    @pl.when(h != y)
    def _():
        home.wait()


def line(g_lesser, g_greater, onsite, lower, upper, rhs):
    count = lax.axis_size("block")
    n, columns = onsite.shape[2], rhs.shape[-1]
    half = n // 2
    r = half // 8
    many, few, fine = 6, 2, r // 2
    f32 = jnp.float32
    dma = pltpu.SemaphoreType.DMA
    anywhere = pl.BlockSpec(memory_space=pl.ANY)
    pair = pltpu.VMEM((2, 2, half, n), f32)
    return pl.pallas_call(
        line_kernel,
        name="line",
        out_shape=pltpu.VMEM((2, 1, n, columns), f32),
        in_specs=[anywhere] * 6,
        out_specs=anywhere,
        scratch_shapes=[
            pair, pair, pair,
            pltpu.VMEM((few, 8, 2, fine, n), f32),
            pltpu.VMEM((few, 6, 2, fine, n), f32),
            pltpu.VMEM((few, 4, 2, fine, n), f32),
            pltpu.VMEM((many, 8, 2, r, n), f32),
            pltpu.VMEM((many, 6, 2, r, n), f32),
            pltpu.VMEM((many, 4, 2, r, n), f32),
            pltpu.VMEM((few, 8, 2, fine, n), f32),
            pltpu.VMEM((few, 6, 2, fine, n), f32),
            pltpu.VMEM((few, 4, 2, fine, n), f32),
            pair,
            pltpu.VMEM((count, 2, n, n), f32),
            pltpu.VMEM((count, 2, n, columns), f32),
            pltpu.VMEM((count, 2, 2, n, n), f32),
            pltpu.VMEM((2, 2, n, n), f32),
            pltpu.VMEM((2, 2, n, n), f32),
            pltpu.VMEM((2, 2, n, columns), f32),
            pltpu.VMEM((2, n, columns), f32),
            dma((2,)), dma((few,)), dma((3, 3)), dma((few,)), dma((many,)), dma((many,)), dma((few,)), dma((few,)),
            dma((3,)), dma((3,)), dma((3,)),
            dma((3,)), dma((3, many + 2 * few)), dma, dma((4,)), dma((4,)), dma((1,)), dma((1,)),
            dma((2,)), dma((3,)), dma, dma((4,)), dma((4,)),
            dma((3, 2)), dma((3, 2)), dma((2,)), dma((3, 2)), dma((3, 2)), dma((2,)),
            pltpu.VMEM((2, n, n), f32), pltpu.VMEM((2, n, columns), f32), dma((4,)),
            pltpu.VMEM((count, 2, 6, n, n), jnp.bfloat16),
        ],
        compiler_params=pltpu.CompilerParams(
            collective_id=1, has_side_effects=True, vmem_limit_bytes=60 * 1024 * 1024
        ),
    )(g_lesser, g_greater, onsite, lower, upper, rhs)


def shifted(value, steps):
    count = lax.axis_size("block")
    leading, last = max(0, -steps), min(count, count - steps)
    pairs = [(k, k + steps) for k in range(leading, last)]
    return lax.ppermute(value, "block", pairs)


def shards(g_lesser, g_greater, onsite, lower, upper, rhs):
    index = lax.axis_index("block")
    count = lax.axis_size("block")
    levels = count.bit_length() - 1
    n = onsite.shape[-1]
    both = jnp.concatenate(
        [jnp.where(index > 0, lower, 0.0), jnp.where(index < count - 1, upper, 0.0)], axis=-1
    )
    if levels == 2 and lax.axis_size("energy") == 8:
        return line(g_lesser, g_greater, onsite, lower, upper, rhs)
    diag, near_lu, near_s = front(g_lesser, g_greater, onsite, lower, upper, rhs)
    diag = parts(diag)
    first, final = index < 2, index >= count - 2
    low, up = cut(parts(both), 0, n), cut(parts(both), n, 2 * n)
    source = parts(rhs[:, 0])
    for depth in range(levels):
        stride = 1 << depth
        inv = inverse(diag)
        if depth == levels - 1:
            coupling = tuple(jnp.where(index < stride, up[k], low[k]) for k in (0, 1))
            sent = product(inv, wide(coupling, source))
            swap = [(k, k ^ stride) for k in range(count)]
            got = parts(lax.ppermute(jnp.stack(sent), "block", swap))
            change = product(coupling, got)
            diag = minus(diag, cut(change, 0, n))
            source = minus(source, cut(change, n, None))
        elif depth == 0:
            packed = jnp.stack(inv)
            inv_left, inv_right = parts(shifted(packed, 1)), parts(shifted(packed, -1))
            t, w = product(low, inv_left), product(up, inv_right)
            lu_l, lu_r = near_lu[0], near_lu[1]
            change = product(t, wide(parts(lu_l[0]), parts(lu_l[1]), parts(near_s[0])))
            other = product(w, wide(parts(lu_r[0]), parts(lu_r[1]), parts(near_s[1])))
            change = tuple(jnp.where(index > 0, v, 0.0) for v in change)
            other = tuple(jnp.where(index < count - 1, v, 0.0) for v in other)
            diag = minus(minus(diag, cut(change, n, 2 * n)), cut(other, 0, n))
            source = minus(minus(source, cut(change, 2 * n, None)), cut(other, 2 * n, None))
            low = tuple(jnp.where(first, 0.0, -v) for v in cut(change, 0, n))
            up = tuple(jnp.where(final, 0.0, -v) for v in cut(other, n, 2 * n))
        else:
            sent = jnp.stack(product(inv, wide(low, up, source)))
            left, right = parts(shifted(sent, stride)), parts(shifted(sent, -stride))
            change, other = product(low, left), product(up, right)
            diag = minus(minus(diag, cut(change, n, 2 * n)), cut(other, 0, n))
            source = minus(minus(source, cut(change, 2 * n, None)), cut(other, 2 * n, None))
            low = tuple(-v for v in cut(change, 0, n))
            up = tuple(-v for v in cut(other, n, 2 * n))
    return jnp.stack(solve(diag, source))[:, None]


def solution(mesh):
    placed = (
        P(None, "energy", "block", None),
        P(None, "energy", "block", None),
        P(None, "energy", "block", None),
        P(None, "block", None),
        P(None, "block", None),
        P(None, "energy", "block", None),
    )
    return jax.shard_map(
        shards,
        mesh=mesh,
        in_specs=placed,
        out_specs=P(None, "energy", "block", None),
        check_vma=False,
    )
```

```python
import math

import jax
import jax.numpy as jnp
from jax import lax
from jax.experimental import pallas as pl
from jax.experimental.pallas import tpu as pltpu
from jax.sharding import PartitionSpec as P

diagonal_guess = 5.0
MODE = lax.Precision.HIGH
MESH = pl.DeviceIdType.MESH


def real_product(a, b):
    return jnp.matmul(a, b, precision=MODE)


def product(a, b):
    ar, ai = a
    br, bi = b
    return (
        real_product(ar, br) - real_product(ai, bi),
        real_product(ar, bi) + real_product(ai, br),
    )


def parts(a):
    return a[0], a[1]


def plus(a, b):
    return a[0] + b[0], a[1] + b[1]


def minus(a, b):
    return a[0] - b[0], a[1] - b[1]


def wide(*pieces):
    return tuple(jnp.concatenate([p[k] for p in pieces], axis=-1) for k in (0, 1))


def cut(a, start, stop):
    return a[0][:, start:stop], a[1][:, start:stop]


def remainder(matrix):
    eye = jnp.eye(matrix[0].shape[-1], dtype=jnp.float32)
    return eye - matrix[0] * (1.0 / diagonal_guess), -matrix[1] * (1.0 / diagonal_guess)


def inverse(matrix):
    eye = jnp.eye(matrix[0].shape[-1], dtype=jnp.float32)
    b = remainder(matrix)
    square = product(b, b)
    cube = product(b, square)
    scale = 1.0 / diagonal_guess
    return (eye + b[0] + square[0] + cube[0]) * scale, (b[1] + square[1] + cube[1]) * scale


def solve(matrix, source):
    b = remainder(matrix)
    value = source
    for _ in range(3):
        value = plus(source, product(b, value))
    scale = 1.0 / diagonal_guess
    return value[0] * scale, value[1] * scale


def front_kernel(
    gl, gg, onsite, lower, upper, rhs, diag, near_lu, near_s,
    lu, gl_all, gg_all, res, pol,
    in_send, in_recv, out_send, out_recv, lu_send, lu_recv, hop_send, hop_recv,
    mate_send, mate_recv, local, rows_out=None, partner=None,
):
    e, i = lax.axis_index("energy"), lax.axis_index("block")
    energies, count = lax.axis_size("energy"), lax.axis_size("block")
    share = gl.shape[2] // energies
    c, p = lax.rem(e, 2), lax.rem(i, 2)
    mate, side = e + 1 - 2 * c, 1 - p
    pair, onward, behind = i + 1 - 2 * p, i + 2 - 4 * p, i - 2 + 4 * p
    has_onward = jnp.logical_and(onward >= 0, onward < count)
    has_behind = jnp.logical_and(behind >= 0, behind < count)

    fill = [pltpu.make_async_copy((lower, upper)[k], lu.at[k], local.at[k]) for k in (0, 1)]
    for copy in fill:
        copy.start()
    barrier = pltpu.get_barrier_semaphore()
    for k in range(1, energies):
        pl.semaphore_signal(barrier, inc=1, device_id={"energy": lax.rem(e + k, energies)}, device_id_type=MESH)
    pl.semaphore_signal(barrier, inc=1, device_id={"block": pair}, device_id_type=MESH)

    @pl.when(has_onward)
    def _():
        pl.semaphore_signal(barrier, inc=1, device_id={"block": onward}, device_id_type=MESH)

    @pl.when(has_behind)
    def _():
        pl.semaphore_signal(barrier, inc=1, device_id={"block": behind}, device_id_type=MESH)

    peers = energies
    if partner is not None:
        peers = energies + 1
        pl.semaphore_signal(barrier, inc=1, device_id={"block": partner}, device_id_type=MESH)
    pl.semaphore_wait(barrier, peers + has_onward.astype(jnp.int32) + has_behind.astype(jnp.int32))

    def remote(src, dst, send, recv, **where):
        return pltpu.make_async_remote_copy(
            src_ref=src, dst_ref=dst, send_sem=send, recv_sem=recv, device_id=where, device_id_type=MESH
        )

    part = share // 2

    def in_copy(h, k, q, source):
        src, dst = ((gl, gl_all), (gg, gg_all))[k]
        rows = src.at[:, 0, pl.ds(q * share + h * part, part), :]
        there = dst.at[source, :, pl.ds(h * part, part), :]
        return remote(rows, there, in_send.at[h, k, q], in_recv.at[h, k, source], energy=q)

    def out_copy(h, w, source):
        rows = pl.ds(h * part, part)
        return remote(
            res.at[w, :, rows, :], pol.at[source, :, rows, :], out_send.at[h, w], out_recv.at[h, source], energy=w
        )

    for copy in fill:
        copy.wait()
    for h in (0, 1):
        for k in (0, 1):
            for q in range(energies):

                @pl.when(q != e)
                def _():
                    in_copy(h, k, q, e).start()

    own = []
    for k, (src, dst) in enumerate(((gl, gl_all), (gg, gg_all))):
        rows = src.at[:, 0, pl.ds(pl.multiple_of(e * share, 8), share), :]
        own.append(pltpu.make_async_copy(rows, dst.at[e], local.at[k]))
        own[-1].start()

    mine = (lu.at[c, 0], lu.at[c, 1], rhs.at[:, 0])

    def slot(s, k):
        return near_s.at[s] if k == 2 else near_lu.at[s, c, k]

    direct = [remote(mine[k], slot(p, k), lu_send.at[k], lu_recv.at[k], block=pair) for k in range(3)]
    hops = [remote(slot(side, k), slot(p, k), hop_send.at[k], hop_recv.at[k], block=onward) for k in range(3)]
    for copy in direct:
        copy.start()
    shared = [
        remote(slot(s, k), slot(s, k), mate_send.at[j, k], mate_recv.at[j, k], energy=mate)
        for j, s in enumerate((side, p))
        for k in (0, 1)
    ]
    for k in range(3):
        direct[k].wait_recv()

        @pl.when(has_onward)
        def _():
            hops[k].start()

        if k < 2:
            shared[k].start()

    for copy in own:
        copy.wait()
    scale = 1.0 / math.sqrt(energies)
    for h in (0, 1):
        for k in (0, 1):
            for q in range(energies):

                @pl.when(q != e)
                def _():
                    in_copy(h, k, q, q).wait_recv()

        for w in range(energies):

            def step(row, carry, w=w, h=h):
                rows = pl.ds(pl.multiple_of(h * part + row * 8, 8), 8)
                real = imag = None
                for k in range(w, energies):
                    a, b = gl_all[k, 0, rows], gl_all[k, 1, rows]
                    x, y = gg_all[k - w, 0, rows], gg_all[k - w, 1, rows]
                    s, t = a * x - b * y, a * y + b * x
                    real, imag = (s, t) if real is None else (real + s, imag + t)
                res[w, 0, rows] = real * scale
                res[w, 1, rows] = imag * scale
                return carry

            lax.fori_loop(0, part // 8, step, 0)

            @pl.when(w != e)
            def _():
                out_copy(h, w, e).start()

    keep = pltpu.make_async_copy(res.at[e], pol.at[e], local.at[0])
    keep.start()

    @pl.when(has_behind)
    def _():
        for k in range(3):
            hops[k].wait_recv()
            if k < 2:
                shared[2 + k].start()

    def hand_on(q):
        rows_out[0][q].wait_recv()

        @pl.when(has_onward)
        def _():
            rows_out[1][q].start()

    keep.wait()
    for q in range(energies):

        @pl.when(q != e)
        def _():
            out_copy(0, q, q).wait_recv()
            out_copy(1, q, q).wait_recv()

        rows = pl.ds(q * share, share)
        for k in (0, 1):
            diag[k, rows] = onsite[k, 0, rows] - pol[q, k]
        if rows_out is not None:
            rows_out[0][q].start()
            if q > 0:
                hand_on(q - 1)
    if rows_out is not None:
        hand_on(energies - 1)

    for k in range(2):
        shared[k].wait_recv()

    @pl.when(has_behind)
    def _():
        for k in range(2):
            shared[2 + k].wait()

    for k in range(2):
        shared[k].wait_send()
    for k in range(3):
        direct[k].wait_send()

        @pl.when(has_onward)
        def _():
            hops[k].wait_send()

    for q in range(energies):

        @pl.when(q != e)
        def _():
            for h in (0, 1):
                in_copy(h, 0, q, e).wait_send()
                in_copy(h, 1, q, e).wait_send()
                out_copy(h, q, e).wait_send()


def front(g_lesser, g_greater, onsite, lower, upper, rhs):
    energies = lax.axis_size("energy")
    n, columns = onsite.shape[2], rhs.shape[-1]
    share = n // energies
    vmem = pl.BlockSpec(memory_space=pltpu.VMEM)
    f32 = jnp.float32
    dma = pltpu.SemaphoreType.DMA
    pieces = pltpu.VMEM((energies, 2, share, n), f32)
    return pl.pallas_call(
        front_kernel,
        name="front",
        out_shape=(
            jax.ShapeDtypeStruct((2, n, n), f32),
            jax.ShapeDtypeStruct((2, 2, 2, n, n), f32),
            jax.ShapeDtypeStruct((2, 2, n, columns), f32),
        ),
        in_specs=[vmem] * 6,
        out_specs=(vmem,) * 3,
        scratch_shapes=[
            pltpu.VMEM((2, 2, n, n), f32),
            pieces, pieces, pieces, pieces,
            dma((2, 2, energies)), dma((2, 2, energies)), dma((2, energies)), dma((2, energies)),
            dma((3,)), dma((3,)), dma((3,)), dma((3,)),
            dma((2, 2)), dma((2, 2)), dma((2,)),
        ],
        compiler_params=pltpu.CompilerParams(collective_id=0, has_side_effects=True),
    )(g_lesser, g_greater, onsite, lower, upper, rhs)


def halves(x):
    high = x.astype(jnp.bfloat16)
    return high, (x - high.astype(jnp.float32)).astype(jnp.bfloat16)


def factor(a):
    return halves(a[0]), halves(a[1]), halves(a[0] + a[1])


def three_pass(a, b):
    dot = lambda u, v: jnp.dot(u, v, preferred_element_type=jnp.float32)
    return dot(a[0], b[0]) + (dot(a[0], b[1]) + dot(a[1], b[0]))


def times(a, b):
    first, second, third = (three_pass(a[k], b[k]) for k in range(3))
    return first - second, third - first - second


def inverse_of(matrix):
    eye_rows = lax.broadcasted_iota(jnp.int32, matrix[0].shape, 0)
    eye_columns = lax.broadcasted_iota(jnp.int32, matrix[0].shape, 1)
    eye = jnp.where(eye_rows == eye_columns, 1.0, 0.0)
    scale = 1.0 / diagonal_guess
    b = eye - matrix[0] * scale, -matrix[1] * scale
    fb = factor(b)
    square = times(fb, fb)
    cube = times(fb, factor(square))
    return (eye + b[0] + square[0] + cube[0]) * scale, (b[1] + square[1] + cube[1]) * scale


def rounded_product(a, b):
    dot = lambda u, v: jnp.dot(u, v, preferred_element_type=jnp.float32)
    first, second, third = (dot(a[k], b[k]) for k in range(3))
    return first - second, third - first - second


def rounded(a):
    return tuple(v.astype(jnp.bfloat16) for v in (a[0], a[1], a[0] + a[1]))


def unit_of(matrix):
    rows = lax.broadcasted_iota(jnp.int32, matrix[0].shape, 0)
    columns = lax.broadcasted_iota(jnp.int32, matrix[0].shape, 1)
    return jnp.where(rows == columns, 1.0, 0.0)


def remainder_of(matrix):
    return unit_of(matrix) - matrix[0] * (1.0 / diagonal_guess), -matrix[1] * (1.0 / diagonal_guess)


def lean_inverse(matrix, shift=0.0):
    eye, b = unit_of(matrix), remainder_of(matrix)
    scale = 1.0 / diagonal_guess
    c = b[0] - shift * eye, b[1]
    split = factor(c)
    square = times(split, split)
    cube = rounded_product(tuple(v[0] for v in split), rounded(square))
    zero, one, two = 1 + shift + shift**2 + shift**3, 1 + 2 * shift + 3 * shift**2, 1 + 3 * shift
    return (
        (zero * eye + one * c[0] + two * square[0] + cube[0]) * scale,
        (one * c[1] + two * square[1] + cube[1]) * scale,
    )


def stacked(a, b):
    return tuple(tuple(jnp.concatenate([a[k][j], b[k][j]], axis=0) for j in (0, 1)) for k in range(3))


def apply(a, b):
    columns = b[0].shape[1]
    w = halves(jnp.concatenate([b[0], b[1]], axis=1))
    p, q = three_pass(a[0], w), three_pass(a[1], w)
    return p[:, :columns] - q[:, columns:], p[:, columns:] + q[:, :columns]


def line_kernel(
    gl, gg, onsite, lower, upper, rhs, out,
    gl2, gg2, on2, zin_h, res_h, pin_h, zin_a, res_a, pin_a, zin_b, res_b, pin_b, dpair, diag, src, lu, dp, fp, sp, value,
    z_send, z_recv_h, p_send, p_recv_h, z_recv_a, p_recv_a, z_recv_b, p_recv_b, pair_send, pair_recv, pair_local,
    d_send, d_recv, d_local, dm_send, dm_recv, t_send, t_recv,
    s_send, s_recv, s_local, sm_send, sm_recv,
    l_send, l_recv, l_local, lm_send, lm_recv, out_sem, edge_diag, edge_src, e_sem, flu,
):
    e, i = lax.axis_index("energy"), lax.axis_index("block")
    energies, count = lax.axis_size("energy"), lax.axis_size("block")
    n = diag.shape[-1]
    half = n // 2
    many, r = zin_a.shape[0], zin_a.shape[3]
    few, fine = zin_b.shape[0], zin_b.shape[3]
    edge, end = few * fine, few + many
    starts = [k * fine for k in range(few)] + [edge + k * r for k in range(many)]
    starts += [half - edge + k * fine for k in range(few + 1)]
    segments = (
        (0, fine, 0, zin_h, res_h, pin_h, z_recv_h, p_recv_h),
        (1, r, edge, zin_a, res_a, pin_a, z_recv_a, p_recv_a),
        (2, fine, half - edge, zin_b, res_b, pin_b, z_recv_b, p_recv_b),
    )
    mid = energies // 2
    z, h = e // 2, lax.rem(e, 2)
    y, x = i // 2, lax.rem(i, 2)
    sib, xn, yn = e + 1 - 2 * h, i + 1 - 2 * x, i + 2 - 4 * y
    dn = yn + 1 - 2 * x
    outer, inner, center, far = z == 0, z == 1, z == 2, z == 3
    before = z < 2
    mine = pl.ds(pl.multiple_of(h * half, half), half)
    other = pl.ds(pl.multiple_of((1 - h) * half, half), half)
    scale = 1.0 / math.sqrt(energies)

    def remote(a, b, send, recv, energy=e, block=i):
        return pltpu.make_async_remote_copy(
            src_ref=a, dst_ref=b, send_sem=send, recv_sem=recv,
            device_id={"energy": energy, "block": block}, device_id_type=MESH,
        )

    barrier = pltpu.get_barrier_semaphore()
    for k in range(1, energies):
        pl.semaphore_signal(barrier, inc=1, device_id={"energy": lax.rem(e + k, energies)}, device_id_type=MESH)
    for block in (xn, yn):
        for c in (0, 1):
            pl.semaphore_signal(
                barrier, inc=1, device_id={"energy": 2 * z + c, "block": block}, device_id_type=MESH
            )
    pair_own = []
    for k, (a, b) in enumerate(((gg, gg2), (gl, gl2), (onsite, on2))):
        pair_own.append(pltpu.make_async_copy(a.at[:, 0, mine], b.at[h], pair_local.at[k]))
        pair_own[-1].start()
    pl.semaphore_wait(barrier, energies + 3)

    def valid(j, w):
        return j > 0 if w == 0 else j < count - 1

    coupling = (lower, upper)
    for w in (0, 1):

        @pl.when(valid(i, w))
        def _(w=w):
            remote(coupling[w].at[:, mine], lu.at[i, w, :, mine], l_send.at[0, w], l_recv.at[0, w], block=xn).start()
            remote(coupling[w].at[:, mine], lu.at[i, w, :, mine], l_send.at[1, w], l_recv.at[1, w], block=yn).start()
            pltpu.make_async_copy(coupling[w], lu.at[i, w], l_local.at[w]).start()

    def rows_of(g):
        return pl.ds(g * half, half)

    @pl.when(y == h)
    def _():
        pltpu.make_async_copy(rhs.at[:, 0], src.at[i], s_local).start()
        remote(rhs.at[:, 0], src.at[i], sm_send.at[0], sm_recv.at[0], energy=sib).start()
        for g in (0, 1):
            remote(
                rhs.at[:, 0, rows_of(g)], src.at[i, :, rows_of(g)], s_send.at[0], s_recv.at[0],
                energy=2 * z + g, block=xn,
            ).start()

    @pl.when(y != h)
    def _():
        for g in (0, 1):
            remote(
                rhs.at[:, 0, rows_of(g)], src.at[i, :, rows_of(g)], s_send.at[0], s_recv.at[1],
                energy=2 * z + g, block=yn,
            ).start()

    def z_copies(seg, k, which):
        _, size, base, zin, _, _, z_recv, _ = seg

        def to(a, slot, g, target, sem):
            piece = a.at[:, 0, pl.ds(pl.multiple_of(g * half + base + k * size, 8), size)]
            return remote(piece, zin.at[k, slot], z_send.at[sem], z_recv.at[k], energy=target + g)

        for g in (0, 1):
            if seg[0] == 0:
                if which == 0:
                    to(gg, e, g, mid - 2, 1).start()
                elif which == 2:
                    to(gl, e - mid + 2, g, mid - 2, 1).start()
                    to(gg, e - mid + 4, g, mid - 2, 0).start()
                elif which == 3:
                    to(gl, e - mid + 4, g, mid - 2, 1).start()
                    to(gg, e - mid + 6, g, mid - 2, 0).start()
            elif which == 0:
                to(gg, e, g, mid, 0).start()
                to(gg, e, g, mid - 2, 1).start()
            elif which == 1:
                to(gg, e, g, mid, 0).start()
            else:
                to(gl, e - mid + 2, g, mid, 1).start()
                to(gg, e - mid + 4, g, mid, 0).start()

    for which, role in ((0, outer), (1, inner), (2, center), (3, far)):

        @pl.when(role)
        def _(which=which):
            for seg, steps in zip(segments, (few, many, few)):
                if which == (1 if seg[0] == 0 else 2):
                    continue

                def body(k, carry, seg=seg):
                    z_copies(seg, k, which)
                    return carry

                lax.fori_loop(0, steps, body, 0)

    pairs = []
    for k, (a, b) in enumerate(((gg, gg2), (gl, gl2), (onsite, on2))):
        pairs.append(remote(a.at[:, 0, other], b.at[h], pair_send.at[k], pair_recv.at[k], energy=sib))
        pairs[-1].start()

    def arrived(ref, sem):
        remote(ref, ref, sem, sem).wait_recv()

    def sent(ref, sem):
        remote(ref, ref, sem, sem).wait_send()

    def lu_direct_x(w):
        @pl.when(valid(xn, w))
        def _():
            part = lu.at[xn, w, :, mine]
            arrived(part, l_recv.at[0, w])
            remote(part, part, l_send.at[2, w], l_recv.at[2, w], block=yn).start()
            remote(part, part, lm_send.at[0, w], lm_recv.at[0, w], energy=sib).start()

    def lu_direct_y(w):
        @pl.when(valid(yn, w))
        def _():
            part = lu.at[yn, w, :, mine]
            arrived(part, l_recv.at[1, w])
            remote(part, part, lm_send.at[1, w], lm_recv.at[1, w], energy=sib).start()

    def lu_passed(w):
        @pl.when(valid(dn, w))
        def _():
            part = lu.at[dn, w, :, mine]
            arrived(part, l_recv.at[2, w])
            remote(part, part, lm_send.at[2, w], lm_recv.at[2, w], energy=sib).start()

    def src_direct():
        part = src.at[yn, :, mine]
        arrived(part, s_recv.at[1])
        remote(part, part, s_send.at[1], s_recv.at[2], block=xn).start()
        remote(part, part, sm_send.at[2], sm_recv.at[2], energy=sib).start()
        part = src.at[xn, :, mine]
        arrived(part, s_recv.at[0])
        remote(part, part, sm_send.at[1], sm_recv.at[1], energy=sib).start()

    def src_passed():
        part = src.at[dn, :, mine]
        arrived(part, s_recv.at[2])
        remote(part, part, sm_send.at[3], sm_recv.at[3], energy=sib).start()

    for copy in pair_own:
        copy.wait()
    for copy in pairs:
        copy.wait_recv()

    def tiles(seg, k):
        size, base = seg[1], seg[2]
        for q in range(size // 8):
            for lane in range(n // 128):
                cols = slice(lane * 128, lane * 128 + 128)
                yield slice(q * 8, q * 8 + 8), pl.ds(pl.multiple_of(base + k * size + q * 8, 8), 8), cols

    def correlate(left, right, w):
        real = imag = None
        for k in left:
            if k - w in right:
                (a, b), (u, v) = left[k], right[k - w]
                s, t = a * u - b * v, a * v + b * u
                real, imag = (s, t) if real is None else (real + s, imag + t)
        return real, imag

    def p_copy(seg, k, part, slot, target, sem=None):
        where, _, _, _, res, pin, _, p_recv = seg
        sem = part if sem is None else sem
        return remote(
            res.at[k, pl.ds(2 * part, 2)], pin.at[k, pl.ds(slot, 2)], p_send.at[where, sem], p_recv.at[k],
            energy=target + h,
        )

    def ahead(seg, k):
        _, _, _, zin, res, _, z_recv, _ = seg

        @pl.when(inner)
        def _():
            arrived(zin.at[k, pl.ds(0, 2)], z_recv.at[k])
            for here, rows, cols in tiles(seg, k):
                both = lambda ref, *at: (ref[(*at, 0, here, cols)], ref[(*at, 1, here, cols)])
                pair = lambda ref, c: (ref[c, 0, rows, cols], ref[c, 1, rows, cols])
                left = {2: pair(gl2, 0), 3: pair(gl2, 1)}
                right = {0: both(zin, k, 0), 1: both(zin, k, 1), 2: pair(gg2, 0), 3: pair(gg2, 1)}
                for w in range(mid):
                    value = correlate(left, right, w)
                    for m in (0, 1):
                        res[k, w, m, here, cols] = value[m]
            p_copy(seg, k, 0, 2, 0).start()

    def polarize_first(k):
        seg = segments[0]
        _, _, _, zin, res, pin, z_recv, p_recv = seg

        @pl.when(inner)
        def _():
            arrived(zin.at[k], z_recv.at[k])
            for here, rows, cols in tiles(seg, k):
                both = lambda c: (zin[k, c, 0, here, cols], zin[k, c, 1, here, cols])
                pair = lambda ref, c: (ref[c, 0, rows, cols], ref[c, 1, rows, cols])
                left = {2: pair(gl2, 0), 3: pair(gl2, 1)}
                right = {0: both(0), 1: both(1), 2: pair(gg2, 0), 3: pair(gg2, 1)}
                for c in (0, 1):
                    left.update({mid + c: both(2 + c), mid + 2 + c: both(6 + c)})
                    right.update({mid + c: both(4 + c), mid + 2 + c: both(8 + c)})
                for w in range(energies):
                    value = correlate(left, right, w)
                    for m in (0, 1):
                        if w in (2, 3):
                            dpair[w - 2, m, rows, cols] = on2[w - 2, m, rows, cols] - value[m] * scale
                        else:
                            res[k, w if w < 2 else w - 2, m, here, cols] = value[m]
            for part, target in enumerate((0, mid, mid + 2)):
                p_copy(seg, k, part, 0, target).start()

        @pl.when(jnp.logical_not(inner))
        def _():
            arrived(pin.at[k, pl.ds(0, 2)], p_recv.at[k])

        @pl.when(outer)
        def _():
            for here, rows, cols in tiles(seg, k):
                pair = lambda ref, c: (ref[c, 0, rows, cols], ref[c, 1, rows, cols])
                left = {0: pair(gl2, 0), 1: pair(gl2, 1)}
                right = {0: pair(gg2, 0), 1: pair(gg2, 1)}
                for c in (0, 1):
                    value = correlate(left, right, c)
                    for m in (0, 1):
                        total = value[m] + pin[k, c, m, here, cols]
                        dpair[c, m, rows, cols] = on2[c, m, rows, cols] - total * scale

        @pl.when(z >= 2)
        def _():
            for here, rows, cols in tiles(seg, k):
                for c in (0, 1):
                    for m in (0, 1):
                        dpair[c, m, rows, cols] = on2[c, m, rows, cols] - pin[k, c, m, here, cols] * scale

    def polarize(seg, k):
        _, _, _, zin, res, pin, z_recv, p_recv = seg

        @pl.when(center)
        def _():
            arrived(zin.at[k], z_recv.at[k])
            for here, rows, cols in tiles(seg, k):
                both = lambda ref, *at: (ref[(*at, 0, here, cols)], ref[(*at, 1, here, cols)])
                pair = lambda ref, c: (ref[c, 0, rows, cols], ref[c, 1, rows, cols])
                left = {mid: pair(gl2, 0), mid + 1: pair(gl2, 1), mid + 2: both(zin, k, 4), mid + 3: both(zin, k, 5)}
                right = {c: both(zin, k, c) for c in range(4)}
                right.update({mid: pair(gg2, 0), mid + 1: pair(gg2, 1)})
                right.update({mid + 2: both(zin, k, 6), mid + 3: both(zin, k, 7)})
                for w in range(energies):
                    value = correlate(left, right, w)
                    for m in (0, 1):
                        if w in (mid, mid + 1):
                            dpair[w - mid, m, rows, cols] = on2[w - mid, m, rows, cols] - value[m] * scale
                        else:
                            res[k, w if w < mid else w - 2, m, here, cols] = value[m]
            for part, target in enumerate((0, 2, mid + 2)):
                p_copy(seg, k, part, 0, target).start()

        @pl.when(inner)
        def _():
            arrived(pin.at[k, pl.ds(0, 2)], p_recv.at[k])
            for here, rows, cols in tiles(seg, k):
                for c in (0, 1):
                    for m in (0, 1):
                        total = res[k, 2 + c, m, here, cols] + pin[k, c, m, here, cols]
                        dpair[c, m, rows, cols] = on2[c, m, rows, cols] - total * scale

        @pl.when(outer)
        def _():
            arrived(pin.at[k], p_recv.at[k])
            for here, rows, cols in tiles(seg, k):
                pair = lambda ref, c: (ref[c, 0, rows, cols], ref[c, 1, rows, cols])
                left = {0: pair(gl2, 0), 1: pair(gl2, 1)}
                right = {0: pair(gg2, 0), 1: pair(gg2, 1)}
                for c in (0, 1):
                    value = correlate(left, right, c)
                    for m in (0, 1):
                        total = value[m] + (pin[k, c, m, here, cols] + pin[k, 2 + c, m, here, cols])
                        dpair[c, m, rows, cols] = on2[c, m, rows, cols] - total * scale

        @pl.when(far)
        def _():
            arrived(pin.at[k, pl.ds(0, 2)], p_recv.at[k])
            for here, rows, cols in tiles(seg, k):
                for c in (0, 1):
                    for m in (0, 1):
                        dpair[c, m, rows, cols] = on2[c, m, rows, cols] - pin[k, c, m, here, cols] * scale

    def strip(first, last):
        return pl.ds(pl.multiple_of(h * half + starts[first], 8), starts[last] - starts[first])

    def spread(seg, k, at, passed=True):
        size, base = seg[1], seg[2]
        sub = pl.ds(pl.multiple_of(base + k * size, 8), size)
        there = diag.at[i, :, pl.ds(pl.multiple_of(h * half + base + k * size, 8), size)]
        if not passed:
            remote(dpair.at[1 - y, :, sub], there, t_send.at[0], d_recv.at[2, at], block=dn).start()
        remote(dpair.at[1 - y, :, sub], there, d_send.at[1], d_recv.at[1, at], block=yn).start()
        remote(dpair.at[y, :, sub], there, d_send.at[0], d_recv.at[0, at], block=xn).start()
        remote(dpair.at[y, :, sub], there, dm_send.at[0], dm_recv.at[0], energy=sib).start()
        pltpu.make_async_copy(dpair.at[y, :, sub], there, d_local).start()

    def gather_y(first, last, passing=True):
        for k in range(first, last):
            arrived(diag.at[yn, :, strip(k, k + 1)], d_recv.at[1, k])
        part = diag.at[yn, :, strip(first, last)]
        if passing:
            remote(part, part, d_send.at[2], d_recv.at[2, first], block=xn).start()
        remote(part, part, dm_send.at[2], dm_recv.at[2], energy=sib).start()

    def gather_x(first, last):
        for k in range(first, last):
            arrived(diag.at[xn, :, strip(k, k + 1)], d_recv.at[0, k])
        part = diag.at[xn, :, strip(first, last)]
        remote(part, part, dm_send.at[1], dm_recv.at[1], energy=sib).start()

    def gather(first, last):
        gather_y(first, last, passing=False)
        gather_x(first, last)

    def gather_passed(first, last):
        part = diag.at[dn, :, strip(first, last)]
        arrived(part, d_recv.at[2, first])
        remote(part, part, dm_send.at[3], dm_recv.at[3], energy=sib).start()

    def prefactor(k, j, w):
        @pl.when(valid(j, w))
        def _():
            if k is None:
                pltpu.make_async_copy(coupling[w], lu.at[i, w], l_local.at[w]).wait()
            else:
                arrived(lu.at[j, w, :, other], lm_recv.at[k, w])

            def step(block, carry):
                rows = pl.ds(pl.multiple_of(block * 16, 16), 16)
                split = factor((lu[j, w, 0, rows], lu[j, w, 1, rows]))
                for at in range(3):
                    for part in (0, 1):
                        flu[j, w, 2 * at + part, rows] = split[at][part]
                return carry

            lax.fori_loop(0, n // 16, step, 0)

    def gather_first():
        @pl.when(before)
        def _():
            gather_y(0, few)

    plan = {
        0: [lambda: prefactor(None, i, 0)],
        1: [lambda: lu_direct_x(1), lambda: prefactor(None, i, 1)],
        2: [src_direct, lambda: prefactor(0, xn, 0)],
        3: [lambda: lu_direct_y(0), lambda: lu_direct_y(1), lambda: prefactor(0, xn, 1)],
        4: [gather_first, lambda: prefactor(1, yn, 0)],
        5: [lambda: gather_y(2, 5), lambda: prefactor(1, yn, 1)],
    }

    def turn(k, carry):
        @pl.when(k < many - 1)
        def _():
            ahead(segments[1], k + 1)

        @pl.when(k == many - 1)
        def _():
            ahead(segments[2], 0)

        polarize(segments[1], k)
        spread(segments[1], k, few + k)
        for at, work in plan.items():

            @pl.when(k == at)
            def _(work=work):
                for step in work:
                    step()

        return carry

    @pl.when(before)
    def _():
        for k in range(few):
            polarize_first(k)
            spread(segments[0], k, k)

    ahead(segments[1], 0)
    lu_direct_x(0)
    lax.fori_loop(0, many, turn, 0)
    ahead(segments[2], 1)
    polarize(segments[2], 0)
    spread(segments[2], 0, end, passed=False)
    gather_y(5, 6)
    polarize(segments[2], 1)
    spread(segments[2], 1, end + 1, passed=False)
    gather_y(6, 8)

    @pl.when(z >= 2)
    def _():
        for k in range(few):
            polarize_first(k)
            spread(segments[0], k, k, passed=False)

    gather_x(2, 8)
    src_passed()
    lu_passed(0)
    lu_passed(1)

    @pl.when(before)
    def _():
        gather_x(0, few)
        gather_passed(0, few)

    gather_passed(2, 5)
    gather_passed(5, 6)
    prefactor(2, dn, 0)
    prefactor(2, dn, 1)
    for k in (end, end + 1):
        gather(k, k + 1)
        gather_passed(k, k + 1)
    gather_passed(6, 8)

    @pl.when(z >= 2)
    def _():
        for k in range(few):
            gather(k, k + 1)
            gather_passed(k, k + 1)


    pltpu.make_async_copy(dpair.at[y], diag.at[i, :, mine], d_local).wait()
    for k, j in enumerate((i, xn, yn, dn)):
        arrived(diag.at[j, :, other], dm_recv.at[k])

    @pl.when(y == h)
    def _():
        pltpu.make_async_copy(rhs.at[:, 0], src.at[i], s_local).wait()

    @pl.when(y != h)
    def _():
        arrived(src.at[i], sm_recv.at[0])

    for k, j in enumerate((xn, yn, dn)):
        arrived(src.at[j, :, other], sm_recv.at[k + 1])

    a, b, m, q = 3 * x, 2 - x, 1 + x, 3 - 3 * x
    couple = lambda j, w: tuple((flu[j, w, 2 * k], flu[j, w, 2 * k + 1]) for k in range(3))
    diagonal = lambda j: (diag[j, 0], diag[j, 1])
    source = lambda j: (src[j, 0], src[j, 1])

    def put(ref, at, v):
        ref[at, 0], ref[at, 1] = v

    edge_d = []
    for k in (0, 1):
        part = edge_diag.at[:, pl.ds(k * half, half)]
        edge_d.append(remote(part, part, e_sem.at[2 * k], e_sem.at[2 * k + 1], energy=sib))
    edge_s = remote(edge_src, edge_src, e_sem.at[4], e_sem.at[5], energy=sib)

    @pl.when(h == y)
    def _():
        t = factor(times(couple(b, 1 - x), factor(lean_inverse(diagonal(q), -0.2))))
        for k in (0, 1):
            rows = slice(k * half, (k + 1) * half)
            v = times(tuple(tuple(u[rows] for u in w) for w in t), couple(q, x))
            edge_diag[0, rows], edge_diag[1, rows] = v
            edge_d[k].start()
        edge_src[0], edge_src[1] = apply(t, source(q))
        edge_s.start()

    inv = factor(lean_inverse(diagonal(m), -0.2))
    t = factor(times(stacked(couple(a, 1 - x), couple(b, x)), inv))
    top, low = (lambda v: (v[0][:n], v[1][:n])), (lambda v: (v[0][n:], v[1][n:]))
    v = times(t, couple(m, x))
    put(dp, 0, minus(diagonal(a), top(v)))
    put(fp, 1, low(v))
    v = times(t, couple(m, 1 - x))
    put(dp, 1, minus(diagonal(b), low(v)))
    put(fp, 0, top(v))
    v = apply(t, source(m))
    put(sp, 0, minus(source(a), top(v)))
    put(sp, 1, minus(source(b), low(v)))

    def add_edge():
        @pl.when(h != y)
        def _():
            for copy in edge_d:
                copy.wait_recv()

        for k in (0, 1):
            dp[1, k] = dp[1, k] - edge_diag[k]

    this = jnp.where(h == x, 0, 1)

    @pl.when(h == x)
    def _():
        add_edge()

    that = 1 - this
    at = lambda ref, k: (ref[k, 0], ref[k, 1])
    t = factor(times(factor(at(fp, this)), factor(lean_inverse(at(dp, that)))))
    v = times(t, factor(at(fp, that)))

    @pl.when(h != x)
    def _():
        add_edge()

    @pl.when(h != y)
    def _():
        edge_s.wait_recv()

    for k in (0, 1):
        sp[1, k] = sp[1, k] - edge_src[k]
    last = minus(at(dp, this), v)
    right = plus(at(sp, this), apply(t, at(sp, that)))
    rest = factor(remainder_of(last))
    inverse_guess = 1.0 / diagonal_guess
    found = right
    for _ in range(3):
        found = plus(right, apply(rest, found))
    value[0], value[1] = found[0] * inverse_guess, found[1] * inverse_guess

    home = remote(value, out.at[:, 0], out_sem.at[0], out_sem.at[1], energy=2 * z + y, block=2 * h + x)
    keep = pltpu.make_async_copy(value, out.at[:, 0], out_sem.at[0])

    @pl.when(h != y)
    def _():
        home.start()

    @pl.when(h == y)
    def _():
        keep.start()
        keep.wait()

    whole_array, most = gg.at[:, 0], gg.at[:, 0, pl.ds(0, n - 2 * edge)]
    rest_of = gg.at[:, 0, pl.ds(0, 2 * edge)]

    def p_sent(seg, parts):
        for k in range(parts):
            sent(seg[4].at[:, pl.ds(2 * k, 2)], p_send.at[seg[0], k])

    @pl.when(outer)
    def _():
        sent(most, z_send.at[0])
        sent(whole_array, z_send.at[1])

    @pl.when(inner)
    def _():
        sent(most, z_send.at[0])
        for seg, parts in zip(segments, (3, 1, 1)):
            p_sent(seg, parts)

    @pl.when(center)
    def _():
        sent(rest_of, z_send.at[0])
        sent(rest_of, z_send.at[1])
        for seg in segments[1:]:
            p_sent(seg, 3)

    @pl.when(far)
    def _():
        sent(whole_array, z_send.at[0])
        sent(whole_array, z_send.at[1])

    for copy in pairs:
        copy.wait_send()
    for k in range(2):
        sent(dpair.at[0], d_send.at[k])

    @pl.when(before)
    def _():
        sent(dpair.at[0, :, pl.ds(0, half - edge)], d_send.at[2])
        sent(dpair.at[0, :, pl.ds(0, edge)], t_send.at[0])

    @pl.when(z >= 2)
    def _():
        sent(dpair.at[0, :, pl.ds(0, half - 2 * edge)], d_send.at[2])
        sent(dpair.at[0, :, pl.ds(0, 2 * edge)], t_send.at[0])

    for k in range(4):
        sent(dpair.at[0], dm_send.at[k])
    part = src.at[0, :, mine]

    @pl.when(y == h)
    def _():
        sent(rhs.at[:, 0], sm_send.at[0])

    sent(rhs.at[:, 0], s_send.at[0])
    sent(part, s_send.at[1])
    for k in range(3):
        sent(part, sm_send.at[k + 1])
    for w in (0, 1):
        part = lu.at[0, w, :, mine]

        @pl.when(valid(i, w))
        def _(w=w, part=part):
            sent(part, l_send.at[0, w])
            sent(part, l_send.at[1, w])

        for k, j in enumerate((xn, yn, dn)):

            @pl.when(valid(j, w))
            def _(k=k, w=w, part=part):
                if k == 0:
                    sent(part, l_send.at[2, w])
                sent(part, lm_send.at[k, w])

    @pl.when(h == y)
    def _():
        for copy in (*edge_d, edge_s):
            copy.wait_send()

    @pl.when(h != y)
    def _():
        home.wait()


def line(g_lesser, g_greater, onsite, lower, upper, rhs):
    count = lax.axis_size("block")
    n, columns = onsite.shape[2], rhs.shape[-1]
    half = n // 2
    r = half // 8
    many, few, fine = 6, 2, r // 2
    f32 = jnp.float32
    dma = pltpu.SemaphoreType.DMA
    anywhere = pl.BlockSpec(memory_space=pl.ANY)
    pair = pltpu.VMEM((2, 2, half, n), f32)
    return pl.pallas_call(
        line_kernel,
        name="line",
        out_shape=pltpu.VMEM((2, 1, n, columns), f32),
        in_specs=[anywhere] * 6,
        out_specs=anywhere,
        scratch_shapes=[
            pair, pair, pair,
            pltpu.VMEM((few, 10, 2, fine, n), f32),
            pltpu.VMEM((few, 6, 2, fine, n), f32),
            pltpu.VMEM((few, 4, 2, fine, n), f32),
            pltpu.VMEM((many, 8, 2, r, n), f32),
            pltpu.VMEM((many, 6, 2, r, n), f32),
            pltpu.VMEM((many, 4, 2, r, n), f32),
            pltpu.VMEM((few, 8, 2, fine, n), f32),
            pltpu.VMEM((few, 6, 2, fine, n), f32),
            pltpu.VMEM((few, 4, 2, fine, n), f32),
            pair,
            pltpu.VMEM((count, 2, n, n), f32),
            pltpu.VMEM((count, 2, n, columns), f32),
            pltpu.VMEM((count, 2, 2, n, n), f32),
            pltpu.VMEM((2, 2, n, n), f32),
            pltpu.VMEM((2, 2, n, n), f32),
            pltpu.VMEM((2, 2, n, columns), f32),
            pltpu.VMEM((2, n, columns), f32),
            dma((2,)), dma((few,)), dma((3, 3)), dma((few,)), dma((many,)), dma((many,)), dma((few,)), dma((few,)),
            dma((3,)), dma((3,)), dma((3,)),
            dma((3,)), dma((3, many + 2 * few)), dma, dma((4,)), dma((4,)), dma((1,)), dma((1,)),
            dma((2,)), dma((3,)), dma, dma((4,)), dma((4,)),
            dma((3, 2)), dma((3, 2)), dma((2,)), dma((3, 2)), dma((3, 2)), dma((2,)),
            pltpu.VMEM((2, n, n), f32), pltpu.VMEM((2, n, columns), f32), dma((6,)),
            pltpu.VMEM((count, 2, 6, n, n), jnp.bfloat16),
        ],
        compiler_params=pltpu.CompilerParams(
            collective_id=1, has_side_effects=True, vmem_limit_bytes=60 * 1024 * 1024
        ),
    )(g_lesser, g_greater, onsite, lower, upper, rhs)


def shifted(value, steps):
    count = lax.axis_size("block")
    leading, last = max(0, -steps), min(count, count - steps)
    pairs = [(k, k + steps) for k in range(leading, last)]
    return lax.ppermute(value, "block", pairs)


def shards(g_lesser, g_greater, onsite, lower, upper, rhs):
    index = lax.axis_index("block")
    count = lax.axis_size("block")
    levels = count.bit_length() - 1
    n = onsite.shape[-1]
    both = jnp.concatenate(
        [jnp.where(index > 0, lower, 0.0), jnp.where(index < count - 1, upper, 0.0)], axis=-1
    )
    if levels == 2 and lax.axis_size("energy") == 8:
        return line(g_lesser, g_greater, onsite, lower, upper, rhs)
    diag, near_lu, near_s = front(g_lesser, g_greater, onsite, lower, upper, rhs)
    diag = parts(diag)
    first, final = index < 2, index >= count - 2
    low, up = cut(parts(both), 0, n), cut(parts(both), n, 2 * n)
    source = parts(rhs[:, 0])
    for depth in range(levels):
        stride = 1 << depth
        inv = inverse(diag)
        if depth == levels - 1:
            coupling = tuple(jnp.where(index < stride, up[k], low[k]) for k in (0, 1))
            sent = product(inv, wide(coupling, source))
            swap = [(k, k ^ stride) for k in range(count)]
            got = parts(lax.ppermute(jnp.stack(sent), "block", swap))
            change = product(coupling, got)
            diag = minus(diag, cut(change, 0, n))
            source = minus(source, cut(change, n, None))
        elif depth == 0:
            packed = jnp.stack(inv)
            inv_left, inv_right = parts(shifted(packed, 1)), parts(shifted(packed, -1))
            t, w = product(low, inv_left), product(up, inv_right)
            lu_l, lu_r = near_lu[0], near_lu[1]
            change = product(t, wide(parts(lu_l[0]), parts(lu_l[1]), parts(near_s[0])))
            other = product(w, wide(parts(lu_r[0]), parts(lu_r[1]), parts(near_s[1])))
            change = tuple(jnp.where(index > 0, v, 0.0) for v in change)
            other = tuple(jnp.where(index < count - 1, v, 0.0) for v in other)
            diag = minus(minus(diag, cut(change, n, 2 * n)), cut(other, 0, n))
            source = minus(minus(source, cut(change, 2 * n, None)), cut(other, 2 * n, None))
            low = tuple(jnp.where(first, 0.0, -v) for v in cut(change, 0, n))
            up = tuple(jnp.where(final, 0.0, -v) for v in cut(other, n, 2 * n))
        else:
            sent = jnp.stack(product(inv, wide(low, up, source)))
            left, right = parts(shifted(sent, stride)), parts(shifted(sent, -stride))
            change, other = product(low, left), product(up, right)
            diag = minus(minus(diag, cut(change, n, 2 * n)), cut(other, 0, n))
            source = minus(minus(source, cut(change, 2 * n, None)), cut(other, 2 * n, None))
            low = tuple(-v for v in cut(change, 0, n))
            up = tuple(-v for v in cut(other, n, 2 * n))
    return jnp.stack(solve(diag, source))[:, None]


def solution(mesh):
    placed = (
        P(None, "energy", "block", None),
        P(None, "energy", "block", None),
        P(None, "energy", "block", None),
        P(None, "block", None),
        P(None, "block", None),
        P(None, "energy", "block", None),
    )
    return jax.shard_map(
        shards,
        mesh=mesh,
        in_specs=placed,
        out_specs=P(None, "energy", "block", None),
        check_vma=False,
    )
```

```python
import math

import jax
import jax.numpy as jnp
from jax import lax
from jax.experimental import pallas as pl
from jax.experimental.pallas import tpu as pltpu
from jax.sharding import PartitionSpec as P

diagonal_guess = 5.0
MODE = lax.Precision.HIGH
MESH = pl.DeviceIdType.MESH


def real_product(a, b):
    return jnp.matmul(a, b, precision=MODE)


def product(a, b):
    ar, ai = a
    br, bi = b
    return (
        real_product(ar, br) - real_product(ai, bi),
        real_product(ar, bi) + real_product(ai, br),
    )


def parts(a):
    return a[0], a[1]


def plus(a, b):
    return a[0] + b[0], a[1] + b[1]


def minus(a, b):
    return a[0] - b[0], a[1] - b[1]


def wide(*pieces):
    return tuple(jnp.concatenate([p[k] for p in pieces], axis=-1) for k in (0, 1))


def cut(a, start, stop):
    return a[0][:, start:stop], a[1][:, start:stop]


def remainder(matrix):
    eye = jnp.eye(matrix[0].shape[-1], dtype=jnp.float32)
    return eye - matrix[0] * (1.0 / diagonal_guess), -matrix[1] * (1.0 / diagonal_guess)


def inverse(matrix):
    eye = jnp.eye(matrix[0].shape[-1], dtype=jnp.float32)
    b = remainder(matrix)
    square = product(b, b)
    cube = product(b, square)
    scale = 1.0 / diagonal_guess
    return (eye + b[0] + square[0] + cube[0]) * scale, (b[1] + square[1] + cube[1]) * scale


def solve(matrix, source):
    b = remainder(matrix)
    value = source
    for _ in range(3):
        value = plus(source, product(b, value))
    scale = 1.0 / diagonal_guess
    return value[0] * scale, value[1] * scale


def front_kernel(
    gl, gg, onsite, lower, upper, rhs, diag, near_lu, near_s,
    lu, gl_all, gg_all, res, pol,
    in_send, in_recv, out_send, out_recv, lu_send, lu_recv, hop_send, hop_recv,
    mate_send, mate_recv, local, rows_out=None, partner=None,
):
    e, i = lax.axis_index("energy"), lax.axis_index("block")
    energies, count = lax.axis_size("energy"), lax.axis_size("block")
    share = gl.shape[2] // energies
    c, p = lax.rem(e, 2), lax.rem(i, 2)
    mate, side = e + 1 - 2 * c, 1 - p
    pair, onward, behind = i + 1 - 2 * p, i + 2 - 4 * p, i - 2 + 4 * p
    has_onward = jnp.logical_and(onward >= 0, onward < count)
    has_behind = jnp.logical_and(behind >= 0, behind < count)

    fill = [pltpu.make_async_copy((lower, upper)[k], lu.at[k], local.at[k]) for k in (0, 1)]
    for copy in fill:
        copy.start()
    barrier = pltpu.get_barrier_semaphore()
    for k in range(1, energies):
        pl.semaphore_signal(barrier, inc=1, device_id={"energy": lax.rem(e + k, energies)}, device_id_type=MESH)
    pl.semaphore_signal(barrier, inc=1, device_id={"block": pair}, device_id_type=MESH)

    @pl.when(has_onward)
    def _():
        pl.semaphore_signal(barrier, inc=1, device_id={"block": onward}, device_id_type=MESH)

    @pl.when(has_behind)
    def _():
        pl.semaphore_signal(barrier, inc=1, device_id={"block": behind}, device_id_type=MESH)

    peers = energies
    if partner is not None:
        peers = energies + 1
        pl.semaphore_signal(barrier, inc=1, device_id={"block": partner}, device_id_type=MESH)
    pl.semaphore_wait(barrier, peers + has_onward.astype(jnp.int32) + has_behind.astype(jnp.int32))

    def remote(src, dst, send, recv, **where):
        return pltpu.make_async_remote_copy(
            src_ref=src, dst_ref=dst, send_sem=send, recv_sem=recv, device_id=where, device_id_type=MESH
        )

    part = share // 2

    def in_copy(h, k, q, source):
        src, dst = ((gl, gl_all), (gg, gg_all))[k]
        rows = src.at[:, 0, pl.ds(q * share + h * part, part), :]
        there = dst.at[source, :, pl.ds(h * part, part), :]
        return remote(rows, there, in_send.at[h, k, q], in_recv.at[h, k, source], energy=q)

    def out_copy(h, w, source):
        rows = pl.ds(h * part, part)
        return remote(
            res.at[w, :, rows, :], pol.at[source, :, rows, :], out_send.at[h, w], out_recv.at[h, source], energy=w
        )

    for copy in fill:
        copy.wait()
    for h in (0, 1):
        for k in (0, 1):
            for q in range(energies):

                @pl.when(q != e)
                def _():
                    in_copy(h, k, q, e).start()

    own = []
    for k, (src, dst) in enumerate(((gl, gl_all), (gg, gg_all))):
        rows = src.at[:, 0, pl.ds(pl.multiple_of(e * share, 8), share), :]
        own.append(pltpu.make_async_copy(rows, dst.at[e], local.at[k]))
        own[-1].start()

    mine = (lu.at[c, 0], lu.at[c, 1], rhs.at[:, 0])

    def slot(s, k):
        return near_s.at[s] if k == 2 else near_lu.at[s, c, k]

    direct = [remote(mine[k], slot(p, k), lu_send.at[k], lu_recv.at[k], block=pair) for k in range(3)]
    hops = [remote(slot(side, k), slot(p, k), hop_send.at[k], hop_recv.at[k], block=onward) for k in range(3)]
    for copy in direct:
        copy.start()
    shared = [
        remote(slot(s, k), slot(s, k), mate_send.at[j, k], mate_recv.at[j, k], energy=mate)
        for j, s in enumerate((side, p))
        for k in (0, 1)
    ]
    for k in range(3):
        direct[k].wait_recv()

        @pl.when(has_onward)
        def _():
            hops[k].start()

        if k < 2:
            shared[k].start()

    for copy in own:
        copy.wait()
    scale = 1.0 / math.sqrt(energies)
    for h in (0, 1):
        for k in (0, 1):
            for q in range(energies):

                @pl.when(q != e)
                def _():
                    in_copy(h, k, q, q).wait_recv()

        for w in range(energies):

            def step(row, carry, w=w, h=h):
                rows = pl.ds(pl.multiple_of(h * part + row * 8, 8), 8)
                real = imag = None
                for k in range(w, energies):
                    a, b = gl_all[k, 0, rows], gl_all[k, 1, rows]
                    x, y = gg_all[k - w, 0, rows], gg_all[k - w, 1, rows]
                    s, t = a * x - b * y, a * y + b * x
                    real, imag = (s, t) if real is None else (real + s, imag + t)
                res[w, 0, rows] = real * scale
                res[w, 1, rows] = imag * scale
                return carry

            lax.fori_loop(0, part // 8, step, 0)

            @pl.when(w != e)
            def _():
                out_copy(h, w, e).start()

    keep = pltpu.make_async_copy(res.at[e], pol.at[e], local.at[0])
    keep.start()

    @pl.when(has_behind)
    def _():
        for k in range(3):
            hops[k].wait_recv()
            if k < 2:
                shared[2 + k].start()

    def hand_on(q):
        rows_out[0][q].wait_recv()

        @pl.when(has_onward)
        def _():
            rows_out[1][q].start()

    keep.wait()
    for q in range(energies):

        @pl.when(q != e)
        def _():
            out_copy(0, q, q).wait_recv()
            out_copy(1, q, q).wait_recv()

        rows = pl.ds(q * share, share)
        for k in (0, 1):
            diag[k, rows] = onsite[k, 0, rows] - pol[q, k]
        if rows_out is not None:
            rows_out[0][q].start()
            if q > 0:
                hand_on(q - 1)
    if rows_out is not None:
        hand_on(energies - 1)

    for k in range(2):
        shared[k].wait_recv()

    @pl.when(has_behind)
    def _():
        for k in range(2):
            shared[2 + k].wait()

    for k in range(2):
        shared[k].wait_send()
    for k in range(3):
        direct[k].wait_send()

        @pl.when(has_onward)
        def _():
            hops[k].wait_send()

    for q in range(energies):

        @pl.when(q != e)
        def _():
            for h in (0, 1):
                in_copy(h, 0, q, e).wait_send()
                in_copy(h, 1, q, e).wait_send()
                out_copy(h, q, e).wait_send()


def front(g_lesser, g_greater, onsite, lower, upper, rhs):
    energies = lax.axis_size("energy")
    n, columns = onsite.shape[2], rhs.shape[-1]
    share = n // energies
    vmem = pl.BlockSpec(memory_space=pltpu.VMEM)
    f32 = jnp.float32
    dma = pltpu.SemaphoreType.DMA
    pieces = pltpu.VMEM((energies, 2, share, n), f32)
    return pl.pallas_call(
        front_kernel,
        name="front",
        out_shape=(
            jax.ShapeDtypeStruct((2, n, n), f32),
            jax.ShapeDtypeStruct((2, 2, 2, n, n), f32),
            jax.ShapeDtypeStruct((2, 2, n, columns), f32),
        ),
        in_specs=[vmem] * 6,
        out_specs=(vmem,) * 3,
        scratch_shapes=[
            pltpu.VMEM((2, 2, n, n), f32),
            pieces, pieces, pieces, pieces,
            dma((2, 2, energies)), dma((2, 2, energies)), dma((2, energies)), dma((2, energies)),
            dma((3,)), dma((3,)), dma((3,)), dma((3,)),
            dma((2, 2)), dma((2, 2)), dma((2,)),
        ],
        compiler_params=pltpu.CompilerParams(collective_id=0, has_side_effects=True),
    )(g_lesser, g_greater, onsite, lower, upper, rhs)


def halves(x):
    high = x.astype(jnp.bfloat16)
    return high, (x - high.astype(jnp.float32)).astype(jnp.bfloat16)


def factor(a):
    return halves(a[0]), halves(a[1]), halves(a[0] + a[1])


def three_pass(a, b):
    dot = lambda u, v: jnp.dot(u, v, preferred_element_type=jnp.float32)
    return dot(a[0], b[0]) + (dot(a[0], b[1]) + dot(a[1], b[0]))


def times(a, b):
    first, second, third = (three_pass(a[k], b[k]) for k in range(3))
    return first - second, third - first - second


def inverse_of(matrix):
    eye_rows = lax.broadcasted_iota(jnp.int32, matrix[0].shape, 0)
    eye_columns = lax.broadcasted_iota(jnp.int32, matrix[0].shape, 1)
    eye = jnp.where(eye_rows == eye_columns, 1.0, 0.0)
    scale = 1.0 / diagonal_guess
    b = eye - matrix[0] * scale, -matrix[1] * scale
    fb = factor(b)
    square = times(fb, fb)
    cube = times(fb, factor(square))
    return (eye + b[0] + square[0] + cube[0]) * scale, (b[1] + square[1] + cube[1]) * scale


def rounded_product(a, b):
    dot = lambda u, v: jnp.dot(u, v, preferred_element_type=jnp.float32)
    first, second, third = (dot(a[k], b[k]) for k in range(3))
    return first - second, third - first - second


def rounded(a):
    return tuple(v.astype(jnp.bfloat16) for v in (a[0], a[1], a[0] + a[1]))


def unit_of(matrix):
    rows = lax.broadcasted_iota(jnp.int32, matrix[0].shape, 0)
    columns = lax.broadcasted_iota(jnp.int32, matrix[0].shape, 1)
    return jnp.where(rows == columns, 1.0, 0.0)


def remainder_of(matrix):
    return unit_of(matrix) - matrix[0] * (1.0 / diagonal_guess), -matrix[1] * (1.0 / diagonal_guess)


def lean_inverse(matrix, shift=0.0):
    eye, b = unit_of(matrix), remainder_of(matrix)
    scale = 1.0 / diagonal_guess
    c = b[0] - shift * eye, b[1]
    split = factor(c)
    square = times(split, split)
    cube = rounded_product(tuple(v[0] for v in split), rounded(square))
    zero, one, two = 1 + shift + shift**2 + shift**3, 1 + 2 * shift + 3 * shift**2, 1 + 3 * shift
    return (
        (zero * eye + one * c[0] + two * square[0] + cube[0]) * scale,
        (one * c[1] + two * square[1] + cube[1]) * scale,
    )


def stacked(a, b):
    return tuple(tuple(jnp.concatenate([a[k][j], b[k][j]], axis=0) for j in (0, 1)) for k in range(3))


def apply(a, b):
    columns = b[0].shape[1]
    w = halves(jnp.concatenate([b[0], b[1]], axis=1))
    p, q = three_pass(a[0], w), three_pass(a[1], w)
    return p[:, :columns] - q[:, columns:], p[:, columns:] + q[:, :columns]


def line_kernel(
    gl, gg, onsite, lower, upper, rhs, out,
    gl2, gg2, on2, zin_h, res_h, pin_h, zin_a, res_a, pin_a, zin_b, res_b, pin_b, dpair, diag, src, lu, dp, fp, sp, value,
    z_send, z_recv_h, p_send, p_recv_h, z_recv_a, p_recv_a, z_recv_b, p_recv_b, pair_send, pair_recv, pair_local,
    d_send, d_recv, d_local, dm_send, dm_recv, t_send, t_recv,
    s_send, s_recv, s_local, sm_send, sm_recv,
    l_send, l_recv, l_local, lm_send, lm_recv, out_sem, edge_diag, edge_src, e_sem, flu,
):
    e, i = lax.axis_index("energy"), lax.axis_index("block")
    energies, count = lax.axis_size("energy"), lax.axis_size("block")
    n = diag.shape[-1]
    half = n // 2
    many, r = zin_a.shape[0], zin_a.shape[3]
    few, fine = zin_b.shape[0], zin_b.shape[3]
    edge, end = few * fine, few + many
    starts = [k * fine for k in range(few)] + [edge + k * r for k in range(many)]
    starts += [half - edge + k * fine for k in range(few + 1)]
    segments = (
        (0, fine, 0, zin_h, res_h, pin_h, z_recv_h, p_recv_h),
        (1, r, edge, zin_a, res_a, pin_a, z_recv_a, p_recv_a),
        (2, fine, half - edge, zin_b, res_b, pin_b, z_recv_b, p_recv_b),
    )
    mid = energies // 2
    z, h = e // 2, lax.rem(e, 2)
    y, x = i // 2, lax.rem(i, 2)
    sib, xn, yn = e + 1 - 2 * h, i + 1 - 2 * x, i + 2 - 4 * y
    dn = yn + 1 - 2 * x
    outer, inner, center, far = z == 0, z == 1, z == 2, z == 3
    before = z < 2
    mine = pl.ds(pl.multiple_of(h * half, half), half)
    other = pl.ds(pl.multiple_of((1 - h) * half, half), half)
    scale = 1.0 / math.sqrt(energies)

    def remote(a, b, send, recv, energy=e, block=i):
        return pltpu.make_async_remote_copy(
            src_ref=a, dst_ref=b, send_sem=send, recv_sem=recv,
            device_id={"energy": energy, "block": block}, device_id_type=MESH,
        )

    barrier = pltpu.get_barrier_semaphore()
    for k in range(1, energies):
        pl.semaphore_signal(barrier, inc=1, device_id={"energy": lax.rem(e + k, energies)}, device_id_type=MESH)
    for block in (xn, yn):
        for c in (0, 1):
            pl.semaphore_signal(
                barrier, inc=1, device_id={"energy": 2 * z + c, "block": block}, device_id_type=MESH
            )
    pair_own = []
    for k, (a, b) in enumerate(((gg, gg2), (gl, gl2), (onsite, on2))):
        pair_own.append(pltpu.make_async_copy(a.at[:, 0, mine], b.at[h], pair_local.at[k]))
        pair_own[-1].start()
    pl.semaphore_wait(barrier, energies + 3)

    def valid(j, w):
        return j > 0 if w == 0 else j < count - 1

    coupling = (lower, upper)
    for w in (0, 1):

        @pl.when(valid(i, w))
        def _(w=w):
            remote(coupling[w].at[:, mine], lu.at[i, w, :, mine], l_send.at[0, w], l_recv.at[0, w], block=xn).start()
            remote(coupling[w].at[:, mine], lu.at[i, w, :, mine], l_send.at[1, w], l_recv.at[1, w], block=yn).start()
            pltpu.make_async_copy(coupling[w], lu.at[i, w], l_local.at[w]).start()

    def rows_of(g):
        return pl.ds(g * half, half)

    @pl.when(y == h)
    def _():
        pltpu.make_async_copy(rhs.at[:, 0], src.at[i], s_local).start()
        remote(rhs.at[:, 0], src.at[i], sm_send.at[0], sm_recv.at[0], energy=sib).start()
        for g in (0, 1):
            remote(
                rhs.at[:, 0, rows_of(g)], src.at[i, :, rows_of(g)], s_send.at[0], s_recv.at[0],
                energy=2 * z + g, block=xn,
            ).start()

    @pl.when(y != h)
    def _():
        for g in (0, 1):
            remote(
                rhs.at[:, 0, rows_of(g)], src.at[i, :, rows_of(g)], s_send.at[0], s_recv.at[1],
                energy=2 * z + g, block=yn,
            ).start()

    def z_copies(seg, k, which):
        _, size, base, zin, _, _, z_recv, _ = seg

        def to(a, slot, g, target, sem):
            piece = a.at[:, 0, pl.ds(pl.multiple_of(g * half + base + k * size, 8), size)]
            return remote(piece, zin.at[k, slot], z_send.at[sem], z_recv.at[k], energy=target + g)

        for g in (0, 1):
            if seg[0] == 0:
                if which == 0:
                    to(gg, e, g, mid - 2, 1).start()
                elif which == 2:
                    to(gl, e - mid + 2, g, mid - 2, 1).start()
                    to(gg, e - mid + 4, g, mid - 2, 0).start()
                elif which == 3:
                    to(gl, e - mid + 4, g, mid - 2, 1).start()
                    to(gg, e - mid + 6, g, mid - 2, 0).start()
            elif which == 0:
                to(gg, e, g, mid, 0).start()
                to(gg, e, g, mid - 2, 1).start()
            elif which == 1:
                to(gg, e, g, mid, 0).start()
            else:
                to(gl, e - mid + 2, g, mid, 1).start()
                to(gg, e - mid + 4, g, mid, 0).start()

    for which, role in ((0, outer), (1, inner), (2, center), (3, far)):

        @pl.when(role)
        def _(which=which):
            for seg, steps in zip(segments, (few, many, few)):
                if (which, seg[0]) in ((1, 0), (1, 2), (2, 1), (2, 2)):
                    continue

                def body(k, carry, seg=seg):
                    z_copies(seg, k, which)
                    return carry

                lax.fori_loop(0, steps, body, 0)

    pairs = []
    for k, (a, b) in enumerate(((gg, gg2), (gl, gl2), (onsite, on2))):
        pairs.append(remote(a.at[:, 0, other], b.at[h], pair_send.at[k], pair_recv.at[k], energy=sib))
        pairs[-1].start()

    def arrived(ref, sem):
        remote(ref, ref, sem, sem).wait_recv()

    def sent(ref, sem):
        remote(ref, ref, sem, sem).wait_send()

    def lu_direct_x(w):
        @pl.when(valid(xn, w))
        def _():
            part = lu.at[xn, w, :, mine]
            arrived(part, l_recv.at[0, w])
            remote(part, part, l_send.at[2, w], l_recv.at[2, w], block=yn).start()
            remote(part, part, lm_send.at[0, w], lm_recv.at[0, w], energy=sib).start()

    def lu_direct_y(w):
        @pl.when(valid(yn, w))
        def _():
            part = lu.at[yn, w, :, mine]
            arrived(part, l_recv.at[1, w])
            remote(part, part, lm_send.at[1, w], lm_recv.at[1, w], energy=sib).start()

    def lu_passed(w):
        @pl.when(valid(dn, w))
        def _():
            part = lu.at[dn, w, :, mine]
            arrived(part, l_recv.at[2, w])
            remote(part, part, lm_send.at[2, w], lm_recv.at[2, w], energy=sib).start()

    def src_direct():
        part = src.at[yn, :, mine]
        arrived(part, s_recv.at[1])
        remote(part, part, s_send.at[1], s_recv.at[2], block=xn).start()
        remote(part, part, sm_send.at[2], sm_recv.at[2], energy=sib).start()
        part = src.at[xn, :, mine]
        arrived(part, s_recv.at[0])
        remote(part, part, sm_send.at[1], sm_recv.at[1], energy=sib).start()

    def src_passed():
        part = src.at[dn, :, mine]
        arrived(part, s_recv.at[2])
        remote(part, part, sm_send.at[3], sm_recv.at[3], energy=sib).start()

    for copy in pair_own:
        copy.wait()
    for copy in pairs:
        copy.wait_recv()

    def tiles(seg, k):
        size, base = seg[1], seg[2]
        for q in range(size // 8):
            for lane in range(n // 128):
                cols = slice(lane * 128, lane * 128 + 128)
                yield slice(q * 8, q * 8 + 8), pl.ds(pl.multiple_of(base + k * size + q * 8, 8), 8), cols

    def correlate(left, right, w):
        real = imag = None
        for k in left:
            if k - w in right:
                (a, b), (u, v) = left[k], right[k - w]
                s, t = a * u - b * v, a * v + b * u
                real, imag = (s, t) if real is None else (real + s, imag + t)
        return real, imag

    def p_copy(seg, k, part, slot, target, sem=None):
        where, _, _, _, res, pin, _, p_recv = seg
        sem = part if sem is None else sem
        return remote(
            res.at[k, pl.ds(2 * part, 2)], pin.at[k, pl.ds(slot, 2)], p_send.at[where, sem], p_recv.at[k],
            energy=target + h,
        )

    def ahead(seg, k):
        _, _, _, zin, res, _, z_recv, _ = seg

        @pl.when(inner)
        def _():
            arrived(zin.at[k, pl.ds(0, 2)], z_recv.at[k])
            for here, rows, cols in tiles(seg, k):
                both = lambda ref, *at: (ref[(*at, 0, here, cols)], ref[(*at, 1, here, cols)])
                pair = lambda ref, c: (ref[c, 0, rows, cols], ref[c, 1, rows, cols])
                left = {2: pair(gl2, 0), 3: pair(gl2, 1)}
                right = {0: both(zin, k, 0), 1: both(zin, k, 1), 2: pair(gg2, 0), 3: pair(gg2, 1)}
                for w in range(mid):
                    value = correlate(left, right, w)
                    for m in (0, 1):
                        res[k, w, m, here, cols] = value[m]
            p_copy(seg, k, 0, 2, 0).start()

    def polarize_first(k):
        seg = segments[0]
        _, _, _, zin, res, pin, z_recv, p_recv = seg

        @pl.when(inner)
        def _():
            arrived(zin.at[k], z_recv.at[k])
            for here, rows, cols in tiles(seg, k):
                both = lambda c: (zin[k, c, 0, here, cols], zin[k, c, 1, here, cols])
                pair = lambda ref, c: (ref[c, 0, rows, cols], ref[c, 1, rows, cols])
                left = {2: pair(gl2, 0), 3: pair(gl2, 1)}
                right = {0: both(0), 1: both(1), 2: pair(gg2, 0), 3: pair(gg2, 1)}
                for c in (0, 1):
                    left.update({mid + c: both(2 + c), mid + 2 + c: both(6 + c)})
                    right.update({mid + c: both(4 + c), mid + 2 + c: both(8 + c)})
                for w in range(energies):
                    value = correlate(left, right, w)
                    for m in (0, 1):
                        if w in (2, 3):
                            dpair[w - 2, m, rows, cols] = on2[w - 2, m, rows, cols] - value[m] * scale
                        else:
                            res[k, w if w < 2 else w - 2, m, here, cols] = value[m]
            for part, target in enumerate((0, mid, mid + 2)):
                p_copy(seg, k, part, 0, target).start()

        @pl.when(jnp.logical_not(inner))
        def _():
            arrived(pin.at[k, pl.ds(0, 2)], p_recv.at[k])

        @pl.when(outer)
        def _():
            for here, rows, cols in tiles(seg, k):
                pair = lambda ref, c: (ref[c, 0, rows, cols], ref[c, 1, rows, cols])
                left = {0: pair(gl2, 0), 1: pair(gl2, 1)}
                right = {0: pair(gg2, 0), 1: pair(gg2, 1)}
                for c in (0, 1):
                    value = correlate(left, right, c)
                    for m in (0, 1):
                        total = value[m] + pin[k, c, m, here, cols]
                        dpair[c, m, rows, cols] = on2[c, m, rows, cols] - total * scale

        @pl.when(z >= 2)
        def _():
            for here, rows, cols in tiles(seg, k):
                for c in (0, 1):
                    for m in (0, 1):
                        dpair[c, m, rows, cols] = on2[c, m, rows, cols] - pin[k, c, m, here, cols] * scale

    def polarize(seg, k):
        _, _, _, zin, res, pin, z_recv, p_recv = seg

        @pl.when(center)
        def _():
            arrived(zin.at[k], z_recv.at[k])
            for here, rows, cols in tiles(seg, k):
                both = lambda ref, *at: (ref[(*at, 0, here, cols)], ref[(*at, 1, here, cols)])
                pair = lambda ref, c: (ref[c, 0, rows, cols], ref[c, 1, rows, cols])
                left = {mid: pair(gl2, 0), mid + 1: pair(gl2, 1), mid + 2: both(zin, k, 4), mid + 3: both(zin, k, 5)}
                right = {c: both(zin, k, c) for c in range(4)}
                right.update({mid: pair(gg2, 0), mid + 1: pair(gg2, 1)})
                right.update({mid + 2: both(zin, k, 6), mid + 3: both(zin, k, 7)})
                for w in range(energies):
                    value = correlate(left, right, w)
                    for m in (0, 1):
                        if w in (mid, mid + 1):
                            dpair[w - mid, m, rows, cols] = on2[w - mid, m, rows, cols] - value[m] * scale
                        else:
                            res[k, w if w < mid else w - 2, m, here, cols] = value[m]
            for part, target in enumerate((0, 2, mid + 2)):
                p_copy(seg, k, part, 0, target).start()

        @pl.when(inner)
        def _():
            arrived(pin.at[k, pl.ds(0, 2)], p_recv.at[k])
            for here, rows, cols in tiles(seg, k):
                for c in (0, 1):
                    for m in (0, 1):
                        total = res[k, 2 + c, m, here, cols] + pin[k, c, m, here, cols]
                        dpair[c, m, rows, cols] = on2[c, m, rows, cols] - total * scale

        @pl.when(outer)
        def _():
            arrived(pin.at[k], p_recv.at[k])
            for here, rows, cols in tiles(seg, k):
                pair = lambda ref, c: (ref[c, 0, rows, cols], ref[c, 1, rows, cols])
                left = {0: pair(gl2, 0), 1: pair(gl2, 1)}
                right = {0: pair(gg2, 0), 1: pair(gg2, 1)}
                for c in (0, 1):
                    value = correlate(left, right, c)
                    for m in (0, 1):
                        total = value[m] + (pin[k, c, m, here, cols] + pin[k, 2 + c, m, here, cols])
                        dpair[c, m, rows, cols] = on2[c, m, rows, cols] - total * scale

        @pl.when(far)
        def _():
            arrived(pin.at[k, pl.ds(0, 2)], p_recv.at[k])
            for here, rows, cols in tiles(seg, k):
                for c in (0, 1):
                    for m in (0, 1):
                        dpair[c, m, rows, cols] = on2[c, m, rows, cols] - pin[k, c, m, here, cols] * scale

    def strip(first, last):
        return pl.ds(pl.multiple_of(h * half + starts[first], 8), starts[last] - starts[first])

    def spread(seg, k, at, passed=True):
        size, base = seg[1], seg[2]
        sub = pl.ds(pl.multiple_of(base + k * size, 8), size)
        there = diag.at[i, :, pl.ds(pl.multiple_of(h * half + base + k * size, 8), size)]
        if not passed:
            remote(dpair.at[1 - y, :, sub], there, t_send.at[0], d_recv.at[2, at], block=dn).start()
        remote(dpair.at[1 - y, :, sub], there, d_send.at[1], d_recv.at[1, at], block=yn).start()
        remote(dpair.at[y, :, sub], there, d_send.at[0], d_recv.at[0, at], block=xn).start()
        remote(dpair.at[y, :, sub], there, dm_send.at[0], dm_recv.at[0], energy=sib).start()
        pltpu.make_async_copy(dpair.at[y, :, sub], there, d_local).start()

    def gather_y(first, last, passing=True):
        for k in range(first, last):
            arrived(diag.at[yn, :, strip(k, k + 1)], d_recv.at[1, k])
        part = diag.at[yn, :, strip(first, last)]
        if passing:
            remote(part, part, d_send.at[2], d_recv.at[2, first], block=xn).start()
        remote(part, part, dm_send.at[2], dm_recv.at[2], energy=sib).start()

    def gather_x(first, last):
        for k in range(first, last):
            arrived(diag.at[xn, :, strip(k, k + 1)], d_recv.at[0, k])
        part = diag.at[xn, :, strip(first, last)]
        remote(part, part, dm_send.at[1], dm_recv.at[1], energy=sib).start()

    def gather(first, last):
        gather_y(first, last, passing=False)
        gather_x(first, last)

    def gather_passed(first, last):
        part = diag.at[dn, :, strip(first, last)]
        arrived(part, d_recv.at[2, first])
        remote(part, part, dm_send.at[3], dm_recv.at[3], energy=sib).start()

    def prefactor(k, j, w):
        @pl.when(valid(j, w))
        def _():
            if k is None:
                pltpu.make_async_copy(coupling[w], lu.at[i, w], l_local.at[w]).wait()
            else:
                arrived(lu.at[j, w, :, other], lm_recv.at[k, w])

            def step(block, carry):
                rows = pl.ds(pl.multiple_of(block * 16, 16), 16)
                split = factor((lu[j, w, 0, rows], lu[j, w, 1, rows]))
                for at in range(3):
                    for part in (0, 1):
                        flu[j, w, 2 * at + part, rows] = split[at][part]
                return carry

            lax.fori_loop(0, n // 16, step, 0)

    def gather_first():
        @pl.when(before)
        def _():
            gather_y(0, few)

    plan = {
        0: [lambda: prefactor(None, i, 0)],
        1: [lambda: lu_direct_x(1), lambda: prefactor(None, i, 1)],
        2: [src_direct, lambda: prefactor(0, xn, 0)],
        3: [lambda: lu_direct_y(0), lambda: lu_direct_y(1), lambda: prefactor(0, xn, 1)],
        4: [gather_first, lambda: prefactor(1, yn, 0)],
        5: [lambda: gather_y(2, 5), lambda: prefactor(1, yn, 1)],
    }

    def turn(k, carry):
        @pl.when(k < many - 1)
        def _():
            ahead(segments[1], k + 1)

        @pl.when(k == many - 1)
        def _():
            ahead(segments[2], 0)

        polarize(segments[1], k)
        spread(segments[1], k, few + k)
        for at, work in plan.items():

            @pl.when(k == at)
            def _(work=work):
                for step in work:
                    step()

        return carry

    @pl.when(before)
    def _():
        for k in range(few):
            polarize_first(k)
            spread(segments[0], k, k)

    @pl.when(inner)
    def _():
        for k in range(few):
            z_copies(segments[2], k, 1)

    ahead(segments[1], 0)
    lu_direct_x(0)
    lax.fori_loop(0, many, turn, 0)

    @pl.when(z >= 2)
    def _():
        for k in range(few):
            polarize_first(k)
            spread(segments[0], k, k, passed=False)

    ahead(segments[2], 1)
    polarize(segments[2], 0)
    spread(segments[2], 0, end, passed=False)
    gather_y(5, 6)
    polarize(segments[2], 1)
    spread(segments[2], 1, end + 1, passed=False)
    gather_y(6, 8)
    gather_x(2, 8)
    src_passed()
    lu_passed(0)
    lu_passed(1)

    @pl.when(before)
    def _():
        gather_x(0, few)
        gather_passed(0, few)

    gather_passed(2, 5)
    gather_passed(5, 6)
    prefactor(2, dn, 0)
    prefactor(2, dn, 1)
    for k in (end, end + 1):
        gather(k, k + 1)
        gather_passed(k, k + 1)
    gather_passed(6, 8)

    @pl.when(z >= 2)
    def _():
        for k in range(few):
            gather(k, k + 1)
            gather_passed(k, k + 1)


    a, b, m, q = 3 * x, 2 - x, 1 + x, 3 - 3 * x
    couple = lambda j, w: tuple((flu[j, w, 2 * k], flu[j, w, 2 * k + 1]) for k in range(3))
    diagonal = lambda j: (diag[j, 0], diag[j, 1])
    source = lambda j: (src[j, 0], src[j, 1])

    def put(ref, at, v):
        ref[at, 0], ref[at, 1] = v

    edge_d = []
    for k in (0, 1):
        part = edge_diag.at[:, pl.ds(k * half, half)]
        edge_d.append(remote(part, part, e_sem.at[2 * k], e_sem.at[2 * k + 1], energy=sib))
    edge_s = remote(edge_src, edge_src, e_sem.at[4], e_sem.at[5], energy=sib)

    def edge_term():
        t = factor(times(couple(b, 1 - x), factor(lean_inverse(diagonal(q), -0.2))))
        for k in (0, 1):
            rows = slice(k * half, (k + 1) * half)
            v = times(tuple(tuple(u[rows] for u in w) for w in t), couple(q, x))
            edge_diag[0, rows], edge_diag[1, rows] = v
            edge_d[k].start()
        edge_src[0], edge_src[1] = apply(t, source(q))
        edge_s.start()

    @pl.when(y == h)
    def _():
        pltpu.make_async_copy(rhs.at[:, 0], src.at[i], s_local).wait()

    @pl.when(y != h)
    def _():
        arrived(src.at[i], sm_recv.at[0])

    for k, j in enumerate((xn, yn, dn)):
        arrived(src.at[j, :, other], sm_recv.at[k + 1])

    arrived(diag.at[xn, :, other], dm_recv.at[1])

    @pl.when(jnp.logical_and(h == y, x != y))
    def _():
        edge_term()

    pltpu.make_async_copy(dpair.at[y], diag.at[i, :, mine], d_local).wait()
    for k, j in ((0, i), (2, yn), (3, dn)):
        arrived(diag.at[j, :, other], dm_recv.at[k])

    @pl.when(jnp.logical_and(h == y, x == y))
    def _():
        edge_term()

    inv = factor(lean_inverse(diagonal(m), -0.2))
    t = factor(times(stacked(couple(a, 1 - x), couple(b, x)), inv))
    top, low = (lambda v: (v[0][:n], v[1][:n])), (lambda v: (v[0][n:], v[1][n:]))
    v = times(t, couple(m, x))
    put(dp, 0, minus(diagonal(a), top(v)))
    put(fp, 1, low(v))
    v = times(t, couple(m, 1 - x))
    put(dp, 1, minus(diagonal(b), low(v)))
    put(fp, 0, top(v))
    v = apply(t, source(m))
    put(sp, 0, minus(source(a), top(v)))
    put(sp, 1, minus(source(b), low(v)))

    def add_edge():
        @pl.when(h != y)
        def _():
            for copy in edge_d:
                copy.wait_recv()

        for k in (0, 1):
            dp[1, k] = dp[1, k] - edge_diag[k]

    this = jnp.where(h == x, 0, 1)

    @pl.when(h == x)
    def _():
        add_edge()

    that = 1 - this
    at = lambda ref, k: (ref[k, 0], ref[k, 1])
    t = factor(times(factor(at(fp, this)), factor(lean_inverse(at(dp, that)))))
    v = times(t, factor(at(fp, that)))

    @pl.when(h != x)
    def _():
        add_edge()

    @pl.when(h != y)
    def _():
        edge_s.wait_recv()

    for k in (0, 1):
        sp[1, k] = sp[1, k] - edge_src[k]
    last = minus(at(dp, this), v)
    right = plus(at(sp, this), apply(t, at(sp, that)))
    rest = factor(remainder_of(last))
    inverse_guess = 1.0 / diagonal_guess
    found = right
    for _ in range(2):
        found = plus(right, apply(rest, found))
    home, keep = [], []
    for k in (0, 1):
        part = pl.ds(k * half, half)
        there = out.at[:, 0, part]
        home.append(
            remote(
                value.at[:, part], there, out_sem.at[k], out_sem.at[2 + k], energy=2 * z + y, block=2 * h + x
            )
        )
        keep.append(pltpu.make_async_copy(value.at[:, part], there, out_sem.at[k]))
    for k in (0, 1):
        rows = slice(k * half, (k + 1) * half)
        upper_part = tuple(tuple(u[rows] for u in w) for w in rest)
        v = plus((right[0][rows], right[1][rows]), apply(upper_part, found))
        value[0, rows], value[1, rows] = v[0] * inverse_guess, v[1] * inverse_guess

        @pl.when(h != y)
        def _(k=k):
            home[k].start()

        @pl.when(h == y)
        def _(k=k):
            keep[k].start()

    @pl.when(h == y)
    def _():
        for copy in keep:
            copy.wait()

    whole_array, most = gg.at[:, 0], gg.at[:, 0, pl.ds(0, n - 2 * edge)]
    rest_of = gg.at[:, 0, pl.ds(0, 2 * edge)]

    def p_sent(seg, parts):
        for k in range(parts):
            sent(seg[4].at[:, pl.ds(2 * k, 2)], p_send.at[seg[0], k])

    @pl.when(outer)
    def _():
        sent(most, z_send.at[0])
        sent(whole_array, z_send.at[1])

    @pl.when(inner)
    def _():
        sent(most, z_send.at[0])
        for seg, parts in zip(segments, (3, 1, 1)):
            p_sent(seg, parts)

    @pl.when(center)
    def _():
        sent(rest_of, z_send.at[0])
        sent(rest_of, z_send.at[1])
        for seg in segments[1:]:
            p_sent(seg, 3)

    @pl.when(far)
    def _():
        sent(whole_array, z_send.at[0])
        sent(whole_array, z_send.at[1])

    for copy in pairs:
        copy.wait_send()
    for k in range(2):
        sent(dpair.at[0], d_send.at[k])

    @pl.when(before)
    def _():
        sent(dpair.at[0, :, pl.ds(0, half - edge)], d_send.at[2])
        sent(dpair.at[0, :, pl.ds(0, edge)], t_send.at[0])

    @pl.when(z >= 2)
    def _():
        sent(dpair.at[0, :, pl.ds(0, half - 2 * edge)], d_send.at[2])
        sent(dpair.at[0, :, pl.ds(0, 2 * edge)], t_send.at[0])

    for k in range(4):
        sent(dpair.at[0], dm_send.at[k])
    part = src.at[0, :, mine]

    @pl.when(y == h)
    def _():
        sent(rhs.at[:, 0], sm_send.at[0])

    sent(rhs.at[:, 0], s_send.at[0])
    sent(part, s_send.at[1])
    for k in range(3):
        sent(part, sm_send.at[k + 1])
    for w in (0, 1):
        part = lu.at[0, w, :, mine]

        @pl.when(valid(i, w))
        def _(w=w, part=part):
            sent(part, l_send.at[0, w])
            sent(part, l_send.at[1, w])

        for k, j in enumerate((xn, yn, dn)):

            @pl.when(valid(j, w))
            def _(k=k, w=w, part=part):
                if k == 0:
                    sent(part, l_send.at[2, w])
                sent(part, lm_send.at[k, w])

    @pl.when(h == y)
    def _():
        for copy in (*edge_d, edge_s):
            copy.wait_send()

    @pl.when(h != y)
    def _():
        for copy in home:
            copy.wait()


def line(g_lesser, g_greater, onsite, lower, upper, rhs):
    count = lax.axis_size("block")
    n, columns = onsite.shape[2], rhs.shape[-1]
    half = n // 2
    r = half // 8
    many, few, fine = 6, 2, r // 2
    f32 = jnp.float32
    dma = pltpu.SemaphoreType.DMA
    anywhere = pl.BlockSpec(memory_space=pl.ANY)
    pair = pltpu.VMEM((2, 2, half, n), f32)
    return pl.pallas_call(
        line_kernel,
        name="line",
        out_shape=pltpu.VMEM((2, 1, n, columns), f32),
        in_specs=[anywhere] * 6,
        out_specs=anywhere,
        scratch_shapes=[
            pair, pair, pair,
            pltpu.VMEM((few, 10, 2, fine, n), f32),
            pltpu.VMEM((few, 6, 2, fine, n), f32),
            pltpu.VMEM((few, 4, 2, fine, n), f32),
            pltpu.VMEM((many, 8, 2, r, n), f32),
            pltpu.VMEM((many, 6, 2, r, n), f32),
            pltpu.VMEM((many, 4, 2, r, n), f32),
            pltpu.VMEM((few, 8, 2, fine, n), f32),
            pltpu.VMEM((few, 6, 2, fine, n), f32),
            pltpu.VMEM((few, 4, 2, fine, n), f32),
            pair,
            pltpu.VMEM((count, 2, n, n), f32),
            pltpu.VMEM((count, 2, n, columns), f32),
            pltpu.VMEM((count, 2, 2, n, n), f32),
            pltpu.VMEM((2, 2, n, n), f32),
            pltpu.VMEM((2, 2, n, n), f32),
            pltpu.VMEM((2, 2, n, columns), f32),
            pltpu.VMEM((2, n, columns), f32),
            dma((2,)), dma((few,)), dma((3, 3)), dma((few,)), dma((many,)), dma((many,)), dma((few,)), dma((few,)),
            dma((3,)), dma((3,)), dma((3,)),
            dma((3,)), dma((3, many + 2 * few)), dma, dma((4,)), dma((4,)), dma((1,)), dma((1,)),
            dma((2,)), dma((3,)), dma, dma((4,)), dma((4,)),
            dma((3, 2)), dma((3, 2)), dma((2,)), dma((3, 2)), dma((3, 2)), dma((4,)),
            pltpu.VMEM((2, n, n), f32), pltpu.VMEM((2, n, columns), f32), dma((6,)),
            pltpu.VMEM((count, 2, 6, n, n), jnp.bfloat16),
        ],
        compiler_params=pltpu.CompilerParams(
            collective_id=1, has_side_effects=True, vmem_limit_bytes=60 * 1024 * 1024
        ),
    )(g_lesser, g_greater, onsite, lower, upper, rhs)


def shifted(value, steps):
    count = lax.axis_size("block")
    leading, last = max(0, -steps), min(count, count - steps)
    pairs = [(k, k + steps) for k in range(leading, last)]
    return lax.ppermute(value, "block", pairs)


def shards(g_lesser, g_greater, onsite, lower, upper, rhs):
    index = lax.axis_index("block")
    count = lax.axis_size("block")
    levels = count.bit_length() - 1
    n = onsite.shape[-1]
    both = jnp.concatenate(
        [jnp.where(index > 0, lower, 0.0), jnp.where(index < count - 1, upper, 0.0)], axis=-1
    )
    if levels == 2 and lax.axis_size("energy") == 8:
        return line(g_lesser, g_greater, onsite, lower, upper, rhs)
    diag, near_lu, near_s = front(g_lesser, g_greater, onsite, lower, upper, rhs)
    diag = parts(diag)
    first, final = index < 2, index >= count - 2
    low, up = cut(parts(both), 0, n), cut(parts(both), n, 2 * n)
    source = parts(rhs[:, 0])
    for depth in range(levels):
        stride = 1 << depth
        inv = inverse(diag)
        if depth == levels - 1:
            coupling = tuple(jnp.where(index < stride, up[k], low[k]) for k in (0, 1))
            sent = product(inv, wide(coupling, source))
            swap = [(k, k ^ stride) for k in range(count)]
            got = parts(lax.ppermute(jnp.stack(sent), "block", swap))
            change = product(coupling, got)
            diag = minus(diag, cut(change, 0, n))
            source = minus(source, cut(change, n, None))
        elif depth == 0:
            packed = jnp.stack(inv)
            inv_left, inv_right = parts(shifted(packed, 1)), parts(shifted(packed, -1))
            t, w = product(low, inv_left), product(up, inv_right)
            lu_l, lu_r = near_lu[0], near_lu[1]
            change = product(t, wide(parts(lu_l[0]), parts(lu_l[1]), parts(near_s[0])))
            other = product(w, wide(parts(lu_r[0]), parts(lu_r[1]), parts(near_s[1])))
            change = tuple(jnp.where(index > 0, v, 0.0) for v in change)
            other = tuple(jnp.where(index < count - 1, v, 0.0) for v in other)
            diag = minus(minus(diag, cut(change, n, 2 * n)), cut(other, 0, n))
            source = minus(minus(source, cut(change, 2 * n, None)), cut(other, 2 * n, None))
            low = tuple(jnp.where(first, 0.0, -v) for v in cut(change, 0, n))
            up = tuple(jnp.where(final, 0.0, -v) for v in cut(other, n, 2 * n))
        else:
            sent = jnp.stack(product(inv, wide(low, up, source)))
            left, right = parts(shifted(sent, stride)), parts(shifted(sent, -stride))
            change, other = product(low, left), product(up, right)
            diag = minus(minus(diag, cut(change, n, 2 * n)), cut(other, 0, n))
            source = minus(minus(source, cut(change, 2 * n, None)), cut(other, 2 * n, None))
            low = tuple(-v for v in cut(change, 0, n))
            up = tuple(-v for v in cut(other, n, 2 * n))
    return jnp.stack(solve(diag, source))[:, None]


def solution(mesh):
    placed = (
        P(None, "energy", "block", None),
        P(None, "energy", "block", None),
        P(None, "energy", "block", None),
        P(None, "block", None),
        P(None, "block", None),
        P(None, "energy", "block", None),
    )
    return jax.shard_map(
        shards,
        mesh=mesh,
        in_specs=placed,
        out_specs=P(None, "energy", "block", None),
        check_vma=False,
    )
```

```python
import math

import jax
import jax.numpy as jnp
from jax import lax
from jax.experimental import pallas as pl
from jax.experimental.pallas import tpu as pltpu
from jax.sharding import PartitionSpec as P

diagonal_guess = 5.0
MODE = lax.Precision.HIGH
MESH = pl.DeviceIdType.MESH


def real_product(a, b):
    return jnp.matmul(a, b, precision=MODE)


def product(a, b):
    ar, ai = a
    br, bi = b
    return (
        real_product(ar, br) - real_product(ai, bi),
        real_product(ar, bi) + real_product(ai, br),
    )


def parts(a):
    return a[0], a[1]


def plus(a, b):
    return a[0] + b[0], a[1] + b[1]


def minus(a, b):
    return a[0] - b[0], a[1] - b[1]


def wide(*pieces):
    return tuple(jnp.concatenate([p[k] for p in pieces], axis=-1) for k in (0, 1))


def cut(a, start, stop):
    return a[0][:, start:stop], a[1][:, start:stop]


def remainder(matrix):
    eye = jnp.eye(matrix[0].shape[-1], dtype=jnp.float32)
    return eye - matrix[0] * (1.0 / diagonal_guess), -matrix[1] * (1.0 / diagonal_guess)


def inverse(matrix):
    eye = jnp.eye(matrix[0].shape[-1], dtype=jnp.float32)
    b = remainder(matrix)
    square = product(b, b)
    cube = product(b, square)
    scale = 1.0 / diagonal_guess
    return (eye + b[0] + square[0] + cube[0]) * scale, (b[1] + square[1] + cube[1]) * scale


def solve(matrix, source):
    b = remainder(matrix)
    value = source
    for _ in range(3):
        value = plus(source, product(b, value))
    scale = 1.0 / diagonal_guess
    return value[0] * scale, value[1] * scale


def front_kernel(
    gl, gg, onsite, lower, upper, rhs, diag, near_lu, near_s,
    lu, gl_all, gg_all, res, pol,
    in_send, in_recv, out_send, out_recv, lu_send, lu_recv, hop_send, hop_recv,
    mate_send, mate_recv, local, rows_out=None, partner=None,
):
    e, i = lax.axis_index("energy"), lax.axis_index("block")
    energies, count = lax.axis_size("energy"), lax.axis_size("block")
    share = gl.shape[2] // energies
    c, p = lax.rem(e, 2), lax.rem(i, 2)
    mate, side = e + 1 - 2 * c, 1 - p
    pair, onward, behind = i + 1 - 2 * p, i + 2 - 4 * p, i - 2 + 4 * p
    has_onward = jnp.logical_and(onward >= 0, onward < count)
    has_behind = jnp.logical_and(behind >= 0, behind < count)

    fill = [pltpu.make_async_copy((lower, upper)[k], lu.at[k], local.at[k]) for k in (0, 1)]
    for copy in fill:
        copy.start()
    barrier = pltpu.get_barrier_semaphore()
    for k in range(1, energies):
        pl.semaphore_signal(barrier, inc=1, device_id={"energy": lax.rem(e + k, energies)}, device_id_type=MESH)
    pl.semaphore_signal(barrier, inc=1, device_id={"block": pair}, device_id_type=MESH)

    @pl.when(has_onward)
    def _():
        pl.semaphore_signal(barrier, inc=1, device_id={"block": onward}, device_id_type=MESH)

    @pl.when(has_behind)
    def _():
        pl.semaphore_signal(barrier, inc=1, device_id={"block": behind}, device_id_type=MESH)

    peers = energies
    if partner is not None:
        peers = energies + 1
        pl.semaphore_signal(barrier, inc=1, device_id={"block": partner}, device_id_type=MESH)
    pl.semaphore_wait(barrier, peers + has_onward.astype(jnp.int32) + has_behind.astype(jnp.int32))

    def remote(src, dst, send, recv, **where):
        return pltpu.make_async_remote_copy(
            src_ref=src, dst_ref=dst, send_sem=send, recv_sem=recv, device_id=where, device_id_type=MESH
        )

    part = share // 2

    def in_copy(h, k, q, source):
        src, dst = ((gl, gl_all), (gg, gg_all))[k]
        rows = src.at[:, 0, pl.ds(q * share + h * part, part), :]
        there = dst.at[source, :, pl.ds(h * part, part), :]
        return remote(rows, there, in_send.at[h, k, q], in_recv.at[h, k, source], energy=q)

    def out_copy(h, w, source):
        rows = pl.ds(h * part, part)
        return remote(
            res.at[w, :, rows, :], pol.at[source, :, rows, :], out_send.at[h, w], out_recv.at[h, source], energy=w
        )

    for copy in fill:
        copy.wait()
    for h in (0, 1):
        for k in (0, 1):
            for q in range(energies):

                @pl.when(q != e)
                def _():
                    in_copy(h, k, q, e).start()

    own = []
    for k, (src, dst) in enumerate(((gl, gl_all), (gg, gg_all))):
        rows = src.at[:, 0, pl.ds(pl.multiple_of(e * share, 8), share), :]
        own.append(pltpu.make_async_copy(rows, dst.at[e], local.at[k]))
        own[-1].start()

    mine = (lu.at[c, 0], lu.at[c, 1], rhs.at[:, 0])

    def slot(s, k):
        return near_s.at[s] if k == 2 else near_lu.at[s, c, k]

    direct = [remote(mine[k], slot(p, k), lu_send.at[k], lu_recv.at[k], block=pair) for k in range(3)]
    hops = [remote(slot(side, k), slot(p, k), hop_send.at[k], hop_recv.at[k], block=onward) for k in range(3)]
    for copy in direct:
        copy.start()
    shared = [
        remote(slot(s, k), slot(s, k), mate_send.at[j, k], mate_recv.at[j, k], energy=mate)
        for j, s in enumerate((side, p))
        for k in (0, 1)
    ]
    for k in range(3):
        direct[k].wait_recv()

        @pl.when(has_onward)
        def _():
            hops[k].start()

        if k < 2:
            shared[k].start()

    for copy in own:
        copy.wait()
    scale = 1.0 / math.sqrt(energies)
    for h in (0, 1):
        for k in (0, 1):
            for q in range(energies):

                @pl.when(q != e)
                def _():
                    in_copy(h, k, q, q).wait_recv()

        for w in range(energies):

            def step(row, carry, w=w, h=h):
                rows = pl.ds(pl.multiple_of(h * part + row * 8, 8), 8)
                real = imag = None
                for k in range(w, energies):
                    a, b = gl_all[k, 0, rows], gl_all[k, 1, rows]
                    x, y = gg_all[k - w, 0, rows], gg_all[k - w, 1, rows]
                    s, t = a * x - b * y, a * y + b * x
                    real, imag = (s, t) if real is None else (real + s, imag + t)
                res[w, 0, rows] = real * scale
                res[w, 1, rows] = imag * scale
                return carry

            lax.fori_loop(0, part // 8, step, 0)

            @pl.when(w != e)
            def _():
                out_copy(h, w, e).start()

    keep = pltpu.make_async_copy(res.at[e], pol.at[e], local.at[0])
    keep.start()

    @pl.when(has_behind)
    def _():
        for k in range(3):
            hops[k].wait_recv()
            if k < 2:
                shared[2 + k].start()

    def hand_on(q):
        rows_out[0][q].wait_recv()

        @pl.when(has_onward)
        def _():
            rows_out[1][q].start()

    keep.wait()
    for q in range(energies):

        @pl.when(q != e)
        def _():
            out_copy(0, q, q).wait_recv()
            out_copy(1, q, q).wait_recv()

        rows = pl.ds(q * share, share)
        for k in (0, 1):
            diag[k, rows] = onsite[k, 0, rows] - pol[q, k]
        if rows_out is not None:
            rows_out[0][q].start()
            if q > 0:
                hand_on(q - 1)
    if rows_out is not None:
        hand_on(energies - 1)

    for k in range(2):
        shared[k].wait_recv()

    @pl.when(has_behind)
    def _():
        for k in range(2):
            shared[2 + k].wait()

    for k in range(2):
        shared[k].wait_send()
    for k in range(3):
        direct[k].wait_send()

        @pl.when(has_onward)
        def _():
            hops[k].wait_send()

    for q in range(energies):

        @pl.when(q != e)
        def _():
            for h in (0, 1):
                in_copy(h, 0, q, e).wait_send()
                in_copy(h, 1, q, e).wait_send()
                out_copy(h, q, e).wait_send()


def front(g_lesser, g_greater, onsite, lower, upper, rhs):
    energies = lax.axis_size("energy")
    n, columns = onsite.shape[2], rhs.shape[-1]
    share = n // energies
    vmem = pl.BlockSpec(memory_space=pltpu.VMEM)
    f32 = jnp.float32
    dma = pltpu.SemaphoreType.DMA
    pieces = pltpu.VMEM((energies, 2, share, n), f32)
    return pl.pallas_call(
        front_kernel,
        name="front",
        out_shape=(
            jax.ShapeDtypeStruct((2, n, n), f32),
            jax.ShapeDtypeStruct((2, 2, 2, n, n), f32),
            jax.ShapeDtypeStruct((2, 2, n, columns), f32),
        ),
        in_specs=[vmem] * 6,
        out_specs=(vmem,) * 3,
        scratch_shapes=[
            pltpu.VMEM((2, 2, n, n), f32),
            pieces, pieces, pieces, pieces,
            dma((2, 2, energies)), dma((2, 2, energies)), dma((2, energies)), dma((2, energies)),
            dma((3,)), dma((3,)), dma((3,)), dma((3,)),
            dma((2, 2)), dma((2, 2)), dma((2,)),
        ],
        compiler_params=pltpu.CompilerParams(collective_id=0, has_side_effects=True),
    )(g_lesser, g_greater, onsite, lower, upper, rhs)


def halves(x):
    high = x.astype(jnp.bfloat16)
    return high, (x - high.astype(jnp.float32)).astype(jnp.bfloat16)


def factor(a):
    return halves(a[0]), halves(a[1]), halves(a[0] + a[1])


def three_pass(a, b):
    dot = lambda u, v: jnp.dot(u, v, preferred_element_type=jnp.float32)
    return dot(a[0], b[0]) + (dot(a[0], b[1]) + dot(a[1], b[0]))


def times(a, b):
    first, second, third = (three_pass(a[k], b[k]) for k in range(3))
    return first - second, third - first - second


def inverse_of(matrix):
    eye_rows = lax.broadcasted_iota(jnp.int32, matrix[0].shape, 0)
    eye_columns = lax.broadcasted_iota(jnp.int32, matrix[0].shape, 1)
    eye = jnp.where(eye_rows == eye_columns, 1.0, 0.0)
    scale = 1.0 / diagonal_guess
    b = eye - matrix[0] * scale, -matrix[1] * scale
    fb = factor(b)
    square = times(fb, fb)
    cube = times(fb, factor(square))
    return (eye + b[0] + square[0] + cube[0]) * scale, (b[1] + square[1] + cube[1]) * scale


def rounded_product(a, b):
    dot = lambda u, v: jnp.dot(u, v, preferred_element_type=jnp.float32)
    first, second, third = (dot(a[k], b[k]) for k in range(3))
    return first - second, third - first - second


def rounded(a):
    return tuple(v.astype(jnp.bfloat16) for v in (a[0], a[1], a[0] + a[1]))


def unit_of(matrix):
    rows = lax.broadcasted_iota(jnp.int32, matrix[0].shape, 0)
    columns = lax.broadcasted_iota(jnp.int32, matrix[0].shape, 1)
    return jnp.where(rows == columns, 1.0, 0.0)


def remainder_of(matrix):
    return unit_of(matrix) - matrix[0] * (1.0 / diagonal_guess), -matrix[1] * (1.0 / diagonal_guess)


def lean_inverse(matrix, shift=0.0):
    eye, b = unit_of(matrix), remainder_of(matrix)
    scale = 1.0 / diagonal_guess
    c = b[0] - shift * eye, b[1]
    split = factor(c)
    square = times(split, split)
    cube = rounded_product(tuple(v[0] for v in split), rounded(square))
    zero, one, two = 1 + shift + shift**2 + shift**3, 1 + 2 * shift + 3 * shift**2, 1 + 3 * shift
    return (
        (zero * eye + one * c[0] + two * square[0] + cube[0]) * scale,
        (one * c[1] + two * square[1] + cube[1]) * scale,
    )


def stacked(a, b):
    return tuple(tuple(jnp.concatenate([a[k][j], b[k][j]], axis=0) for j in (0, 1)) for k in range(3))


def apply(a, b):
    columns = b[0].shape[1]
    w = halves(jnp.concatenate([b[0], b[1]], axis=1))
    p, q = three_pass(a[0], w), three_pass(a[1], w)
    return p[:, :columns] - q[:, columns:], p[:, columns:] + q[:, :columns]


def line_kernel(
    gl, gg, onsite, lower, upper, rhs, out,
    gl2, gg2, on2, zin_h, res_h, pin_h, zin_a, res_a, pin_a, zin_b, res_b, pin_b, dpair, diag, src, lu, dp, fp, sp, value,
    z_send, z_recv_h, p_send, p_recv_h, z_recv_a, p_recv_a, z_recv_b, p_recv_b, pair_send, pair_recv, pair_local,
    d_send, d_recv, d_local, dm_send, dm_recv, t_send, t_recv,
    s_send, s_recv, s_local, sm_send, sm_recv,
    l_send, l_recv, l_local, lm_send, lm_recv, out_sem, edge_diag, edge_src, e_sem, flu,
):
    e, i = lax.axis_index("energy"), lax.axis_index("block")
    energies, count = lax.axis_size("energy"), lax.axis_size("block")
    n = diag.shape[-1]
    half = n // 2
    many, r = zin_a.shape[0], zin_a.shape[3]
    few, fine = zin_b.shape[0], zin_b.shape[3]
    edge, end = few * fine, few + many
    starts = [k * fine for k in range(few)] + [edge + k * r for k in range(many)]
    starts += [half - edge + k * fine for k in range(few + 1)]
    segments = (
        (0, fine, 0, zin_h, res_h, pin_h, z_recv_h, p_recv_h),
        (1, r, edge, zin_a, res_a, pin_a, z_recv_a, p_recv_a),
        (2, fine, half - edge, zin_b, res_b, pin_b, z_recv_b, p_recv_b),
    )
    mid = energies // 2
    z, h = e // 2, lax.rem(e, 2)
    y, x = i // 2, lax.rem(i, 2)
    sib, xn, yn = e + 1 - 2 * h, i + 1 - 2 * x, i + 2 - 4 * y
    dn = yn + 1 - 2 * x
    outer, inner, center, far = z == 0, z == 1, z == 2, z == 3
    before = z < 2
    mine = pl.ds(pl.multiple_of(h * half, half), half)
    other = pl.ds(pl.multiple_of((1 - h) * half, half), half)
    scale = 1.0 / math.sqrt(energies)

    def remote(a, b, send, recv, energy=e, block=i):
        return pltpu.make_async_remote_copy(
            src_ref=a, dst_ref=b, send_sem=send, recv_sem=recv,
            device_id={"energy": energy, "block": block}, device_id_type=MESH,
        )

    barrier = pltpu.get_barrier_semaphore()
    for k in range(1, energies):
        pl.semaphore_signal(barrier, inc=1, device_id={"energy": lax.rem(e + k, energies)}, device_id_type=MESH)
    for block in (xn, yn):
        for c in (0, 1):
            pl.semaphore_signal(
                barrier, inc=1, device_id={"energy": 2 * z + c, "block": block}, device_id_type=MESH
            )
    pair_own = []
    for k, (a, b) in enumerate(((gg, gg2), (gl, gl2), (onsite, on2))):
        pair_own.append(pltpu.make_async_copy(a.at[:, 0, mine], b.at[h], pair_local.at[k]))
        pair_own[-1].start()
    pl.semaphore_wait(barrier, energies + 3)

    def valid(j, w):
        return j > 0 if w == 0 else j < count - 1

    coupling = (lower, upper)
    for w in (0, 1):

        @pl.when(valid(i, w))
        def _(w=w):
            remote(coupling[w].at[:, mine], lu.at[i, w, :, mine], l_send.at[0, w], l_recv.at[0, w], block=xn).start()
            remote(coupling[w].at[:, mine], lu.at[i, w, :, mine], l_send.at[1, w], l_recv.at[1, w], block=yn).start()
            pltpu.make_async_copy(coupling[w], lu.at[i, w], l_local.at[w]).start()

    def rows_of(g):
        return pl.ds(g * half, half)

    @pl.when(y == h)
    def _():
        pltpu.make_async_copy(rhs.at[:, 0], src.at[i], s_local).start()
        remote(rhs.at[:, 0], src.at[i], sm_send.at[0], sm_recv.at[0], energy=sib).start()
        for g in (0, 1):
            remote(
                rhs.at[:, 0, rows_of(g)], src.at[i, :, rows_of(g)], s_send.at[0], s_recv.at[0],
                energy=2 * z + g, block=xn,
            ).start()

    @pl.when(y != h)
    def _():
        for g in (0, 1):
            remote(
                rhs.at[:, 0, rows_of(g)], src.at[i, :, rows_of(g)], s_send.at[0], s_recv.at[1],
                energy=2 * z + g, block=yn,
            ).start()

    def z_copies(seg, k, which):
        _, size, base, zin, _, _, z_recv, _ = seg

        def to(a, slot, g, target, sem):
            piece = a.at[:, 0, pl.ds(pl.multiple_of(g * half + base + k * size, 8), size)]
            return remote(piece, zin.at[k, slot], z_send.at[sem], z_recv.at[k], energy=target + g)

        for g in (0, 1):
            if seg[0] == 0:
                if which == 0:
                    to(gg, e, g, mid - 2, 1).start()
                elif which == 2:
                    to(gl, e - mid + 2, g, mid - 2, 1).start()
                    to(gg, e - mid + 4, g, mid - 2, 0).start()
                elif which == 3:
                    to(gl, e - mid + 4, g, mid - 2, 1).start()
                    to(gg, e - mid + 6, g, mid - 2, 0).start()
            elif which == 0:
                to(gg, e, g, mid, 0).start()
                to(gg, e, g, mid - 2, 1).start()
            elif which == 1:
                to(gg, e, g, mid, 0).start()
            else:
                to(gl, e - mid + 2, g, mid, 1).start()
                to(gg, e - mid + 4, g, mid, 0).start()

    for which, role in ((0, outer), (1, inner), (2, center), (3, far)):

        @pl.when(role)
        def _(which=which):
            for seg, steps in zip(segments, (few, many, few)):
                if (which, seg[0]) in ((1, 0), (1, 2), (2, 1), (2, 2)):
                    continue

                def body(k, carry, seg=seg):
                    z_copies(seg, k, which)
                    return carry

                lax.fori_loop(0, steps, body, 0)

    pairs = []
    for k, (a, b) in enumerate(((gg, gg2), (gl, gl2), (onsite, on2))):
        pairs.append(remote(a.at[:, 0, other], b.at[h], pair_send.at[k], pair_recv.at[k], energy=sib))
        pairs[-1].start()

    def arrived(ref, sem):
        remote(ref, ref, sem, sem).wait_recv()

    def sent(ref, sem):
        remote(ref, ref, sem, sem).wait_send()

    def lu_direct_x(w):
        @pl.when(valid(xn, w))
        def _():
            part = lu.at[xn, w, :, mine]
            arrived(part, l_recv.at[0, w])
            remote(part, part, l_send.at[2, w], l_recv.at[2, w], block=yn).start()
            remote(part, part, lm_send.at[0, w], lm_recv.at[0, w], energy=sib).start()

    def lu_direct_y(w):
        @pl.when(valid(yn, w))
        def _():
            part = lu.at[yn, w, :, mine]
            arrived(part, l_recv.at[1, w])
            remote(part, part, lm_send.at[1, w], lm_recv.at[1, w], energy=sib).start()

    def lu_passed(w):
        @pl.when(valid(dn, w))
        def _():
            part = lu.at[dn, w, :, mine]
            arrived(part, l_recv.at[2, w])
            remote(part, part, lm_send.at[2, w], lm_recv.at[2, w], energy=sib).start()

    def src_direct():
        part = src.at[yn, :, mine]
        arrived(part, s_recv.at[1])
        remote(part, part, s_send.at[1], s_recv.at[2], block=xn).start()
        remote(part, part, sm_send.at[2], sm_recv.at[2], energy=sib).start()
        part = src.at[xn, :, mine]
        arrived(part, s_recv.at[0])
        remote(part, part, sm_send.at[1], sm_recv.at[1], energy=sib).start()

    def src_passed():
        part = src.at[dn, :, mine]
        arrived(part, s_recv.at[2])
        remote(part, part, sm_send.at[3], sm_recv.at[3], energy=sib).start()

    for copy in pair_own:
        copy.wait()
    for copy in pairs:
        copy.wait_recv()

    def tiles(seg, k):
        size, base = seg[1], seg[2]
        for q in range(size // 8):
            for lane in range(n // 128):
                cols = slice(lane * 128, lane * 128 + 128)
                yield slice(q * 8, q * 8 + 8), pl.ds(pl.multiple_of(base + k * size + q * 8, 8), 8), cols

    def correlate(left, right, w):
        real = imag = None
        for k in left:
            if k - w in right:
                (a, b), (u, v) = left[k], right[k - w]
                s, t = a * u - b * v, a * v + b * u
                real, imag = (s, t) if real is None else (real + s, imag + t)
        return real, imag

    def p_copy(seg, k, part, slot, target, sem=None):
        where, _, _, _, res, pin, _, p_recv = seg
        sem = part if sem is None else sem
        return remote(
            res.at[k, pl.ds(2 * part, 2)], pin.at[k, pl.ds(slot, 2)], p_send.at[where, sem], p_recv.at[k],
            energy=target + h,
        )

    def ahead(seg, k):
        _, _, _, zin, res, _, z_recv, _ = seg

        @pl.when(inner)
        def _():
            arrived(zin.at[k, pl.ds(0, 2)], z_recv.at[k])
            for here, rows, cols in tiles(seg, k):
                both = lambda ref, *at: (ref[(*at, 0, here, cols)], ref[(*at, 1, here, cols)])
                pair = lambda ref, c: (ref[c, 0, rows, cols], ref[c, 1, rows, cols])
                left = {2: pair(gl2, 0), 3: pair(gl2, 1)}
                right = {0: both(zin, k, 0), 1: both(zin, k, 1), 2: pair(gg2, 0), 3: pair(gg2, 1)}
                for w in range(mid):
                    value = correlate(left, right, w)
                    for m in (0, 1):
                        res[k, w, m, here, cols] = value[m]
            p_copy(seg, k, 0, 2, 0).start()

    def polarize_first(k):
        seg = segments[0]
        _, _, _, zin, res, pin, z_recv, p_recv = seg

        @pl.when(inner)
        def _():
            arrived(zin.at[k], z_recv.at[k])
            for here, rows, cols in tiles(seg, k):
                both = lambda c: (zin[k, c, 0, here, cols], zin[k, c, 1, here, cols])
                pair = lambda ref, c: (ref[c, 0, rows, cols], ref[c, 1, rows, cols])
                left = {2: pair(gl2, 0), 3: pair(gl2, 1)}
                right = {0: both(0), 1: both(1), 2: pair(gg2, 0), 3: pair(gg2, 1)}
                for c in (0, 1):
                    left.update({mid + c: both(2 + c), mid + 2 + c: both(6 + c)})
                    right.update({mid + c: both(4 + c), mid + 2 + c: both(8 + c)})
                for w in range(energies):
                    value = correlate(left, right, w)
                    for m in (0, 1):
                        if w in (2, 3):
                            dpair[w - 2, m, rows, cols] = on2[w - 2, m, rows, cols] - value[m] * scale
                        else:
                            res[k, w if w < 2 else w - 2, m, here, cols] = value[m]
            for part, target in enumerate((0, mid, mid + 2)):
                p_copy(seg, k, part, 0, target).start()

        @pl.when(jnp.logical_not(inner))
        def _():
            arrived(pin.at[k, pl.ds(0, 2)], p_recv.at[k])

        @pl.when(outer)
        def _():
            for here, rows, cols in tiles(seg, k):
                pair = lambda ref, c: (ref[c, 0, rows, cols], ref[c, 1, rows, cols])
                left = {0: pair(gl2, 0), 1: pair(gl2, 1)}
                right = {0: pair(gg2, 0), 1: pair(gg2, 1)}
                for c in (0, 1):
                    value = correlate(left, right, c)
                    for m in (0, 1):
                        total = value[m] + pin[k, c, m, here, cols]
                        dpair[c, m, rows, cols] = on2[c, m, rows, cols] - total * scale

        @pl.when(z >= 2)
        def _():
            for here, rows, cols in tiles(seg, k):
                for c in (0, 1):
                    for m in (0, 1):
                        dpair[c, m, rows, cols] = on2[c, m, rows, cols] - pin[k, c, m, here, cols] * scale

    def polarize(seg, k):
        _, _, _, zin, res, pin, z_recv, p_recv = seg

        @pl.when(center)
        def _():
            arrived(zin.at[k], z_recv.at[k])
            for here, rows, cols in tiles(seg, k):
                both = lambda ref, *at: (ref[(*at, 0, here, cols)], ref[(*at, 1, here, cols)])
                pair = lambda ref, c: (ref[c, 0, rows, cols], ref[c, 1, rows, cols])
                left = {mid: pair(gl2, 0), mid + 1: pair(gl2, 1), mid + 2: both(zin, k, 4), mid + 3: both(zin, k, 5)}
                right = {c: both(zin, k, c) for c in range(4)}
                right.update({mid: pair(gg2, 0), mid + 1: pair(gg2, 1)})
                right.update({mid + 2: both(zin, k, 6), mid + 3: both(zin, k, 7)})
                for w in range(energies):
                    value = correlate(left, right, w)
                    for m in (0, 1):
                        if w in (mid, mid + 1):
                            dpair[w - mid, m, rows, cols] = on2[w - mid, m, rows, cols] - value[m] * scale
                        else:
                            res[k, w if w < mid else w - 2, m, here, cols] = value[m]
            for part, target in enumerate((0, 2, mid + 2)):
                p_copy(seg, k, part, 0, target).start()

        @pl.when(inner)
        def _():
            arrived(pin.at[k, pl.ds(0, 2)], p_recv.at[k])
            for here, rows, cols in tiles(seg, k):
                for c in (0, 1):
                    for m in (0, 1):
                        total = res[k, 2 + c, m, here, cols] + pin[k, c, m, here, cols]
                        dpair[c, m, rows, cols] = on2[c, m, rows, cols] - total * scale

        @pl.when(outer)
        def _():
            arrived(pin.at[k], p_recv.at[k])
            for here, rows, cols in tiles(seg, k):
                pair = lambda ref, c: (ref[c, 0, rows, cols], ref[c, 1, rows, cols])
                left = {0: pair(gl2, 0), 1: pair(gl2, 1)}
                right = {0: pair(gg2, 0), 1: pair(gg2, 1)}
                for c in (0, 1):
                    value = correlate(left, right, c)
                    for m in (0, 1):
                        total = value[m] + (pin[k, c, m, here, cols] + pin[k, 2 + c, m, here, cols])
                        dpair[c, m, rows, cols] = on2[c, m, rows, cols] - total * scale

        @pl.when(far)
        def _():
            arrived(pin.at[k, pl.ds(0, 2)], p_recv.at[k])
            for here, rows, cols in tiles(seg, k):
                for c in (0, 1):
                    for m in (0, 1):
                        dpair[c, m, rows, cols] = on2[c, m, rows, cols] - pin[k, c, m, here, cols] * scale

    def strip(first, last):
        return pl.ds(pl.multiple_of(h * half + starts[first], 8), starts[last] - starts[first])

    def spread(seg, k, at, passed=True):
        size, base = seg[1], seg[2]
        sub = pl.ds(pl.multiple_of(base + k * size, 8), size)
        there = diag.at[i, :, pl.ds(pl.multiple_of(h * half + base + k * size, 8), size)]
        if not passed:
            remote(dpair.at[1 - y, :, sub], there, t_send.at[0], d_recv.at[2, at], block=dn).start()
        remote(dpair.at[1 - y, :, sub], there, d_send.at[1], d_recv.at[1, at], block=yn).start()
        remote(dpair.at[y, :, sub], there, d_send.at[0], d_recv.at[0, at], block=xn).start()
        remote(dpair.at[y, :, sub], there, dm_send.at[0], dm_recv.at[0], energy=sib).start()
        pltpu.make_async_copy(dpair.at[y, :, sub], there, d_local).start()

    def gather_y(first, last, passing=True):
        for k in range(first, last):
            arrived(diag.at[yn, :, strip(k, k + 1)], d_recv.at[1, k])
        part = diag.at[yn, :, strip(first, last)]
        if passing:
            remote(part, part, d_send.at[2], d_recv.at[2, first], block=xn).start()
        remote(part, part, dm_send.at[2], dm_recv.at[2], energy=sib).start()

    def gather_x(first, last):
        for k in range(first, last):
            arrived(diag.at[xn, :, strip(k, k + 1)], d_recv.at[0, k])
        part = diag.at[xn, :, strip(first, last)]
        remote(part, part, dm_send.at[1], dm_recv.at[1], energy=sib).start()

    def gather(first, last):
        gather_y(first, last, passing=False)
        gather_x(first, last)

    def gather_passed(first, last):
        part = diag.at[dn, :, strip(first, last)]
        arrived(part, d_recv.at[2, first])
        remote(part, part, dm_send.at[3], dm_recv.at[3], energy=sib).start()

    def prefactor(k, j, w):
        @pl.when(valid(j, w))
        def _():
            if k is None:
                pltpu.make_async_copy(coupling[w], lu.at[i, w], l_local.at[w]).wait()
            else:
                arrived(lu.at[j, w, :, other], lm_recv.at[k, w])

            def step(block, carry):
                rows = pl.ds(pl.multiple_of(block * 16, 16), 16)
                split = factor((lu[j, w, 0, rows], lu[j, w, 1, rows]))
                for at in range(3):
                    for part in (0, 1):
                        flu[j, w, 2 * at + part, rows] = split[at][part]
                return carry

            lax.fori_loop(0, n // 16, step, 0)

    def gather_first():
        @pl.when(before)
        def _():
            gather_y(0, few)

    plan = {
        0: [lambda: prefactor(None, i, 0)],
        1: [lambda: lu_direct_x(1), lambda: prefactor(None, i, 1)],
        2: [src_direct, lambda: prefactor(0, xn, 0)],
        3: [lambda: lu_direct_y(0), lambda: lu_direct_y(1), lambda: prefactor(0, xn, 1)],
        4: [gather_first, lambda: prefactor(1, yn, 0)],
        5: [lambda: gather_y(2, 5), lambda: prefactor(1, yn, 1)],
    }

    def turn(k, carry):
        @pl.when(k < many - 1)
        def _():
            ahead(segments[1], k + 1)

        @pl.when(k == many - 1)
        def _():
            ahead(segments[2], 0)

        polarize(segments[1], k)
        spread(segments[1], k, few + k)
        for at, work in plan.items():

            @pl.when(k == at)
            def _(work=work):
                for step in work:
                    step()

        return carry

    @pl.when(before)
    def _():
        for k in range(few):
            polarize_first(k)
            spread(segments[0], k, k)

    @pl.when(inner)
    def _():
        for k in range(few):
            z_copies(segments[2], k, 1)

    ahead(segments[1], 0)
    lu_direct_x(0)
    lax.fori_loop(0, many, turn, 0)

    @pl.when(z >= 2)
    def _():
        for k in range(few):
            polarize_first(k)
            spread(segments[0], k, k, passed=False)

    ahead(segments[2], 1)
    polarize(segments[2], 0)
    spread(segments[2], 0, end, passed=False)
    gather_y(5, 7)
    polarize(segments[2], 1)
    spread(segments[2], 1, end + 1, passed=False)
    gather_y(7, 8)
    gather_x(2, 8)
    src_passed()
    lu_passed(0)
    lu_passed(1)

    @pl.when(before)
    def _():
        gather_x(0, few)
        gather_passed(0, few)

    gather_passed(2, 5)
    gather_passed(5, 7)
    prefactor(2, dn, 0)
    prefactor(2, dn, 1)
    for k in (end, end + 1):
        gather(k, k + 1)
        gather_passed(k, k + 1)
    gather_passed(7, 8)

    @pl.when(z >= 2)
    def _():
        for k in range(few):
            gather(k, k + 1)
            gather_passed(k, k + 1)


    a, b, m, q = 3 * x, 2 - x, 1 + x, 3 - 3 * x
    couple = lambda j, w: tuple((flu[j, w, 2 * k], flu[j, w, 2 * k + 1]) for k in range(3))
    diagonal = lambda j: (diag[j, 0], diag[j, 1])
    source = lambda j: (src[j, 0], src[j, 1])

    def put(ref, at, v):
        ref[at, 0], ref[at, 1] = v

    edge_d = []
    for k in (0, 1):
        part = edge_diag.at[:, pl.ds(k * half, half)]
        edge_d.append(remote(part, part, e_sem.at[2 * k], e_sem.at[2 * k + 1], energy=sib))
    edge_s = remote(edge_src, edge_src, e_sem.at[4], e_sem.at[5], energy=sib)

    def edge_term():
        t = factor(times(couple(b, 1 - x), factor(lean_inverse(diagonal(q), -0.2))))
        for k in (0, 1):
            rows = slice(k * half, (k + 1) * half)
            v = times(tuple(tuple(u[rows] for u in w) for w in t), couple(q, x))
            edge_diag[0, rows], edge_diag[1, rows] = v
            edge_d[k].start()
        edge_src[0], edge_src[1] = apply(t, source(q))
        edge_s.start()

    @pl.when(y == h)
    def _():
        pltpu.make_async_copy(rhs.at[:, 0], src.at[i], s_local).wait()

    @pl.when(y != h)
    def _():
        arrived(src.at[i], sm_recv.at[0])

    for k, j in enumerate((xn, yn, dn)):
        arrived(src.at[j, :, other], sm_recv.at[k + 1])

    arrived(diag.at[xn, :, other], dm_recv.at[1])

    @pl.when(jnp.logical_and(h == y, x != y))
    def _():
        edge_term()

    pltpu.make_async_copy(dpair.at[y], diag.at[i, :, mine], d_local).wait()
    for k, j in ((0, i), (2, yn), (3, dn)):
        arrived(diag.at[j, :, other], dm_recv.at[k])

    @pl.when(jnp.logical_and(h == y, x == y))
    def _():
        edge_term()

    inv = factor(lean_inverse(diagonal(m), -0.2))
    t = factor(times(stacked(couple(a, 1 - x), couple(b, x)), inv))
    top, low = (lambda v: (v[0][:n], v[1][:n])), (lambda v: (v[0][n:], v[1][n:]))
    v = times(t, couple(m, x))
    put(dp, 0, minus(diagonal(a), top(v)))
    put(fp, 1, low(v))
    v = times(t, couple(m, 1 - x))
    put(dp, 1, minus(diagonal(b), low(v)))
    put(fp, 0, top(v))
    v = apply(t, source(m))
    put(sp, 0, minus(source(a), top(v)))
    put(sp, 1, minus(source(b), low(v)))

    def add_edge():
        @pl.when(h != y)
        def _():
            for copy in edge_d:
                copy.wait_recv()

        for k in (0, 1):
            dp[1, k] = dp[1, k] - edge_diag[k]

    this = jnp.where(h == x, 0, 1)

    @pl.when(h == x)
    def _():
        add_edge()

    that = 1 - this
    at = lambda ref, k: (ref[k, 0], ref[k, 1])
    t = factor(times(factor(at(fp, this)), factor(lean_inverse(at(dp, that)))))
    v = times(t, factor(at(fp, that)))

    @pl.when(h != x)
    def _():
        add_edge()

    @pl.when(h != y)
    def _():
        edge_s.wait_recv()

    for k in (0, 1):
        sp[1, k] = sp[1, k] - edge_src[k]
    last = minus(at(dp, this), v)
    right = plus(at(sp, this), apply(t, at(sp, that)))
    rest = factor(remainder_of(last))
    inverse_guess = 1.0 / diagonal_guess
    found = right
    for _ in range(2):
        found = plus(right, apply(rest, found))
    home, keep = [], []
    for k in (0, 1):
        part = pl.ds(k * half, half)
        there = out.at[:, 0, part]
        home.append(
            remote(
                value.at[:, part], there, out_sem.at[k], out_sem.at[2 + k], energy=2 * z + y, block=2 * h + x
            )
        )
        keep.append(pltpu.make_async_copy(value.at[:, part], there, out_sem.at[k]))
    for k in (0, 1):
        rows = slice(k * half, (k + 1) * half)
        upper_part = tuple(tuple(u[rows] for u in w) for w in rest)
        v = plus((right[0][rows], right[1][rows]), apply(upper_part, found))
        value[0, rows], value[1, rows] = v[0] * inverse_guess, v[1] * inverse_guess

        @pl.when(h != y)
        def _(k=k):
            home[k].start()

        @pl.when(h == y)
        def _(k=k):
            keep[k].start()

    @pl.when(h == y)
    def _():
        for copy in keep:
            copy.wait()

    whole_array, most = gg.at[:, 0], gg.at[:, 0, pl.ds(0, n - 2 * edge)]
    rest_of = gg.at[:, 0, pl.ds(0, 2 * edge)]

    def p_sent(seg, parts):
        for k in range(parts):
            sent(seg[4].at[:, pl.ds(2 * k, 2)], p_send.at[seg[0], k])

    @pl.when(outer)
    def _():
        sent(most, z_send.at[0])
        sent(whole_array, z_send.at[1])

    @pl.when(inner)
    def _():
        sent(most, z_send.at[0])
        for seg, parts in zip(segments, (3, 1, 1)):
            p_sent(seg, parts)

    @pl.when(center)
    def _():
        sent(rest_of, z_send.at[0])
        sent(rest_of, z_send.at[1])
        for seg in segments[1:]:
            p_sent(seg, 3)

    @pl.when(far)
    def _():
        sent(whole_array, z_send.at[0])
        sent(whole_array, z_send.at[1])

    for copy in pairs:
        copy.wait_send()
    for k in range(2):
        sent(dpair.at[0], d_send.at[k])

    @pl.when(before)
    def _():
        sent(dpair.at[0, :, pl.ds(0, half - edge)], d_send.at[2])
        sent(dpair.at[0, :, pl.ds(0, edge)], t_send.at[0])

    @pl.when(z >= 2)
    def _():
        sent(dpair.at[0, :, pl.ds(0, half - 2 * edge)], d_send.at[2])
        sent(dpair.at[0, :, pl.ds(0, 2 * edge)], t_send.at[0])

    for k in range(4):
        sent(dpair.at[0], dm_send.at[k])
    part = src.at[0, :, mine]

    @pl.when(y == h)
    def _():
        sent(rhs.at[:, 0], sm_send.at[0])

    sent(rhs.at[:, 0], s_send.at[0])
    sent(part, s_send.at[1])
    for k in range(3):
        sent(part, sm_send.at[k + 1])
    for w in (0, 1):
        part = lu.at[0, w, :, mine]

        @pl.when(valid(i, w))
        def _(w=w, part=part):
            sent(part, l_send.at[0, w])
            sent(part, l_send.at[1, w])

        for k, j in enumerate((xn, yn, dn)):

            @pl.when(valid(j, w))
            def _(k=k, w=w, part=part):
                if k == 0:
                    sent(part, l_send.at[2, w])
                sent(part, lm_send.at[k, w])

    @pl.when(h == y)
    def _():
        for copy in (*edge_d, edge_s):
            copy.wait_send()

    @pl.when(h != y)
    def _():
        for copy in home:
            copy.wait()


def line(g_lesser, g_greater, onsite, lower, upper, rhs):
    count = lax.axis_size("block")
    n, columns = onsite.shape[2], rhs.shape[-1]
    half = n // 2
    r = half // 8
    many, few, fine = 6, 2, r // 2
    f32 = jnp.float32
    dma = pltpu.SemaphoreType.DMA
    anywhere = pl.BlockSpec(memory_space=pl.ANY)
    pair = pltpu.VMEM((2, 2, half, n), f32)
    return pl.pallas_call(
        line_kernel,
        name="line",
        out_shape=pltpu.VMEM((2, 1, n, columns), f32),
        in_specs=[anywhere] * 6,
        out_specs=anywhere,
        scratch_shapes=[
            pair, pair, pair,
            pltpu.VMEM((few, 10, 2, fine, n), f32),
            pltpu.VMEM((few, 6, 2, fine, n), f32),
            pltpu.VMEM((few, 4, 2, fine, n), f32),
            pltpu.VMEM((many, 8, 2, r, n), f32),
            pltpu.VMEM((many, 6, 2, r, n), f32),
            pltpu.VMEM((many, 4, 2, r, n), f32),
            pltpu.VMEM((few, 8, 2, fine, n), f32),
            pltpu.VMEM((few, 6, 2, fine, n), f32),
            pltpu.VMEM((few, 4, 2, fine, n), f32),
            pair,
            pltpu.VMEM((count, 2, n, n), f32),
            pltpu.VMEM((count, 2, n, columns), f32),
            pltpu.VMEM((count, 2, 2, n, n), f32),
            pltpu.VMEM((2, 2, n, n), f32),
            pltpu.VMEM((2, 2, n, n), f32),
            pltpu.VMEM((2, 2, n, columns), f32),
            pltpu.VMEM((2, n, columns), f32),
            dma((2,)), dma((few,)), dma((3, 3)), dma((few,)), dma((many,)), dma((many,)), dma((few,)), dma((few,)),
            dma((3,)), dma((3,)), dma((3,)),
            dma((3,)), dma((3, many + 2 * few)), dma, dma((4,)), dma((4,)), dma((1,)), dma((1,)),
            dma((2,)), dma((3,)), dma, dma((4,)), dma((4,)),
            dma((3, 2)), dma((3, 2)), dma((2,)), dma((3, 2)), dma((3, 2)), dma((4,)),
            pltpu.VMEM((2, n, n), f32), pltpu.VMEM((2, n, columns), f32), dma((6,)),
            pltpu.VMEM((count, 2, 6, n, n), jnp.bfloat16),
        ],
        compiler_params=pltpu.CompilerParams(
            collective_id=1, has_side_effects=True, vmem_limit_bytes=60 * 1024 * 1024
        ),
    )(g_lesser, g_greater, onsite, lower, upper, rhs)


def shifted(value, steps):
    count = lax.axis_size("block")
    leading, last = max(0, -steps), min(count, count - steps)
    pairs = [(k, k + steps) for k in range(leading, last)]
    return lax.ppermute(value, "block", pairs)


def shards(g_lesser, g_greater, onsite, lower, upper, rhs):
    index = lax.axis_index("block")
    count = lax.axis_size("block")
    levels = count.bit_length() - 1
    n = onsite.shape[-1]
    both = jnp.concatenate(
        [jnp.where(index > 0, lower, 0.0), jnp.where(index < count - 1, upper, 0.0)], axis=-1
    )
    if levels == 2 and lax.axis_size("energy") == 8:
        return line(g_lesser, g_greater, onsite, lower, upper, rhs)
    diag, near_lu, near_s = front(g_lesser, g_greater, onsite, lower, upper, rhs)
    diag = parts(diag)
    first, final = index < 2, index >= count - 2
    low, up = cut(parts(both), 0, n), cut(parts(both), n, 2 * n)
    source = parts(rhs[:, 0])
    for depth in range(levels):
        stride = 1 << depth
        inv = inverse(diag)
        if depth == levels - 1:
            coupling = tuple(jnp.where(index < stride, up[k], low[k]) for k in (0, 1))
            sent = product(inv, wide(coupling, source))
            swap = [(k, k ^ stride) for k in range(count)]
            got = parts(lax.ppermute(jnp.stack(sent), "block", swap))
            change = product(coupling, got)
            diag = minus(diag, cut(change, 0, n))
            source = minus(source, cut(change, n, None))
        elif depth == 0:
            packed = jnp.stack(inv)
            inv_left, inv_right = parts(shifted(packed, 1)), parts(shifted(packed, -1))
            t, w = product(low, inv_left), product(up, inv_right)
            lu_l, lu_r = near_lu[0], near_lu[1]
            change = product(t, wide(parts(lu_l[0]), parts(lu_l[1]), parts(near_s[0])))
            other = product(w, wide(parts(lu_r[0]), parts(lu_r[1]), parts(near_s[1])))
            change = tuple(jnp.where(index > 0, v, 0.0) for v in change)
            other = tuple(jnp.where(index < count - 1, v, 0.0) for v in other)
            diag = minus(minus(diag, cut(change, n, 2 * n)), cut(other, 0, n))
            source = minus(minus(source, cut(change, 2 * n, None)), cut(other, 2 * n, None))
            low = tuple(jnp.where(first, 0.0, -v) for v in cut(change, 0, n))
            up = tuple(jnp.where(final, 0.0, -v) for v in cut(other, n, 2 * n))
        else:
            sent = jnp.stack(product(inv, wide(low, up, source)))
            left, right = parts(shifted(sent, stride)), parts(shifted(sent, -stride))
            change, other = product(low, left), product(up, right)
            diag = minus(minus(diag, cut(change, n, 2 * n)), cut(other, 0, n))
            source = minus(minus(source, cut(change, 2 * n, None)), cut(other, 2 * n, None))
            low = tuple(-v for v in cut(change, 0, n))
            up = tuple(-v for v in cut(other, n, 2 * n))
    return jnp.stack(solve(diag, source))[:, None]


def solution(mesh):
    placed = (
        P(None, "energy", "block", None),
        P(None, "energy", "block", None),
        P(None, "energy", "block", None),
        P(None, "block", None),
        P(None, "block", None),
        P(None, "energy", "block", None),
    )
    return jax.shard_map(
        shards,
        mesh=mesh,
        in_specs=placed,
        out_specs=P(None, "energy", "block", None),
        check_vma=False,
    )
```
